512 devices in a mesh: line: 4 (over x), tile: 128 (over z, y, core).
Axes of the slice: x: 4, y: 8, z: 8, core: 2. Of those that a mesh axis runs over, the one named last changes fastest.
Arguments:
- forcing: float32 [10, 64, 128, 512], P(None, None, 'tile', 'line'), may hold values from -1100 to 1100
- block_inverse: float32 [10, 10, 128, 512], P(None, None, 'tile', 'line'), may hold values from -0.8 to 1
- wall_rates: float32 [2, 10, 128, 512], P(None, None, 'tile', 'line'), may hold values from 0 to 1, as said below
- span_couple: float32 [10], replicated, may hold values from 0.1 to 0.4
Outputs:
- basis: float32 [10, 64, 128, 512], P(None, None, 'tile', 'line')
The draws below stay inside these ranges and needn't reach their ends.
Inputs may be any that keep to these rules, and one draw needn't show every extreme that they name: `wall_rates`: every entry lies strictly between 0 and 1.
All inputs are finite; a program needn't handle non-finite values.
Results may differ from the reference program's by a relative error of at most 0.00022.
Values sent between devices are 32-bit elements; how exact they have to be, the bound alone decides.
No kernel may reach another device: no remote copies, remote signals or barrier semaphores. Data moves between devices by JAX's collectives and lax.ppermute only.
A program may use at most 64 MiB of HBM per device.

```python
import math
import jax
import jax.numpy as jnp
from jax import lax

VOLUME_VARIABLES = 10
NF = 64
LD = 128
NORMAL_NODES = 512
LATERAL_NODES = 128


def draw_forcing(key, part):
    generator_seeds = jax.random.split(key, 3)
    shape_full = (VOLUME_VARIABLES, NF, LATERAL_NODES, NORMAL_NODES)
    base = jax.random.truncated_normal(generator_seeds[0], -6.0, 6.0, shape_full, jnp.float32)
    comp_scale = jnp.exp(jax.random.uniform(generator_seeds[1], (VOLUME_VARIABLES, 1, 1, 1), jnp.float32, 0.0, math.log(10.0)))
    column_scale = jnp.exp(jax.random.uniform(generator_seeds[2], (1, NF, 1, 1), jnp.float32, 0.0, math.log(2.0)))
    station = 3.0 ** (jnp.arange(LATERAL_NODES, dtype=jnp.float32) / LATERAL_NODES)
    height = 3.0 ** (1.0 - jnp.arange(NORMAL_NODES, dtype=jnp.float32) / NORMAL_NODES)
    return base * comp_scale * column_scale * station[None, None, :, None] * height[None, None, None, :]


def draw_block_inverse(key, part):
    generator_seeds = jax.random.split(key, 2)
    diagonal = jax.random.uniform(generator_seeds[0], (VOLUME_VARIABLES, 1, LATERAL_NODES, NORMAL_NODES), jnp.float32, 0.5, 1.0)
    offside = 0.2 * jax.random.truncated_normal(generator_seeds[1], -4.0, 4.0, (VOLUME_VARIABLES, VOLUME_VARIABLES, LATERAL_NODES, NORMAL_NODES), jnp.float32)
    unit = jnp.eye(VOLUME_VARIABLES, dtype=jnp.float32)[:, :, None, None]
    return offside * (1.0 - unit) + unit * diagonal


def draw_wall_rates(key, part):
    generator_seeds = jax.random.split(key, 7)
    slow_count = 5
    order = jnp.stack([jax.random.permutation(jax.random.fold_in(generator_seeds[0], 0), VOLUME_VARIABLES), jax.random.permutation(jax.random.fold_in(generator_seeds[0], 1), VOLUME_VARIABLES)])
    slow = order < slow_count
    slow_length = NORMAL_NODES * jax.random.uniform(generator_seeds[1], (2, VOLUME_VARIABLES), jnp.float32, 1.5, 4.0)
    fast_length = LD * jax.random.uniform(generator_seeds[2], (2, VOLUME_VARIABLES), jnp.float32, 0.25, 0.4)
    length = jnp.where(slow, slow_length, fast_length)
    phase = jax.random.uniform(generator_seeds[3], (2, VOLUME_VARIABLES), jnp.float32, 0.0, 2.0 * math.pi)
    position = jnp.arange(NORMAL_NODES, dtype=jnp.float32) / NORMAL_NODES
    profile = 2.0 ** jnp.sin(2.0 * math.pi * position[None, None, :] + phase[:, :, None])
    rough = jnp.exp(jax.random.uniform(generator_seeds[4], (2, VOLUME_VARIABLES, LATERAL_NODES, NORMAL_NODES), jnp.float32, math.log(0.7), math.log(1.4)))
    rate = profile[:, :, None, :] * rough / length[:, :, None, None]
    survival_fraction = jnp.exp(-rate)
    excitation_batch = jax.random.bernoulli(generator_seeds[5], 3.0 / NORMAL_NODES, (2, VOLUME_VARIABLES, LATERAL_NODES, NORMAL_NODES))
    relaxation_passes = jax.random.uniform(generator_seeds[6], (2, VOLUME_VARIABLES, LATERAL_NODES, NORMAL_NODES), jnp.float32, 0.5, 0.8)
    return jnp.where(excitation_batch, survival_fraction * relaxation_passes, survival_fraction)


def setup_inputs(seed: int = 0) -> dict:
    arg_keys = jax.random.split(jax.random.key(seed), 5)
    forcing = draw_forcing(jax.random.fold_in(arg_keys[4], 71), 0)
    block_inverse = draw_block_inverse(jax.random.fold_in(arg_keys[4], 71), 0)
    wall_rates = draw_wall_rates(jax.random.fold_in(arg_keys[4], 71), 0)
    span_couple = jnp.clip(jnp.exp(jax.random.uniform(arg_keys[3], (VOLUME_VARIABLES,), jnp.float32, math.log(0.1), math.log(0.4))), 0.1, 0.4)
    return dict(forcing=forcing, block_inverse=block_inverse, wall_rates=wall_rates, span_couple=span_couple)


def apply_block(blocks, values_in):
    return jnp.einsum('kmzj,mrzj->krzj', blocks, values_in, precision=lax.Precision.HIGHEST)

def span_pair(values_in):
    return jnp.roll(values_in, 1, axis=2) + jnp.roll(values_in, -1, axis=2)

def line_solve(survival_fraction, source, backward):
    rates_first = jnp.moveaxis(survival_fraction, -1, 0)
    source_first = jnp.moveaxis(source, -1, 0)

    def advance(state, inputs):
        rate_now, source_now = inputs
        state = rate_now[:, None, :] * state + source_now
        return (state, state)
    _, states = lax.scan(advance, jnp.zeros_like(source[..., 0]), (rates_first, source_first), reverse=backward)
    return jnp.moveaxis(states, 0, -1)

def reference(forcing, block_inverse, wall_rates, span_couple):
    coupling = span_couple[:, None, None, None]
    rise_rate = wall_rates[0]
    fall_rate = wall_rates[1]
    start_field = apply_block(block_inverse, forcing)
    zero_row = jnp.zeros_like(forcing[..., :1])
    above_row = jnp.concatenate([start_field[..., 1:], zero_row], axis=-1)
    source_one = apply_block(block_inverse, forcing + coupling * span_pair(start_field)) + fall_rate[:, None] * above_row
    rising = line_solve(rise_rate, source_one, False)
    below_row = jnp.concatenate([zero_row, rising[..., :-1]], axis=-1)
    source_two = apply_block(block_inverse, forcing + coupling * span_pair(rising)) + rise_rate[:, None] * below_row
    falling = line_solve(fall_rate, source_two, True)
    gram = jnp.einsum('krzj,kszj->rs', falling, falling, precision=lax.Precision.HIGHEST)
    upper_factor = jnp.linalg.cholesky(gram).T
    identity_matrix = jnp.eye(NF, dtype=gram.dtype)
    inverse_factor = jax.scipy.linalg.solve_triangular(upper_factor, identity_matrix, lower=False)
    scale_value = math.sqrt(VOLUME_VARIABLES * LATERAL_NODES * NORMAL_NODES)
    return jnp.einsum('krzj,rs->kszj', falling, inverse_factor, precision=lax.Precision.HIGHEST) * scale_value
```

```python
import math

import jax
import jax.numpy as jnp
from jax import lax
from jax.experimental import pallas as pl
from jax.experimental.pallas import tpu as pltpu
from jax.sharding import Mesh, PartitionSpec as P

NZ, NY, NCORE = 8, 8, 2
TILE = ("z", "y", "core")
HIGH = lax.Precision.HIGHEST
F32 = jnp.float32
LANES = 128
STEPS = (1, 2, 4, 8, 16, 32, 64)
VMEM = pl.BlockSpec(memory_space=pltpu.VMEM)
SMEM = pl.BlockSpec(memory_space=pltpu.SMEM)


def lane_ids(rows):
    return lax.broadcasted_iota(jnp.int32, (rows, LANES), 1)


def row_ids(rows):
    return lax.broadcasted_iota(jnp.int32, (rows, LANES), 0)


def dot_nt(a, b):
    return lax.dot_general(
        a, b, (((1,), (1,)), ((), ())), precision=HIGH, preferred_element_type=F32
    )


def call(body, outs, flops=0, scratch=()):
    many = isinstance(outs[0], tuple)
    shapes = [jax.ShapeDtypeStruct(s, F32) for s in (outs if many else [outs])]

    def run(*args):
        size = sum(a.size for a in args) + sum(math.prod(s.shape) for s in shapes)
        return pl.pallas_call(
            body,
            out_shape=shapes if many else shapes[0],
            in_specs=[SMEM if a.ndim == 1 else VMEM for a in args],
            out_specs=[VMEM] * len(shapes) if many else VMEM,
            scratch_shapes=list(scratch),
            cost_estimate=pl.CostEstimate(
                flops=flops, bytes_accessed=4 * size, transcendentals=0
            ),
        )(*args)

    return run


def apply_rows(b_ref, k, n, take, rows):
    total = b_ref[k * n : k * n + 1, :] * take(0)
    for m in range(1, n):
        total = total + b_ref[k * n + m : k * n + m + 1, :] * take(m)
    return total


def start_body(f_ref, b_ref, s_ref):
    n, cols, _ = f_ref.shape
    for g in range(0, cols, 16):
        vals = [f_ref[m, g : g + 16, :] for m in range(n)]
        for k in range(n):
            s_ref[k, g : g + 16, :] = apply_rows(b_ref, k, n, lambda m: vals[m], 16)


def rates_body(w_ref, up_ref, down_ref, pre_ref, suf_ref, row_ref, ext_ref):
    n = w_ref.shape[0] // 2
    lane = lane_ids(n)
    up, down = w_ref[0:n, :], w_ref[n : 2 * n, :]
    pre, suf = up, down
    p = jnp.where(lane >= 1, up, 0.0)
    q = jnp.where(lane < LANES - 1, down, 0.0)
    for i, d in enumerate(STEPS):
        up_ref[i, 0:n, :] = p
        down_ref[i, 0:n, :] = q
        p = p * pltpu.roll(p, d, 1)
        q = q * pltpu.roll(q, LANES - d, 1)
        pre = jnp.where(lane >= d, pre * pltpu.roll(pre, d, 1), pre)
        suf = jnp.where(lane < LANES - d, suf * pltpu.roll(suf, LANES - d, 1), suf)
    pre_ref[0:n, :] = pre
    suf_ref[0:n, :] = suf
    norm = jnp.sum(suf * suf, axis=1, keepdims=True)
    table = jnp.zeros((8, LANES), F32)
    at, row = lane_ids(8), row_ids(8)
    for k in range(n):
        mine = jnp.where(row == 0, pre[k : k + 1, LANES - 1 : LANES], 0.0)
        mine = jnp.where(row == 1, down[k : k + 1, LANES - 1 : LANES], mine)
        mine = jnp.where(row == 2, suf[k : k + 1, 0:1], mine)
        mine = jnp.where(row == 3, norm[k : k + 1, 0:1], mine)
        table = jnp.where(lax.rem(at, 16) == k, mine, table)
    row_ref[...] = table
    place = row_ids(64)
    first = (lane_ids(64) == 0).astype(F32)
    for k in range(n):
        block = jnp.where(place == k, jnp.broadcast_to(suf[k : k + 1, :], (64, LANES)), 0.0)
        block = jnp.where(place == 16 + k, first, block)
        ext_ref[:, k * LANES : (k + 1) * LANES] = block


def neighbours_into(h_ref, c_ref, n_ref, g_ref):
    other = 1 - lax.axis_index("core")
    for m in range(n_ref.shape[0]):
        h_ref[m] = c_ref[m] * (n_ref[m] + g_ref[other, m])


def up_body(c_ref, b_ref, w_ref, s_ref, n_ref, g_ref, up_ref, row_ref, loc_ref, pay_ref, h_ref):
    n, cols, _ = s_ref.shape
    neighbours_into(h_ref, c_ref, n_ref, g_ref)
    lane = lane_ids(16)
    inner = lane < LANES - 1
    groups = cols // 16
    pay = jnp.zeros((16, LANES), F32)
    for k in range(n):
        fall = w_ref[n + k : n + k + 1, :]
        for g in range(groups):
            rows = slice(16 * g, 16 * g + 16)
            s = s_ref[k, rows, :]
            above = jnp.where(inner, pltpu.roll(s, LANES - 1, 1), 0.0)
            v = s + fall * above + apply_rows(b_ref, k, n, lambda m: h_ref[m, rows, :], 16)
            for i, d in enumerate(STEPS):
                v = v + up_ref[i, k : k + 1, :] * pltpu.roll(v, d, 1)
            loc_ref[k, rows, :] = v
            pay = jnp.where(lane == 32 * g + k, v[:, LANES - 1 : LANES], pay)
            pay = jnp.where(lane == 32 * g + 16 + k, s[:, 0:1], pay)
    for peer in range(pay_ref.shape[0]):
        pay_ref[peer, 0:16, :] = pay
        pay_ref[peer, 16:24, :] = row_ref[...]


def enter_body(r_ref, loc_ref, pre_ref, w_ref, out_ref, edge_ref):
    n, cols, _ = loc_ref.shape
    peers = r_ref.shape[0]
    mine = lax.axis_index("line")
    state = jnp.zeros((16, LANES), F32)
    entry = state
    top = state
    for at in range(peers - 1):
        lead = pltpu.roll(r_ref[at + 1, 0:16, :], LANES - 16, 1)
        tail = r_ref[at, 17:18, :] * lead
        top = jnp.where(mine == at, tail, top)
        state = r_ref[at, 16:17, :] * state + (r_ref[at, 0:16, :] + tail)
        entry = jnp.where(mine == at + 1, state, entry)
    lane = lane_ids(16)
    for k in range(n):
        pre = pre_ref[k : k + 1, :]
        for g in range(cols // 16):
            rows = slice(16 * g, 16 * g + 16)
            at = 32 * g + k
            v = loc_ref[k, rows, :] + pre * entry[:, at : at + 1]
            out_ref[k, rows, :] = jnp.where(lane == LANES - 1, v + top[:, at : at + 1], v)
    edge_ref[...] = entry


def below_body(s_ref, up_ref, edge_ref, w_ref, out_ref):
    n, cols, _ = s_ref.shape
    lane = lane_ids(16)
    entry = edge_ref[...]
    for k in range(n):
        rise = w_ref[k : k + 1, :]
        for g in range(cols // 16):
            rows = slice(16 * g, 16 * g + 16)
            at = 32 * g + k
            below = pltpu.roll(up_ref[k, rows, :], 1, 1)
            below = jnp.where(lane == 0, entry[:, at : at + 1], below)
            out_ref[k, rows, :] = s_ref[k, rows, :] + rise * below


def down_body(c_ref, b_ref, base_ref, n_ref, g_ref, down_ref, ext_ref, loc_ref, pay_ref, h_ref, a_ref):
    n, cols, _ = base_ref.shape
    neighbours_into(h_ref, c_ref, n_ref, g_ref)
    for k in range(n):
        for g in range(cols // 16):
            rows = slice(16 * g, 16 * g + 16)
            v = base_ref[k, rows, :] + apply_rows(b_ref, k, n, lambda m: h_ref[m, rows, :], 16)
            for i, d in enumerate(STEPS):
                v = v + down_ref[i, k : k + 1, :] * pltpu.roll(v, LANES - d, 1)
            loc_ref[k, rows, :] = v
            a_ref[rows, k * LANES : (k + 1) * LANES] = v
    a_ref[cols : 2 * cols, :] = ext_ref[...]
    total = dot_nt(a_ref[0:cols, :], a_ref[...])
    for peer in range(pay_ref.shape[0]):
        pay_ref[peer] = total


def line_body(r_ref, q_ref, gram_ref, entry_ref):
    peers, cols, _ = r_ref.shape
    mine = lax.axis_index("line")
    lane = lane_ids(cols)
    state = jnp.zeros((cols, LANES), F32)
    entry = state
    left = state
    total = r_ref[peers - 1]
    for at in range(peers - 2, -1, -1):
        state = q_ref[at + 1, 18:19, :] * state + r_ref[at + 1]
        entry = jnp.where(mine == at, state, entry)
        total = total + r_ref[at]
        cross = r_ref[at] + (0.5 * q_ref[at, 19:20, :]) * pltpu.roll(state, LANES - 16, 1)
        here = (lane >= 16 * at) & (lane < 16 * at + 10)
        left = jnp.where(here, pltpu.roll(cross, (LANES + 16 * at - 64) % LANES, 1), left)
        here = (lane >= 64 + 16 * at) & (lane < 64 + 16 * at + 10)
        left = jnp.where(here, pltpu.roll(state, (LANES + 16 * at - 16) % LANES, 1), left)
    fix = dot_nt(left, pltpu.roll(left, 64, 1))
    half = cols // 2
    gram = total[:, 0:64] + fix
    gram_ref[:, 0:64] = gram[0:half, :]
    gram_ref[:, 64:128] = gram[half:cols, :]
    entry_ref[...] = entry


def sum_body(r_ref, o_ref):
    total = r_ref[0]
    for i in range(1, r_ref.shape[0]):
        total = total + r_ref[i]
    for peer in range(o_ref.shape[0]):
        o_ref[peer] = total


def basis_body(scale, r_ref, loc_ref, suf_ref, entry_ref, out_ref, f_ref):
    n, cols, _ = loc_ref.shape
    for k in range(n):
        e = entry_ref[:, 80 + k : 81 + k]
        f_ref[:, k * LANES : (k + 1) * LANES] = loc_ref[k] + suf_ref[k : k + 1, :] * e
    packed = r_ref[0]
    for i in range(1, r_ref.shape[0]):
        packed = packed + r_ref[i]
    low = pltpu.roll(packed, 64, 1)
    lane, row = lane_ids(cols), row_ids(cols)
    m = jnp.concatenate([packed, low], axis=0)
    m = jnp.where(lane < 64, m, jnp.where(lane - 64 == row, 1.0, 0.0))
    diag = jnp.zeros((cols, LANES), F32)
    for j in range(cols):
        col = jnp.broadcast_to(m[:, j : j + 1], (cols, LANES))
        pivot = jnp.broadcast_to(col[j : j + 1, :], (cols, LANES))
        diag = jnp.where(row == j, pivot, diag)
        factor = jnp.where(row > j, col / pivot, 0.0)
        m = m - factor * m[j : j + 1, :]
    inv = pltpu.roll(m * (scale / jnp.sqrt(diag)), 64, 1)[:, 0:64]
    out = jnp.dot(inv, f_ref[...], precision=HIGH, preferred_element_type=F32)
    for k in range(n):
        out_ref[k] = out[:, k * LANES : (k + 1) * LANES]


def exchange(value, axis):
    return lax.all_to_all(value, axis, 0, 0, tiled=True)


def local(forcing, block_inverse, wall_rates, span_couple):
    n, cols, _, pts = forcing.shape
    peers = lax.axis_size("line")
    stations = lax.axis_size("z") * lax.axis_size("y") * lax.axis_size("core")
    rows = n * stations * pts * peers
    field = (n, cols, pts)
    f = forcing.reshape(field)
    b = block_inverse.reshape(n * n, pts)
    w = wall_rates.reshape(2 * n, pts)
    across = [(i, (i + 1) % stations if i % 2 else (i - 1) % stations) for i in range(stations)]
    work = 2 * n * n * cols * pts
    scratch = pltpu.VMEM(field, F32)

    start = call(start_body, field, work)(f, b)
    far = lax.ppermute(start, TILE, across)
    near = lax.all_gather(start, "core")
    steps = (len(STEPS), 16, pts)
    up, down, pre, suf, row, ext = call(
        rates_body, [steps, steps, (16, pts), (16, pts), (8, pts), (64, n * pts)], work // 8
    )(w)
    loc, pay = call(up_body, [field, (peers, 24, pts)], 2 * work, [scratch])(
        span_couple, b, w, start, far, near, up, row
    )
    got = exchange(pay, "line")
    rising, edge = call(enter_body, [field, (16, pts)], work // 4)(got, loc, pre, w)
    far = lax.ppermute(rising, TILE, across)
    near = lax.all_gather(rising, "core")
    base = call(below_body, field, work // 4)(start, rising, edge, w)
    wide = pltpu.VMEM((2 * cols, n * pts), F32)
    loc, pay = call(down_body, [field, (peers, cols, pts)], 4 * work, [scratch, wide])(
        span_couple, b, base, far, near, down, ext
    )
    sums = exchange(pay, "line")
    gram, entry = call(line_body, [(cols // 2, pts), (cols, pts)], work // 4)(sums, got)
    half = (cols // 2, pts)
    both = lax.all_gather(gram, "core")
    gram = call(sum_body, (NY,) + half)(both)
    gram = call(sum_body, (NZ,) + half)(exchange(gram, "y"))
    gram = exchange(gram, "z")

    def basis(*refs):
        basis_body(math.sqrt(rows), *refs)

    out = call(basis, field, 4 * work, [pltpu.VMEM((cols, n * pts), F32)])(gram, loc, suf, entry)
    return out.reshape(n, cols, 1, pts)


def solution(mesh):
    devices = mesh.devices.reshape(mesh.shape["line"], NZ, NY, NCORE)
    inner = Mesh(devices, ("line",) + TILE)
    spec = P(None, None, TILE, "line")
    return jax.shard_map(
        local, mesh=inner, in_specs=(spec, spec, spec, P()), out_specs=spec, check_vma=False
    )
```

```python
import math

import jax
import jax.numpy as jnp
from jax import lax
from jax.experimental import pallas as pl
from jax.experimental.pallas import tpu as pltpu
from jax.sharding import Mesh, PartitionSpec as P

NZ, NY, NCORE = 8, 8, 2
TILE = ("z", "y", "core")
HIGH = lax.Precision.HIGHEST
F32 = jnp.float32
LANES = 128
LIMIT = 16 << 20
STEPS = (1, 2, 4, 8, 16, 32, 64)
VMEM = pl.BlockSpec(memory_space=pltpu.VMEM)
SMEM = pl.BlockSpec(memory_space=pltpu.SMEM)
HBM = pl.BlockSpec(memory_space=pltpu.HBM)


def lane_ids(rows):
    return lax.broadcasted_iota(jnp.int32, (rows, LANES), 1)


def row_ids(rows):
    return lax.broadcasted_iota(jnp.int32, (rows, LANES), 0)


def dot_nt(a, b):
    return lax.dot_general(
        a, b, (((1,), (1,)), ((), ())), precision=HIGH, preferred_element_type=F32
    )


def call(body, outs, flops=0, scratch=(), space=VMEM):
    many = isinstance(outs[0], tuple)
    shapes = [jax.ShapeDtypeStruct(s, F32) for s in (outs if many else [outs])]

    def run(*args):
        size = sum(a.size for a in args) + sum(math.prod(s.shape) for s in shapes)
        return pl.pallas_call(
            body,
            out_shape=shapes if many else shapes[0],
            in_specs=[SMEM if a.ndim == 1 else space for a in args],
            out_specs=[VMEM] * len(shapes) if many else VMEM,
            scratch_shapes=list(scratch),
            compiler_params=pltpu.CompilerParams(vmem_limit_bytes=LIMIT),
            cost_estimate=pl.CostEstimate(
                flops=flops, bytes_accessed=4 * size, transcendentals=0
            ),
        )(*args)

    return run


def apply_rows(block, n, take):
    total = block(0) * take(0)
    for m in range(1, n):
        total = total + block(m) * take(m)
    return total


def pick(values, mask):
    total = None
    for _ in range(3):
        piece = values.astype(jnp.bfloat16)
        values = values - piece.astype(F32)
        part = lax.dot_general(
            piece, mask, (((1,), (1,)), ((), ())), preferred_element_type=F32
        )
        total = part if total is None else total + part
    return total


def lane_mask(rows, n, shift, at):
    wide = (rows, n * LANES)
    col = lax.broadcasted_iota(jnp.int32, wide, 1)
    row = lax.broadcasted_iota(jnp.int32, wide, 0)
    return (col == (row - shift) * LANES + at).astype(jnp.bfloat16)


def start_body(f_hbm, b_hbm, w_hbm, s_ref, b_ref, w_ref, f_ref, sems):
    copies = [
        pltpu.make_async_copy(src, dst, sems.at[i])
        for i, (src, dst) in enumerate(((f_hbm, f_ref), (b_hbm, b_ref), (w_hbm, w_ref)))
    ]
    for copy in copies:
        copy.start()
    for copy in copies:
        copy.wait()
    n, cols, _ = f_ref.shape
    for g in range(0, cols, 16):
        vals = [f_ref[m, g : g + 16, :] for m in range(n)]
        for k in range(n):
            s_ref[k, g : g + 16, :] = apply_rows(lambda m: b_ref[k, m], n, lambda m: vals[m])


def side_body(
    c_ref, b_ref, w_ref, s_ref,
    cb_ref, base_ref, edge_ref, up_ref, down_ref, pre_ref, suf_ref, row_ref, ext_ref, a_ref,
):
    n = w_ref.shape[1]
    lane = lane_ids(n)
    up, down = (jnp.concatenate([w_ref[i, k] for k in range(n)], axis=0) for i in range(2))
    pre, suf = up, down
    p = jnp.where(lane >= 1, up, 0.0)
    q = jnp.where(lane < LANES - 1, down, 0.0)
    for i, d in enumerate(STEPS):
        up_ref[i, 0:n, :] = p
        down_ref[i, 0:n, :] = q
        p = p * pltpu.roll(p, d, 1)
        q = q * pltpu.roll(q, LANES - d, 1)
        pre = jnp.where(lane >= d, pre * pltpu.roll(pre, d, 1), pre)
        suf = jnp.where(lane < LANES - d, suf * pltpu.roll(suf, LANES - d, 1), suf)
    pre_ref[0:n, :] = pre
    suf_ref[0:n, :] = suf
    norm = jnp.sum(suf * suf, axis=1, keepdims=True)
    table = jnp.zeros((8, LANES), F32)
    at, row = lane_ids(8), row_ids(8)
    for k in range(n):
        mine = jnp.where(row == 0, pre[k : k + 1, LANES - 1 : LANES], 0.0)
        mine = jnp.where(row == 1, down[k : k + 1, LANES - 1 : LANES], mine)
        mine = jnp.where(row == 2, suf[k : k + 1, 0:1], mine)
        mine = jnp.where(row == 3, norm[k : k + 1, 0:1], mine)
        table = jnp.where(lax.rem(at, 16) == k, mine, table)
    row_ref[...] = table
    place = row_ids(64)
    first = (lane_ids(64) == 0).astype(F32)
    for k in range(n):
        block = jnp.where(place == k, jnp.broadcast_to(suf[k : k + 1, :], (64, LANES)), 0.0)
        block = jnp.where(place == 16 + k, first, block)
        ext_ref[:, k * LANES : (k + 1) * LANES] = block


    inner = lane_ids(64) < LANES - 1
    for k in range(n):
        for m in range(n):
            cb_ref[k * n + m : k * n + m + 1, :] = c_ref[m] * b_ref[k, m]
        start = s_ref[k]
        a_ref[:, k * LANES : (k + 1) * LANES] = start
        above = jnp.where(inner, pltpu.roll(start, LANES - 1, 1), 0.0)
        base_ref[k] = start + w_ref[1, k] * above
    edge_ref[...] = pick(a_ref[...], lane_mask(32, n, 16, 0))


def neighbours_into(h_ref, n_ref, g_ref):
    other = 1 - lax.axis_index("core")
    for m in range(n_ref.shape[0]):
        h_ref[m] = n_ref[m] + g_ref[other, m]


def coupled(cb_ref, h_ref, k, n, rows):
    return apply_rows(
        lambda m: cb_ref[k * n + m : k * n + m + 1, :], n, lambda m: h_ref[m, rows, :]
    )


def up_body(cb_ref, base_ref, n_ref, g_ref, up_ref, edge_ref, row_ref, loc_ref, pay_ref, h_ref, a_ref):
    n, cols, _ = base_ref.shape
    neighbours_into(h_ref, n_ref, g_ref)
    for k in range(n):
        for g in range(cols // 16):
            rows = slice(16 * g, 16 * g + 16)
            v = base_ref[k, rows, :] + coupled(cb_ref, h_ref, k, n, rows)
            for i, d in enumerate(STEPS):
                v = v + up_ref[i, k : k + 1, :] * pltpu.roll(v, d, 1)
            loc_ref[k, rows, :] = v
            a_ref[rows, k * LANES : (k + 1) * LANES] = v
    ends = pick(a_ref[...], lane_mask(32, n, 0, LANES - 1)) + edge_ref[...]
    ends = jnp.concatenate([ends, jnp.zeros((cols, LANES - 32), F32)], axis=1)
    pay = ends[0:16, :]
    for g in range(1, cols // 16):
        pay = pay + pltpu.roll(ends[16 * g : 16 * g + 16, :], 32 * g, 1)
    for peer in range(pay_ref.shape[0]):
        pay_ref[peer, 0:16, :] = pay
        pay_ref[peer, 16:24, :] = row_ref[...]


def enter_body(r_ref, loc_ref, pre_ref, out_ref, edge_ref):
    n, cols, _ = loc_ref.shape
    peers = r_ref.shape[0]
    mine = lax.axis_index("line")
    state = jnp.zeros((16, LANES), F32)
    entry = state
    top = state
    for at in range(peers - 1):
        lead = pltpu.roll(r_ref[at + 1, 0:16, :], LANES - 16, 1)
        tail = r_ref[at, 17:18, :] * lead
        top = jnp.where(mine == at, tail, top)
        state = r_ref[at, 16:17, :] * state + (r_ref[at, 0:16, :] + tail)
        entry = jnp.where(mine == at + 1, state, entry)
    lane = lane_ids(16)
    for k in range(n):
        pre = pre_ref[k : k + 1, :]
        for g in range(cols // 16):
            rows = slice(16 * g, 16 * g + 16)
            at = 32 * g + k
            v = loc_ref[k, rows, :] + pre * entry[:, at : at + 1]
            out_ref[k, rows, :] = jnp.where(lane == LANES - 1, v + top[:, at : at + 1], v)
    edge_ref[...] = entry


def below_body(s_ref, up_ref, edge_ref, w_ref, out_ref):
    n, cols, _ = s_ref.shape
    lane = lane_ids(16)
    entry = edge_ref[...]
    for k in range(n):
        rise = w_ref[0, k]
        for g in range(cols // 16):
            rows = slice(16 * g, 16 * g + 16)
            at = 32 * g + k
            below = pltpu.roll(up_ref[k, rows, :], 1, 1)
            below = jnp.where(lane == 0, entry[:, at : at + 1], below)
            out_ref[k, rows, :] = s_ref[k, rows, :] + rise * below


def down_body(cb_ref, base_ref, n_ref, g_ref, down_ref, ext_ref, loc_ref, pay_ref, h_ref, a_ref):
    n, cols, _ = base_ref.shape
    neighbours_into(h_ref, n_ref, g_ref)
    for k in range(n):
        for g in range(cols // 16):
            rows = slice(16 * g, 16 * g + 16)
            v = base_ref[k, rows, :] + coupled(cb_ref, h_ref, k, n, rows)
            for i, d in enumerate(STEPS):
                v = v + down_ref[i, k : k + 1, :] * pltpu.roll(v, LANES - d, 1)
            loc_ref[k, rows, :] = v
            a_ref[rows, k * LANES : (k + 1) * LANES] = v
    a_ref[cols : 2 * cols, :] = ext_ref[...]
    total = dot_nt(a_ref[0:cols, :], a_ref[...])
    for peer in range(pay_ref.shape[0]):
        pay_ref[peer] = total


def line_body(r_ref, q_ref, gram_ref, entry_ref):
    peers, cols, _ = r_ref.shape
    mine = lax.axis_index("line")
    lane = lane_ids(cols)
    state = jnp.zeros((cols, LANES), F32)
    entry = state
    left = state
    total = r_ref[peers - 1]
    for at in range(peers - 2, -1, -1):
        state = q_ref[at + 1, 18:19, :] * state + r_ref[at + 1]
        entry = jnp.where(mine == at, state, entry)
        total = total + r_ref[at]
        cross = r_ref[at] + (0.5 * q_ref[at, 19:20, :]) * pltpu.roll(state, LANES - 16, 1)
        here = (lane >= 16 * at) & (lane < 16 * at + 10)
        left = jnp.where(here, pltpu.roll(cross, (LANES + 16 * at - 64) % LANES, 1), left)
        here = (lane >= 64 + 16 * at) & (lane < 64 + 16 * at + 10)
        left = jnp.where(here, pltpu.roll(state, (LANES + 16 * at - 16) % LANES, 1), left)
    fix = dot_nt(left, pltpu.roll(left, 64, 1))
    half = cols // 2
    gram = total[:, 0:64] + fix
    gram_ref[:, 0:64] = gram[0:half, :]
    gram_ref[:, 64:128] = gram[half:cols, :]
    entry_ref[...] = entry


def sum_body(r_ref, o_ref):
    total = r_ref[0]
    for i in range(1, r_ref.shape[0]):
        total = total + r_ref[i]
    for peer in range(o_ref.shape[0]):
        o_ref[peer] = total


def inverse_factor(scale, gram, v_ref):
    cols = gram.shape[0]
    count = cols // 8
    lane, row = lane_ids(8), row_ids(8)
    tiles = []
    for t in range(count):
        unit = jnp.where(lane - 64 == row + 8 * t, 1.0, 0.0)
        tiles.append(jnp.where(lane < 64, gram[8 * t : 8 * t + 8, :], unit))
    for p in range(count):
        later = range(p + 1, count)
        r = [tiles[p][i : i + 1, :] for i in range(8)]
        s = {}
        for i in range(8):
            for j in range(i + 1):
                at = 8 * p + j
                s[i, j] = jnp.broadcast_to(r[i][:, at : at + 1], (1, LANES))
        c = []
        for i in range(8):
            at = 8 * p + i
            c.append([jnp.broadcast_to(tiles[t][:, at : at + 1], (8, LANES)) for t in later])
        scaled = []
        for i in range(8):
            inv = 1.0 / s[i, i]
            for t in range(i + 1, 8):
                f = s[t, i] * inv
                for u in range(i + 1, t + 1):
                    s[t, u] = s[t, u] - f * s[u, i]
                r[t] = r[t] - f * r[i]
                c[t] = [x - f * y for x, y in zip(c[t], c[i])]
            v_ref[8 * p + i : 8 * p + i + 1, :] = r[i] * (scale / jnp.sqrt(s[i, i]))
            scaled.append(r[i] * inv)
        for x, t in enumerate(later):
            for i in range(8):
                tiles[t] = tiles[t] - c[i][x] * scaled[i]
    return pltpu.roll(v_ref[...], 64, 1)[:, 0:64]


def basis_body(scale, r_ref, loc_ref, suf_ref, entry_ref, out_ref, f_ref, v_ref):
    n, cols, _ = loc_ref.shape
    for k in range(n):
        e = entry_ref[:, 80 + k : 81 + k]
        f_ref[:, k * LANES : (k + 1) * LANES] = loc_ref[k] + suf_ref[k : k + 1, :] * e
    packed = r_ref[0]
    for i in range(1, r_ref.shape[0]):
        packed = packed + r_ref[i]
    unpacked = jnp.concatenate([packed, pltpu.roll(packed, 64, 1)], axis=0)
    inv = inverse_factor(scale, unpacked, v_ref)
    out = jnp.dot(inv, f_ref[...], precision=HIGH, preferred_element_type=F32)
    for k in range(n):
        out_ref[k] = out[:, k * LANES : (k + 1) * LANES]


def in_hbm(value):
    return pltpu.with_memory_space_constraint(value, pltpu.HBM)


def exchange(value, axis):
    return lax.all_to_all(value, axis, 0, 0, tiled=True)


def local(forcing, block_inverse, wall_rates, span_couple):
    n, cols, _, pts = forcing.shape
    peers = lax.axis_size("line")
    stations = lax.axis_size("z") * lax.axis_size("y") * lax.axis_size("core")
    rows = n * stations * pts * peers
    field = (n, cols, pts)
    f, b, w, c = map(in_hbm, (forcing.reshape(field), block_inverse, wall_rates, span_couple))
    across = [(i, (i + 1) % stations if i % 2 else (i - 1) % stations) for i in range(stations)]
    work = 2 * n * n * cols * pts
    scratch = pltpu.VMEM(field, F32)

    start, b, w = call(
        start_body, [field, b.shape, w.shape], work, [scratch, pltpu.SemaphoreType.DMA((3,))], HBM
    )(f, b, w)
    far = lax.ppermute(start, TILE, across)
    near = lax.all_gather(start, "core")
    steps = (len(STEPS), 16, pts)
    wide = pltpu.VMEM((cols, n * pts), F32)
    cb, base, edge, up, down, pre, suf, row, ext = call(
        side_body,
        [(n * n, pts), field, (cols, 32), steps, steps, (16, pts), (16, pts), (8, pts), (64, n * pts)],
        work // 4,
        [wide],
    )(c, b, w, start)
    loc, pay = call(up_body, [field, (peers, 24, pts)], 2 * work, [scratch, wide])(
        cb, base, far, near, up, edge, row
    )
    got = exchange(pay, "line")
    rising, edge = call(enter_body, [field, (16, pts)], work // 4)(got, loc, pre)
    far = lax.ppermute(rising, TILE, across)
    near = lax.all_gather(rising, "core")
    base = call(below_body, field, work // 4)(start, rising, edge, w)
    tall = pltpu.VMEM((2 * cols, n * pts), F32)
    loc, pay = call(down_body, [field, (peers, cols, pts)], 4 * work, [scratch, tall])(
        cb, base, far, near, down, ext
    )
    sums = exchange(pay, "line")
    gram, entry = call(line_body, [(cols // 2, pts), (cols, pts)], work // 4)(sums, got)
    half = (cols // 2, pts)
    both = lax.all_gather(gram, "core")
    gram = call(sum_body, (NY,) + half)(both)
    gram = call(sum_body, (NZ,) + half)(exchange(gram, "y"))
    gram = exchange(gram, "z")

    def basis(*refs):
        basis_body(math.sqrt(rows), *refs)

    out = call(basis, field, 4 * work, [wide, pltpu.VMEM((cols, pts), F32)])(
        gram, loc, suf, entry
    )
    return out.reshape(n, cols, 1, pts)


def solution(mesh):
    devices = mesh.devices.reshape(mesh.shape["line"], NZ, NY, NCORE)
    inner = Mesh(devices, ("line",) + TILE)
    spec = P(None, None, TILE, "line")
    return jax.shard_map(
        local, mesh=inner, in_specs=(spec, spec, spec, P()), out_specs=spec, check_vma=False
    )
```

```python
import math

import jax
import jax.numpy as jnp
from jax import lax
from jax.experimental import pallas as pl
from jax.experimental.pallas import tpu as pltpu
from jax.sharding import Mesh, PartitionSpec as P

NZ, NY, NCORE = 8, 8, 2
TILE = ("z", "y", "core")
HIGH = lax.Precision.HIGHEST
F32 = jnp.float32
LANES = 128
LIMIT = 16 << 20
STEPS = (1, 2, 4, 8, 16, 32, 64)
VMEM = pl.BlockSpec(memory_space=pltpu.VMEM)
SMEM = pl.BlockSpec(memory_space=pltpu.SMEM)
HBM = pl.BlockSpec(memory_space=pltpu.HBM)


def lane_ids(rows):
    return lax.broadcasted_iota(jnp.int32, (rows, LANES), 1)


def row_ids(rows):
    return lax.broadcasted_iota(jnp.int32, (rows, LANES), 0)


def dot_nt(a, b):
    return lax.dot_general(
        a, b, (((1,), (1,)), ((), ())), precision=HIGH, preferred_element_type=F32
    )


def call(body, outs, flops=0, scratch=(), space=VMEM):
    many = isinstance(outs[0], tuple)
    shapes = [jax.ShapeDtypeStruct(s, F32) for s in (outs if many else [outs])]

    def run(*args):
        size = sum(a.size for a in args) + sum(math.prod(s.shape) for s in shapes)
        return pl.pallas_call(
            body,
            out_shape=shapes if many else shapes[0],
            in_specs=[SMEM if a.ndim == 1 else space for a in args],
            out_specs=[VMEM] * len(shapes) if many else VMEM,
            scratch_shapes=list(scratch),
            compiler_params=pltpu.CompilerParams(vmem_limit_bytes=LIMIT),
            cost_estimate=pl.CostEstimate(
                flops=flops, bytes_accessed=4 * size, transcendentals=0
            ),
        )(*args)

    return run


def apply_rows(block, n, take):
    total = block(0) * take(0)
    for m in range(1, n):
        total = total + block(m) * take(m)
    return total


def pick(values, mask):
    total = None
    for _ in range(3):
        piece = values.astype(jnp.bfloat16)
        values = values - piece.astype(F32)
        part = lax.dot_general(
            piece, mask, (((1,), (1,)), ((), ())), preferred_element_type=F32
        )
        total = part if total is None else total + part
    return total


def lane_mask(rows, n, shift, at):
    wide = (rows, n * LANES)
    col = lax.broadcasted_iota(jnp.int32, wide, 1)
    row = lax.broadcasted_iota(jnp.int32, wide, 0)
    return (col == (row - shift) * LANES + at).astype(jnp.bfloat16)


def start_body(f_hbm, b_hbm, w_hbm, s_ref, b_ref, w_ref, f_ref, sems):
    copies = [
        pltpu.make_async_copy(src, dst, sems.at[i])
        for i, (src, dst) in enumerate(((f_hbm, f_ref), (b_hbm, b_ref), (w_hbm, w_ref)))
    ]
    for copy in copies:
        copy.start()
    for copy in copies:
        copy.wait()
    n, cols, _ = f_ref.shape
    for g in range(0, cols, 16):
        vals = [f_ref[m, g : g + 16, :] for m in range(n)]
        for k in range(n):
            s_ref[k, g : g + 16, :] = apply_rows(lambda m: b_ref[k, m], n, lambda m: vals[m])


def side_body(
    c_ref, b_ref, w_ref, s_ref,
    cb_ref, base_ref, edge_ref, up_ref, down_ref, pre_ref, suf_ref, row_ref, ext_ref, a_ref,
):
    n = w_ref.shape[1]
    lane = lane_ids(n)
    up, down = (jnp.concatenate([w_ref[i, k] for k in range(n)], axis=0) for i in range(2))
    pre, suf = up, down
    p = jnp.where(lane >= 1, up, 0.0)
    q = jnp.where(lane < LANES - 1, down, 0.0)
    for i, d in enumerate(STEPS):
        up_ref[i, 0:n, :] = p
        down_ref[i, 0:n, :] = q
        p = p * pltpu.roll(p, d, 1)
        q = q * pltpu.roll(q, LANES - d, 1)
        pre = jnp.where(lane >= d, pre * pltpu.roll(pre, d, 1), pre)
        suf = jnp.where(lane < LANES - d, suf * pltpu.roll(suf, LANES - d, 1), suf)
    pre_ref[0:n, :] = pre
    suf_ref[0:n, :] = suf
    norm = jnp.sum(suf * suf, axis=1, keepdims=True)
    table = jnp.zeros((8, LANES), F32)
    at, row = lane_ids(8), row_ids(8)
    for k in range(n):
        mine = jnp.where(row == 0, pre[k : k + 1, LANES - 1 : LANES], 0.0)
        mine = jnp.where(row == 1, down[k : k + 1, LANES - 1 : LANES], mine)
        mine = jnp.where(row == 2, suf[k : k + 1, 0:1], mine)
        mine = jnp.where(row == 3, norm[k : k + 1, 0:1], mine)
        table = jnp.where(lax.rem(at, 16) == k, mine, table)
    row_ref[...] = table
    place = row_ids(64)
    first = (lane_ids(64) == 0).astype(F32)
    for k in range(n):
        block = jnp.where(place == k, jnp.broadcast_to(suf[k : k + 1, :], (64, LANES)), 0.0)
        block = jnp.where(place == 16 + k, first, block)
        ext_ref[:, k * LANES : (k + 1) * LANES] = block


    inner = lane_ids(64) < LANES - 1
    for k in range(n):
        for m in range(n):
            cb_ref[k * n + m : k * n + m + 1, :] = c_ref[m] * b_ref[k, m]
        start = s_ref[k]
        a_ref[:, k * LANES : (k + 1) * LANES] = start
        above = jnp.where(inner, pltpu.roll(start, LANES - 1, 1), 0.0)
        base_ref[k] = start + w_ref[1, k] * above
    edge_ref[...] = pick(a_ref[...], lane_mask(32, n, 16, 0))


def neighbours_into(h_ref, n_ref, g_ref):
    other = 1 - lax.axis_index("core")
    for m in range(n_ref.shape[0]):
        h_ref[m] = n_ref[m] + g_ref[other, m]


def coupled(cb_ref, h_ref, k, n, rows):
    return apply_rows(
        lambda m: cb_ref[k * n + m : k * n + m + 1, :], n, lambda m: h_ref[m, rows, :]
    )


def up_body(cb_ref, base_ref, n_ref, g_ref, up_ref, edge_ref, row_ref, loc_ref, pay_ref, h_ref, a_ref):
    n, cols, _ = base_ref.shape
    neighbours_into(h_ref, n_ref, g_ref)
    for k in range(n):
        for g in range(cols // 16):
            rows = slice(16 * g, 16 * g + 16)
            v = base_ref[k, rows, :] + coupled(cb_ref, h_ref, k, n, rows)
            for i, d in enumerate(STEPS):
                v = v + up_ref[i, k : k + 1, :] * pltpu.roll(v, d, 1)
            loc_ref[k, rows, :] = v
            a_ref[rows, k * LANES : (k + 1) * LANES] = v
    ends = pick(a_ref[...], lane_mask(32, n, 0, LANES - 1)) + edge_ref[...]
    ends = jnp.concatenate([ends, jnp.zeros((cols, LANES - 32), F32)], axis=1)
    pay = ends[0:16, :]
    for g in range(1, cols // 16):
        pay = pay + pltpu.roll(ends[16 * g : 16 * g + 16, :], 32 * g, 1)
    for peer in range(pay_ref.shape[0]):
        pay_ref[peer, 0:16, :] = pay
        pay_ref[peer, 16:24, :] = row_ref[...]


def enter_body(r_ref, loc_ref, pre_ref, out_ref, edge_ref):
    n, cols, _ = loc_ref.shape
    peers = r_ref.shape[0]
    mine = lax.axis_index("line")
    state = jnp.zeros((16, LANES), F32)
    entry = state
    top = state
    for at in range(peers - 1):
        lead = pltpu.roll(r_ref[at + 1, 0:16, :], LANES - 16, 1)
        tail = r_ref[at, 17:18, :] * lead
        top = jnp.where(mine == at, tail, top)
        state = r_ref[at, 16:17, :] * state + (r_ref[at, 0:16, :] + tail)
        entry = jnp.where(mine == at + 1, state, entry)
    lane = lane_ids(16)
    for k in range(n):
        pre = pre_ref[k : k + 1, :]
        for g in range(cols // 16):
            rows = slice(16 * g, 16 * g + 16)
            at = 32 * g + k
            v = loc_ref[k, rows, :] + pre * entry[:, at : at + 1]
            out_ref[k, rows, :] = jnp.where(lane == LANES - 1, v + top[:, at : at + 1], v)
    edge_ref[...] = entry


def below_body(s_ref, up_ref, edge_ref, w_ref, out_ref):
    n, cols, _ = s_ref.shape
    lane = lane_ids(16)
    entry = edge_ref[...]
    for k in range(n):
        rise = w_ref[0, k]
        for g in range(cols // 16):
            rows = slice(16 * g, 16 * g + 16)
            at = 32 * g + k
            below = pltpu.roll(up_ref[k, rows, :], 1, 1)
            below = jnp.where(lane == 0, entry[:, at : at + 1], below)
            out_ref[k, rows, :] = s_ref[k, rows, :] + rise * below


def down_body(
    cb_ref, base_ref, n_ref, g_ref, down_ref, ext_ref, row_ref, loc_ref, pay_ref, h_ref, a_ref
):
    n, cols, _ = base_ref.shape
    neighbours_into(h_ref, n_ref, g_ref)
    for k in range(n):
        for g in range(cols // 16):
            rows = slice(16 * g, 16 * g + 16)
            v = base_ref[k, rows, :] + coupled(cb_ref, h_ref, k, n, rows)
            for i, d in enumerate(STEPS):
                v = v + down_ref[i, k : k + 1, :] * pltpu.roll(v, LANES - d, 1)
            loc_ref[k, rows, :] = v
            a_ref[rows, k * LANES : (k + 1) * LANES] = v
    a_ref[cols : 2 * cols, :] = ext_ref[...]
    total = dot_nt(a_ref[0:cols, :], a_ref[...])
    lane = lane_ids(16)
    edges = jnp.zeros((16, LANES), F32)
    for g in range(cols // 16):
        moved = pltpu.roll(total[16 * g : 16 * g + 16, :], (32 * g + 64) % LANES, 1)
        edges = jnp.where(lane // 32 == g, moved, edges)
    half = cols // 2
    for peer in range(pay_ref.shape[0]):
        at = half * (peer % NCORE)
        low = pltpu.roll(total[at + 16 : at + 32, :], 64, 1)
        pay_ref[peer, 0:16, :] = jnp.where(lane < 64, total[at : at + 16, :], low)
        pay_ref[peer, 16:32, :] = edges
        pay_ref[peer, 32:40, :] = row_ref[...]


def line_body(r_ref, gram_ref, entry_ref, left_ref, right_ref):
    peers = r_ref.shape[0] // NCORE
    cols = left_ref.shape[0]
    mine, core = lax.axis_index("line"), lax.axis_index("core")
    lane = lane_ids(16)
    first = lane % 32 < 16
    zero = jnp.zeros((16, LANES), F32)
    entry = zero
    for station in range(NCORE):
        state = zero
        left = [zero] * (cols // 16)
        right = [zero] * (cols // 16)
        for at in range(peers - 2, -1, -1):
            above, here = NCORE * (at + 1) + station, NCORE * at + station
            state = r_ref[above, 34:35, :] * state + r_ref[above, 16:32, :]
            entry = jnp.where((mine == at) & (core == station), state, entry)
            back = pltpu.roll(state, LANES - 16, 1)
            cross = r_ref[here, 16:32, :] + (0.5 * r_ref[here, 35:36, :]) * back
            a = jnp.where(first, cross, state)
            b = jnp.where(first, back, pltpu.roll(cross, 16, 1))
            for g in range(cols // 16):
                shift = (32 * (at - g)) % LANES
                left[g] = jnp.where(lane // 32 == at, pltpu.roll(a, shift, 1), left[g])
                right[g] = jnp.where(lane // 32 == at, pltpu.roll(b, shift, 1), right[g])
        for g in range(cols // 16):
            rows = slice(16 * g, 16 * g + 16)
            left_ref[rows, station * LANES : (station + 1) * LANES] = left[g]
            right_ref[rows, station * LANES : (station + 1) * LANES] = right[g]
    half = cols // 2
    mine = left_ref[pl.ds(pl.multiple_of(half * core, half), half), :]
    fix = dot_nt(mine, right_ref[...])
    total = jnp.concatenate([fix[0:16, :], fix[16:32, :]], axis=1)
    for i in range(r_ref.shape[0]):
        total = total + r_ref[i, 0:16, :]
    for peer in range(gram_ref.shape[0]):
        gram_ref[peer] = total
    entry_ref[...] = entry


def sum_body(r_ref, o_ref):
    total = r_ref[0]
    for i in range(1, r_ref.shape[0]):
        total = total + r_ref[i]
    for peer in range(o_ref.shape[0]):
        o_ref[peer] = total


def inverse_factor(scale, gram, v_ref):
    cols = gram.shape[0]
    count = cols // 8
    lane, row = lane_ids(8), row_ids(8)
    tiles = []
    for t in range(count):
        unit = jnp.where(lane - 64 == row + 8 * t, 1.0, 0.0)
        tiles.append(jnp.where(lane < 64, gram[8 * t : 8 * t + 8, :], unit))
    for p in range(count):
        later = range(p + 1, count)
        r = [tiles[p][i : i + 1, :] for i in range(8)]
        s = {}
        for i in range(8):
            for j in range(i + 1):
                at = 8 * p + j
                s[i, j] = jnp.broadcast_to(r[i][:, at : at + 1], (1, LANES))
        c = []
        for i in range(8):
            at = 8 * p + i
            c.append([jnp.broadcast_to(tiles[t][:, at : at + 1], (8, LANES)) for t in later])
        scaled = []
        for i in range(8):
            inv = 1.0 / s[i, i]
            for t in range(i + 1, 8):
                f = s[t, i] * inv
                for u in range(i + 1, t + 1):
                    s[t, u] = s[t, u] - f * s[u, i]
                r[t] = r[t] - f * r[i]
                c[t] = [x - f * y for x, y in zip(c[t], c[i])]
            v_ref[8 * p + i : 8 * p + i + 1, :] = r[i] * (scale / jnp.sqrt(s[i, i]))
            scaled.append(r[i] * inv)
        for x, t in enumerate(later):
            for i in range(8):
                tiles[t] = tiles[t] - c[i][x] * scaled[i]
    return pltpu.roll(v_ref[...], 64, 1)[:, 0:64]


def basis_body(scale, r_ref, loc_ref, suf_ref, entry_ref, out_ref, f_ref, v_ref):
    n, cols, _ = loc_ref.shape
    for k in range(n):
        suf = suf_ref[k : k + 1, :]
        for g in range(cols // 16):
            rows, at = slice(16 * g, 16 * g + 16), 32 * g + 16 + k
            v = loc_ref[k, rows, :] + suf * entry_ref[:, at : at + 1]
            f_ref[rows, k * LANES : (k + 1) * LANES] = v
    parts = []
    for core in range(NCORE):
        packed = r_ref[core]
        for i in range(NCORE + core, r_ref.shape[0], NCORE):
            packed = packed + r_ref[i]
        parts += [packed, pltpu.roll(packed, 64, 1)]
    unpacked = jnp.concatenate(parts, axis=0)
    inv = inverse_factor(scale, unpacked, v_ref)
    out = jnp.dot(inv, f_ref[...], precision=HIGH, preferred_element_type=F32)
    for k in range(n):
        out_ref[k] = out[:, k * LANES : (k + 1) * LANES]


def in_hbm(value):
    return pltpu.with_memory_space_constraint(value, pltpu.HBM)


def exchange(value, axis):
    return lax.all_to_all(value, axis, 0, 0, tiled=True)


def local(forcing, block_inverse, wall_rates, span_couple):
    n, cols, _, pts = forcing.shape
    peers = lax.axis_size("line")
    stations = lax.axis_size("z") * lax.axis_size("y") * lax.axis_size("core")
    rows = n * stations * pts * peers
    field = (n, cols, pts)
    f, b, w, c = map(in_hbm, (forcing.reshape(field), block_inverse, wall_rates, span_couple))
    across = [(i, (i + 1) % stations if i % 2 else (i - 1) % stations) for i in range(stations)]
    work = 2 * n * n * cols * pts
    scratch = pltpu.VMEM(field, F32)

    start, b, w = call(
        start_body, [field, b.shape, w.shape], work, [scratch, pltpu.SemaphoreType.DMA((3,))], HBM
    )(f, b, w)
    far = lax.ppermute(start, TILE, across)
    near = lax.all_gather(start, "core")
    steps = (len(STEPS), 16, pts)
    wide = pltpu.VMEM((cols, n * pts), F32)
    cb, base, edge, up, down, pre, suf, row, ext = call(
        side_body,
        [(n * n, pts), field, (cols, 32), steps, steps, (16, pts), (16, pts), (8, pts), (64, n * pts)],
        work // 4,
        [wide],
    )(c, b, w, start)
    loc, pay = call(up_body, [field, (peers, 24, pts)], 2 * work, [scratch, wide])(
        cb, base, far, near, up, edge, row
    )
    got = exchange(pay, "line")
    rising, edge = call(enter_body, [field, (16, pts)], work // 4)(got, loc, pre)
    far = lax.ppermute(rising, TILE, across)
    near = lax.all_gather(rising, "core")
    base = call(below_body, field, work // 4)(start, rising, edge, w)
    tall = pltpu.VMEM((2 * cols, n * pts), F32)
    loc, pay = call(down_body, [field, (peers * NCORE, 40, pts)], 4 * work, [scratch, tall])(
        cb, base, far, near, down, ext, row
    )
    side = pltpu.VMEM((cols, NCORE * pts), F32)
    part = (cols // 4, pts)
    gram, entry = call(line_body, [(NY,) + part, (16, pts)], work // 4, [side, side])(
        exchange(pay, ("line", "core"))
    )
    gram = call(sum_body, (NZ * NCORE,) + part)(exchange(gram, "y"))
    gram = exchange(gram, ("z", "core"))

    def basis(*refs):
        basis_body(math.sqrt(rows), *refs)

    out = call(basis, field, 4 * work, [wide, pltpu.VMEM((cols, pts), F32)])(
        gram, loc, suf, entry
    )
    return out.reshape(n, cols, 1, pts)


def solution(mesh):
    devices = mesh.devices.reshape(mesh.shape["line"], NZ, NY, NCORE)
    inner = Mesh(devices, ("line",) + TILE)
    spec = P(None, None, TILE, "line")
    return jax.shard_map(
        local, mesh=inner, in_specs=(spec, spec, spec, P()), out_specs=spec, check_vma=False
    )
```

```python
import math

import jax
import jax.numpy as jnp
from jax import lax
from jax.experimental import pallas as pl
from jax.experimental.pallas import tpu as pltpu
from jax.sharding import Mesh, PartitionSpec as P

NZ, NY, NCORE = 8, 8, 2
TILE = ("z", "y", "core")
HIGH = lax.Precision.HIGHEST
F32 = jnp.float32
LANES = 128
LIMIT = 16 << 20
STEPS = (1, 2, 4, 8, 16, 32, 64)
VMEM = pl.BlockSpec(memory_space=pltpu.VMEM)
SMEM = pl.BlockSpec(memory_space=pltpu.SMEM)
HBM = pl.BlockSpec(memory_space=pltpu.HBM)


def lane_ids(rows):
    return lax.broadcasted_iota(jnp.int32, (rows, LANES), 1)


def row_ids(rows):
    return lax.broadcasted_iota(jnp.int32, (rows, LANES), 0)


def dot_nt(a, b):
    return lax.dot_general(
        a, b, (((1,), (1,)), ((), ())), precision=HIGH, preferred_element_type=F32
    )


def call(body, outs, flops=0, scratch=(), space=VMEM):
    many = isinstance(outs[0], tuple)
    shapes = [jax.ShapeDtypeStruct(s, F32) for s in (outs if many else [outs])]

    def run(*args):
        size = sum(a.size for a in args) + sum(math.prod(s.shape) for s in shapes)
        return pl.pallas_call(
            body,
            out_shape=shapes if many else shapes[0],
            in_specs=[SMEM if a.ndim == 1 else space for a in args],
            out_specs=[VMEM] * len(shapes) if many else VMEM,
            scratch_shapes=list(scratch),
            compiler_params=pltpu.CompilerParams(vmem_limit_bytes=LIMIT),
            cost_estimate=pl.CostEstimate(
                flops=flops, bytes_accessed=4 * size, transcendentals=0
            ),
        )(*args)

    return run


def apply_rows(block, n, take):
    total = block(0) * take(0)
    for m in range(1, n):
        total = total + block(m) * take(m)
    return total


def pick(values, mask):
    total = None
    for _ in range(3):
        piece = values.astype(jnp.bfloat16)
        values = values - piece.astype(F32)
        part = lax.dot_general(
            piece, mask, (((1,), (1,)), ((), ())), preferred_element_type=F32
        )
        total = part if total is None else total + part
    return total


def lane_mask(rows, n, shift, at):
    wide = (rows, n * LANES)
    col = lax.broadcasted_iota(jnp.int32, wide, 1)
    row = lax.broadcasted_iota(jnp.int32, wide, 0)
    return (col == (row - shift) * LANES + at).astype(jnp.bfloat16)


def start_body(f_hbm, b_hbm, w_hbm, s_ref, pack_ref, f_ref, b_ref, w_ref, sems):
    copies = [
        pltpu.make_async_copy(src, dst, sems.at[i])
        for i, (src, dst) in enumerate(((f_hbm, f_ref), (b_hbm, b_ref), (w_hbm, w_ref)))
    ]
    for copy in copies:
        copy.start()
    for copy in copies:
        copy.wait()
    n, cols, _ = f_ref.shape
    for g in range(0, cols, 16):
        vals = [f_ref[m, g : g + 16, :] for m in range(n)]
        for k in range(n):
            v = apply_rows(lambda m: b_ref[k, m], n, lambda m: vals[m])
            s_ref[k * cols + g : k * cols + g + 16, :] = v
            pack_ref[k * cols + g : k * cols + g + 16, :] = v
    at = n * cols
    for k in range(n):
        for m in range(n):
            pack_ref[at + k * n + m : at + k * n + m + 1, :] = b_ref[k, m]
    at += n * n
    for i in range(2):
        for k in range(n):
            pack_ref[at + i * n + k : at + i * n + k + 1, :] = w_ref[i, k]


def rate_tables(up, down):
    n = up.shape[0]
    lane = lane_ids(n)
    pre, suf = up, down
    p = jnp.where(lane >= 1, up, 0.0)
    q = jnp.where(lane < LANES - 1, down, 0.0)
    ps, qs = [], []
    for d in STEPS:
        ps.append(p)
        qs.append(q)
        p = p * pltpu.roll(p, d, 1)
        q = q * pltpu.roll(q, LANES - d, 1)
        pre = jnp.where(lane >= d, pre * pltpu.roll(pre, d, 1), pre)
        suf = jnp.where(lane < LANES - d, suf * pltpu.roll(suf, LANES - d, 1), suf)
    norm = jnp.sum(suf * suf, axis=1, keepdims=True)
    table = jnp.zeros((8, LANES), F32)
    at, row = lane_ids(8), row_ids(8)
    for k in range(n):
        mine = jnp.where(row == 0, pre[k : k + 1, LANES - 1 : LANES], 0.0)
        mine = jnp.where(row == 1, down[k : k + 1, LANES - 1 : LANES], mine)
        mine = jnp.where(row == 2, suf[k : k + 1, 0:1], mine)
        mine = jnp.where(row == 3, norm[k : k + 1, 0:1], mine)
        table = jnp.where(lax.rem(at, 16) == k, mine, table)
    return ps, qs, pre, suf, table


def sweep_tables(n, cols, pack_ref, base_ref, edge_ref, up_ref, pre_ref, row_ref, a_ref):
    at = n * cols + n * n
    up, down = pack_ref[at : at + n, :], pack_ref[at + n : at + 2 * n, :]
    ps, qs, pre, suf, table = rate_tables(up, down)
    for i, p in enumerate(ps):
        up_ref[i, 0:n, :] = p
    pre_ref[0:n, :] = pre
    row_ref[...] = table
    inner = lane_ids(cols) < LANES - 1
    for k in range(n):
        start = pack_ref[k * cols : (k + 1) * cols, :]
        a_ref[:, k * LANES : (k + 1) * LANES] = start
        above = jnp.where(inner, pltpu.roll(start, LANES - 1, 1), 0.0)
        base_ref[k] = start + down[k : k + 1, :] * above
    edge_ref[...] = pick(a_ref[...], lane_mask(32, n, 16, 0))
    return qs, suf


def side_body(
    pack_ref, base_ref, edge_ref, up_ref, pre_ref, row_ref, down_ref, suf_ref, ext_ref, a_ref
):
    n, cols, _ = base_ref.shape
    qs, suf = sweep_tables(n, cols, pack_ref, base_ref, edge_ref, up_ref, pre_ref, row_ref, a_ref)
    for i, q in enumerate(qs):
        down_ref[i, 0:n, :] = q
    suf_ref[0:n, :] = suf
    place = row_ids(64)
    first = (lane_ids(64) == 0).astype(F32)
    for k in range(n):
        block = jnp.where(place == k, jnp.broadcast_to(suf[k : k + 1, :], (64, LANES)), 0.0)
        block = jnp.where(place == 16 + k, first, block)
        ext_ref[:, k * LANES : (k + 1) * LANES] = block


def far_side_body(pack_ref, base_ref, edge_ref, up_ref, pre_ref, row_ref, a_ref):
    n, cols, _ = base_ref.shape
    sweep_tables(n, cols, pack_ref, base_ref, edge_ref, up_ref, pre_ref, row_ref, a_ref)


def coupled(pack_ref, h_ref, k, n, rows):
    at = n * h_ref.shape[1] + k * n
    return apply_rows(
        lambda m: pack_ref[at + m : at + m + 1, :], n, lambda m: h_ref[m, rows, :]
    )


def rise(c_ref, pack_ref, base_ref, one, two, up_ref, edge_ref, row_ref, loc_ref, h_ref, a_ref):
    n, cols, _ = base_ref.shape
    for m in range(n):
        rows = slice(m * cols, (m + 1) * cols)
        h_ref[m] = c_ref[m] * (one(rows) + two(rows))
    for k in range(n):
        for g in range(cols // 16):
            rows = slice(16 * g, 16 * g + 16)
            v = base_ref[k, rows, :] + coupled(pack_ref, h_ref, k, n, rows)
            for i, d in enumerate(STEPS):
                v = v + up_ref[i, k : k + 1, :] * pltpu.roll(v, d, 1)
            loc_ref[k * cols + 16 * g : k * cols + 16 * g + 16, :] = v
            a_ref[rows, k * LANES : (k + 1) * LANES] = v
    ends = pick(a_ref[...], lane_mask(32, n, 0, LANES - 1)) + edge_ref[...]
    ends = jnp.concatenate([ends, jnp.zeros((cols, LANES - 32), F32)], axis=1)
    pay = ends[0:16, :]
    for g in range(1, cols // 16):
        pay = pay + pltpu.roll(ends[16 * g : 16 * g + 16, :], 32 * g, 1)
    return jnp.concatenate([pay, row_ref[...]], axis=0)


def own_body(
    c_ref, pack_ref, base_ref, far_ref, near_ref, up_ref, edge_ref, row_ref, pre_ref,
    buf_ref, h_ref, a_ref,
):
    size = base_ref.shape[0] * base_ref.shape[1]
    other = 1 - lax.axis_index("core")
    pay = rise(
        c_ref, pack_ref, base_ref, lambda rows: far_ref[rows, :], lambda rows: near_ref[other, rows, :],
        up_ref, edge_ref, row_ref, buf_ref, h_ref, a_ref,
    )
    buf_ref[size : size + 24, :] = pay
    buf_ref[size + 24 : size + 40, :] = pre_ref[...]


def far_body(
    c_ref, pack_ref, base_ref, start_ref, next_ref, up_ref, edge_ref, row_ref, buf_ref, both_ref,
    loc_ref, pay_ref, h_ref, a_ref,
):
    size = base_ref.shape[0] * base_ref.shape[1]
    other = 1 - lax.axis_index("core")
    pay = rise(
        c_ref, pack_ref, base_ref, lambda rows: start_ref[rows, :], lambda rows: next_ref[rows, :],
        up_ref, edge_ref, row_ref, loc_ref, h_ref, a_ref,
    )
    for peer in range(pay_ref.shape[0]):
        pay_ref[peer, 0:24, :] = buf_ref[size : size + 24, :]
        pay_ref[peer, 24:48, :] = both_ref[other, size : size + 24, :]
        pay_ref[peer, 48:72, :] = pay


def entering(r_ref, station):
    mine = lax.axis_index("line")
    at0 = 24 * station
    state = jnp.zeros((16, LANES), F32)
    entry = state
    top = state
    for at in range(r_ref.shape[0] - 1):
        lead = pltpu.roll(r_ref[at + 1, at0 : at0 + 16, :], LANES - 16, 1)
        tail = r_ref[at, at0 + 17 : at0 + 18, :] * lead
        top = jnp.where(mine == at, tail, top)
        state = r_ref[at, at0 + 16 : at0 + 17, :] * state + (r_ref[at, at0 : at0 + 16, :] + tail)
        entry = jnp.where(mine == at + 1, state, entry)
    return entry, top


def down_body(
    c_ref, pack_ref, r_ref, buf_ref, both_ref, floc_ref, fpre_ref, down_ref, ext_ref, row_ref,
    loc_ref, pay_ref, h_ref, a_ref,
):
    n, cols, _ = loc_ref.shape
    size = n * cols
    other = 1 - lax.axis_index("core")
    mine, _ = entering(r_ref, 0)
    near, near_top = entering(r_ref, 1)
    far, far_top = entering(r_ref, 2)
    top = near_top + far_top
    lane = lane_ids(16)
    last, first = lane == LANES - 1, lane == 0
    for m in range(n):
        npre = both_ref[other, size + 24 + m : size + 25 + m, :]
        fpre = fpre_ref[m : m + 1, :]
        for g in range(cols // 16):
            rows, at = slice(m * cols + 16 * g, m * cols + 16 * g + 16), 32 * g + m
            v = both_ref[other, rows, :] + floc_ref[rows, :]
            v = v + npre * near[:, at : at + 1] + fpre * far[:, at : at + 1]
            h_ref[m, 16 * g : 16 * g + 16, :] = c_ref[m] * jnp.where(last, v + top[:, at : at + 1], v)
    one = lane_ids(1) == 0
    for k in range(n):
        up = pack_ref[size + n * n + k : size + n * n + k + 1, :]
        pre = buf_ref[size + 24 + k : size + 25 + k, :]
        pre = jnp.where(one, 1.0, pltpu.roll(pre, 1, 1))
        for g in range(cols // 16):
            rows = slice(16 * g, 16 * g + 16)
            wide, at = slice(k * cols + 16 * g, k * cols + 16 * g + 16), 32 * g + k
            below = jnp.where(first, 0.0, pltpu.roll(buf_ref[wide, :], 1, 1)) + pre * mine[:, at : at + 1]
            v = pack_ref[wide, :] + up * below + coupled(pack_ref, h_ref, k, n, rows)
            for i, d in enumerate(STEPS):
                v = v + down_ref[i, k : k + 1, :] * pltpu.roll(v, LANES - d, 1)
            loc_ref[k, rows, :] = v
            a_ref[rows, k * LANES : (k + 1) * LANES] = v
    a_ref[cols : 2 * cols, :] = ext_ref[...]
    total = dot_nt(a_ref[0:cols, :], a_ref[...])
    lane = lane_ids(16)
    edges = jnp.zeros((16, LANES), F32)
    for g in range(cols // 16):
        moved = pltpu.roll(total[16 * g : 16 * g + 16, :], (32 * g + 64) % LANES, 1)
        edges = jnp.where(lane // 32 == g, moved, edges)
    half = cols // 2
    for peer in range(pay_ref.shape[0]):
        at = half * (peer % NCORE)
        low = pltpu.roll(total[at + 16 : at + 32, :], 64, 1)
        pay_ref[peer, 0:16, :] = jnp.where(lane < 64, total[at : at + 16, :], low)
        pay_ref[peer, 16:32, :] = edges
        pay_ref[peer, 32:40, :] = row_ref[...]


def line_body(r_ref, gram_ref, entry_ref, left_ref, right_ref):
    peers = r_ref.shape[0] // NCORE
    cols = left_ref.shape[0]
    mine, core = lax.axis_index("line"), lax.axis_index("core")
    lane = lane_ids(16)
    first = lane % 32 < 16
    zero = jnp.zeros((16, LANES), F32)
    entry = zero
    for station in range(NCORE):
        state = zero
        left = [zero] * (cols // 16)
        right = [zero] * (cols // 16)
        for at in range(peers - 2, -1, -1):
            above, here = NCORE * (at + 1) + station, NCORE * at + station
            state = r_ref[above, 34:35, :] * state + r_ref[above, 16:32, :]
            entry = jnp.where((mine == at) & (core == station), state, entry)
            back = pltpu.roll(state, LANES - 16, 1)
            cross = r_ref[here, 16:32, :] + (0.5 * r_ref[here, 35:36, :]) * back
            a = jnp.where(first, cross, state)
            b = jnp.where(first, back, pltpu.roll(cross, 16, 1))
            for g in range(cols // 16):
                shift = (32 * (at - g)) % LANES
                left[g] = jnp.where(lane // 32 == at, pltpu.roll(a, shift, 1), left[g])
                right[g] = jnp.where(lane // 32 == at, pltpu.roll(b, shift, 1), right[g])
        for g in range(cols // 16):
            rows = slice(16 * g, 16 * g + 16)
            left_ref[rows, station * LANES : (station + 1) * LANES] = left[g]
            right_ref[rows, station * LANES : (station + 1) * LANES] = right[g]
    half = cols // 2
    mine = left_ref[pl.ds(pl.multiple_of(half * core, half), half), :]
    fix = dot_nt(mine, right_ref[...])
    total = jnp.concatenate([fix[0:16, :], fix[16:32, :]], axis=1)
    for i in range(r_ref.shape[0]):
        total = total + r_ref[i, 0:16, :]
    for peer in range(gram_ref.shape[0]):
        gram_ref[peer] = total
    entry_ref[...] = entry


def sum_body(r_ref, o_ref):
    total = r_ref[0]
    for i in range(1, r_ref.shape[0]):
        total = total + r_ref[i]
    for peer in range(o_ref.shape[0]):
        o_ref[peer] = total


def inverse_factor(scale, gram, v_ref):
    cols = gram.shape[0]
    count = cols // 8
    lane, row = lane_ids(8), row_ids(8)
    tiles = []
    for t in range(count):
        unit = jnp.where(lane - 64 == row + 8 * t, 1.0, 0.0)
        tiles.append(jnp.where(lane < 64, gram[8 * t : 8 * t + 8, :], unit))
    for p in range(count):
        later = range(p + 1, count)
        r = [tiles[p][i : i + 1, :] for i in range(8)]
        s = {}
        for i in range(8):
            for j in range(i + 1):
                at = 8 * p + j
                s[i, j] = jnp.broadcast_to(r[i][:, at : at + 1], (1, LANES))
        c = []
        for i in range(8):
            at = 8 * p + i
            c.append([jnp.broadcast_to(tiles[t][:, at : at + 1], (8, LANES)) for t in later])
        scaled = []
        for i in range(8):
            inv = 1.0 / s[i, i]
            for t in range(i + 1, 8):
                f = s[t, i] * inv
                for u in range(i + 1, t + 1):
                    s[t, u] = s[t, u] - f * s[u, i]
                r[t] = r[t] - f * r[i]
                c[t] = [x - f * y for x, y in zip(c[t], c[i])]
            v_ref[8 * p + i : 8 * p + i + 1, :] = r[i] * (scale / jnp.sqrt(s[i, i]))
            scaled.append(r[i] * inv)
        for x, t in enumerate(later):
            for i in range(8):
                tiles[t] = tiles[t] - c[i][x] * scaled[i]
    return pltpu.roll(v_ref[...], 64, 1)[:, 0:64]


def basis_body(scale, r_ref, loc_ref, suf_ref, entry_ref, out_ref, f_ref, v_ref):
    n, cols, _ = loc_ref.shape
    for k in range(n):
        suf = suf_ref[k : k + 1, :]
        for g in range(cols // 16):
            rows, at = slice(16 * g, 16 * g + 16), 32 * g + 16 + k
            v = loc_ref[k, rows, :] + suf * entry_ref[:, at : at + 1]
            f_ref[rows, k * LANES : (k + 1) * LANES] = v
    parts = []
    for core in range(NCORE):
        packed = r_ref[core]
        for i in range(NCORE + core, r_ref.shape[0], NCORE):
            packed = packed + r_ref[i]
        parts += [packed, pltpu.roll(packed, 64, 1)]
    unpacked = jnp.concatenate(parts, axis=0)
    inv = inverse_factor(scale, unpacked, v_ref)
    out = jnp.dot(inv, f_ref[...], precision=HIGH, preferred_element_type=F32)
    for k in range(n):
        out_ref[k] = out[:, k * LANES : (k + 1) * LANES]


def in_hbm(value):
    return pltpu.with_memory_space_constraint(value, pltpu.HBM)


def exchange(value, axis):
    return lax.all_to_all(value, axis, 0, 0, tiled=True)


def local(forcing, block_inverse, wall_rates, span_couple):
    n, cols, _, pts = forcing.shape
    peers = lax.axis_size("line")
    stations = lax.axis_size("z") * lax.axis_size("y") * lax.axis_size("core")
    rows = n * stations * pts * peers
    field = (n, cols, pts)
    f, b, w, c = map(in_hbm, (forcing.reshape(field), block_inverse, wall_rates, span_couple))
    pairs = [(i, 1 if i % 2 else -1) for i in range(stations)]
    across = [(i, (i + d) % stations) for i, d in pairs]
    beyond = [(i, (i - 2 * d) % stations) for i, d in pairs]
    work = 2 * n * n * cols * pts
    size = n * cols
    scratch = pltpu.VMEM(field, F32)
    wide = pltpu.VMEM((cols, n * pts), F32)
    tall = pltpu.VMEM((2 * cols, n * pts), F32)

    inputs = [pltpu.VMEM(a.shape, F32) for a in (f, b, w)]
    start, pack = call(
        start_body,
        [(size, pts), (size + n * n + 2 * n, pts)],
        work,
        inputs + [pltpu.SemaphoreType.DMA((3,))],
        HBM,
    )(f, b, w)
    fpack = lax.ppermute(pack, TILE, across)
    near = lax.all_gather(start, "core")
    steps, rows16 = (len(STEPS), 16, pts), (16, pts)
    tables = [field, (cols, 32), steps, rows16, (8, pts)]
    base, edge, up, pre, row, down, suf, ext = call(
        side_body, tables + [steps, rows16, (64, n * pts)], work // 4, [wide]
    )(pack)
    held, _, _ = lax.optimization_barrier((start, near, base))
    beyond = lax.ppermute(held, TILE, beyond)
    buf = call(own_body, [(size + 40, pts)], 2 * work, [scratch, wide])(
        c, pack, base, fpack, near, up, edge, row, pre
    )[0]
    both = lax.all_gather(buf, "core")
    fbase, fedge, fup, fpre, frow = call(far_side_body, tables, work // 4, [wide])(fpack)
    floc, pay = call(far_body, [(size, pts), (peers, 72, pts)], 2 * work, [scratch, wide])(
        c, fpack, fbase, start, beyond, fup, fedge, frow, buf, both
    )
    got = exchange(pay, "line")
    loc, pay = call(down_body, [field, (peers * NCORE, 40, pts)], 4 * work, [scratch, tall])(
        c, pack, got, buf, both, floc, fpre, down, ext, row
    )
    side = pltpu.VMEM((cols, NCORE * pts), F32)
    part = (cols // 4, pts)
    gram, entry = call(line_body, [(NY,) + part, (16, pts)], work // 4, [side, side])(
        exchange(pay, ("line", "core"))
    )
    gram = call(sum_body, (NZ * NCORE,) + part)(exchange(gram, "y"))
    gram = exchange(gram, ("z", "core"))

    def basis(*refs):
        basis_body(math.sqrt(rows), *refs)

    out = call(basis, field, 4 * work, [wide, pltpu.VMEM((cols, pts), F32)])(
        gram, loc, suf, entry
    )
    return out.reshape(n, cols, 1, pts)


def solution(mesh):
    devices = mesh.devices.reshape(mesh.shape["line"], NZ, NY, NCORE)
    inner = Mesh(devices, ("line",) + TILE)
    spec = P(None, None, TILE, "line")
    return jax.shard_map(
        local, mesh=inner, in_specs=(spec, spec, spec, P()), out_specs=spec, check_vma=False
    )
```

```python
import math

import jax
import jax.numpy as jnp
from jax import lax
from jax.experimental import pallas as pl
from jax.experimental.pallas import tpu as pltpu
from jax.sharding import Mesh, PartitionSpec as P

NZ, NY, NCORE = 8, 8, 2
TILE = ("z", "y", "core")
HIGH = lax.Precision.HIGHEST
F32 = jnp.float32
LANES = 128
LIMIT = 16 << 20
STEPS = (1, 2, 4, 8, 16, 32, 64)
VMEM = pl.BlockSpec(memory_space=pltpu.VMEM)
HBM = pl.BlockSpec(memory_space=pltpu.HBM)


def lane_ids(rows):
    return lax.broadcasted_iota(jnp.int32, (rows, LANES), 1)


def row_ids(rows):
    return lax.broadcasted_iota(jnp.int32, (rows, LANES), 0)


def dot_nt(a, b):
    return lax.dot_general(
        a, b, (((1,), (1,)), ((), ())), precision=HIGH, preferred_element_type=F32
    )


def call(body, outs, flops=0, scratch=(), space=VMEM):
    many = isinstance(outs[0], tuple)
    shapes = [jax.ShapeDtypeStruct(s, F32) for s in (outs if many else [outs])]

    def run(*args):
        size = sum(a.size for a in args) + sum(math.prod(s.shape) for s in shapes)
        return pl.pallas_call(
            body,
            out_shape=shapes if many else shapes[0],
            in_specs=[space] * len(args),
            out_specs=[VMEM] * len(shapes) if many else VMEM,
            scratch_shapes=list(scratch),
            compiler_params=pltpu.CompilerParams(vmem_limit_bytes=LIMIT),
            cost_estimate=pl.CostEstimate(
                flops=flops, bytes_accessed=4 * size, transcendentals=0
            ),
        )(*args)

    return run


def apply_rows(block, n, take):
    total = block(0) * take(0)
    for m in range(1, n):
        total = total + block(m) * take(m)
    return total


def pick(values, mask):
    total = None
    for _ in range(3):
        piece = values.astype(jnp.bfloat16)
        values = values - piece.astype(F32)
        part = lax.dot_general(
            piece, mask, (((1,), (1,)), ((), ())), preferred_element_type=F32
        )
        total = part if total is None else total + part
    return total


def lane_mask(rows, n, shift, at):
    wide = (rows, n * LANES)
    col = lax.broadcasted_iota(jnp.int32, wide, 1)
    row = lax.broadcasted_iota(jnp.int32, wide, 0)
    return (col == (row - shift) * LANES + at).astype(jnp.bfloat16)


def start_body(f_hbm, b_hbm, w_hbm, c_hbm, s_ref, pack_ref, f_ref, b_ref, w_ref, c_ref, sems):
    copies = [
        pltpu.make_async_copy(src, dst, sems.at[i])
        for i, (src, dst) in enumerate(
            ((f_hbm, f_ref), (b_hbm, b_ref), (w_hbm, w_ref), (c_hbm, c_ref))
        )
    ]
    for copy in copies:
        copy.start()
    for copy in copies:
        copy.wait()
    n, cols, _ = f_ref.shape
    for g in range(0, cols, 16):
        vals = [f_ref[m, g : g + 16, :] for m in range(n)]
        for k in range(n):
            v = apply_rows(lambda m: b_ref[k, m], n, lambda m: vals[m])
            s_ref[k * cols + g : k * cols + g + 16, :] = v
            pack_ref[k * cols + g : k * cols + g + 16, :] = v
    at = n * cols
    for k in range(n):
        for m in range(n):
            pack_ref[at + k * n + m : at + k * n + m + 1, :] = c_ref[m] * b_ref[k, m]
    at += n * n
    for i in range(2):
        for k in range(n):
            pack_ref[at + i * n + k : at + i * n + k + 1, :] = w_ref[i, k]


def rate_tables(up, down):
    n = up.shape[0]
    lane = lane_ids(n)
    pre, suf = up, down
    p = jnp.where(lane >= 1, up, 0.0)
    q = jnp.where(lane < LANES - 1, down, 0.0)
    ps, qs = [], []
    for d in STEPS:
        ps.append(p)
        qs.append(q)
        p = p * pltpu.roll(p, d, 1)
        q = q * pltpu.roll(q, LANES - d, 1)
        pre = jnp.where(lane >= d, pre * pltpu.roll(pre, d, 1), pre)
        suf = jnp.where(lane < LANES - d, suf * pltpu.roll(suf, LANES - d, 1), suf)
    norm = jnp.sum(suf * suf, axis=1, keepdims=True)
    table = jnp.zeros((8, LANES), F32)
    at, row = lane_ids(8), row_ids(8)
    for k in range(n):
        mine = jnp.where(row == 0, pre[k : k + 1, LANES - 1 : LANES], 0.0)
        mine = jnp.where(row == 1, down[k : k + 1, LANES - 1 : LANES], mine)
        mine = jnp.where(row == 2, suf[k : k + 1, 0:1], mine)
        mine = jnp.where(row == 3, norm[k : k + 1, 0:1], mine)
        table = jnp.where(lax.rem(at, 16) == k, mine, table)
    return ps, qs, pre, suf, table


def sweep_tables(n, cols, pack_ref, base_ref, edge_ref, up_ref, pre_ref, row_ref, a_ref):
    at = n * cols + n * n
    up, down = pack_ref[at : at + n, :], pack_ref[at + n : at + 2 * n, :]
    ps, qs, pre, suf, table = rate_tables(up, down)
    for i, p in enumerate(ps):
        up_ref[i, 0:n, :] = p
    pre_ref[0:n, :] = pre
    row_ref[...] = table
    inner = lane_ids(cols) < LANES - 1
    for k in range(n):
        start = pack_ref[k * cols : (k + 1) * cols, :]
        a_ref[:, k * LANES : (k + 1) * LANES] = start
        above = jnp.where(inner, pltpu.roll(start, LANES - 1, 1), 0.0)
        base_ref[k] = start + down[k : k + 1, :] * above
    edge_ref[...] = pick(a_ref[...], lane_mask(32, n, 16, 0))
    return qs, suf


def side_body(
    pack_ref, base_ref, edge_ref, up_ref, pre_ref, row_ref, down_ref, suf_ref, ext_ref, a_ref
):
    n, cols, _ = base_ref.shape
    qs, suf = sweep_tables(n, cols, pack_ref, base_ref, edge_ref, up_ref, pre_ref, row_ref, a_ref)
    for i, q in enumerate(qs):
        down_ref[i, 0:n, :] = q
    suf_ref[0:n, :] = suf
    place = row_ids(64)
    first = (lane_ids(64) == 0).astype(F32)
    for k in range(n):
        block = jnp.where(place == k, jnp.broadcast_to(suf[k : k + 1, :], (64, LANES)), 0.0)
        block = jnp.where(place == 16 + k, first, block)
        ext_ref[:, k * LANES : (k + 1) * LANES] = block


def far_side_body(pack_ref, base_ref, edge_ref, up_ref, pre_ref, row_ref, a_ref):
    n, cols, _ = base_ref.shape
    sweep_tables(n, cols, pack_ref, base_ref, edge_ref, up_ref, pre_ref, row_ref, a_ref)


def coupled(pack_ref, h_ref, k, n, rows):
    at = n * h_ref.shape[1] + k * n
    return apply_rows(
        lambda m: pack_ref[at + m : at + m + 1, :], n, lambda m: h_ref[m, rows, :]
    )


def rise(pack_ref, base_ref, one, two, up_ref, edge_ref, row_ref, loc_ref, h_ref, a_ref):
    n, cols, _ = base_ref.shape
    for m in range(n):
        rows = slice(m * cols, (m + 1) * cols)
        h_ref[m] = one(rows) + two(rows)
    for k in range(n):
        for g in range(cols // 16):
            rows = slice(16 * g, 16 * g + 16)
            v = base_ref[k, rows, :] + coupled(pack_ref, h_ref, k, n, rows)
            for i, d in enumerate(STEPS):
                v = v + up_ref[i, k : k + 1, :] * pltpu.roll(v, d, 1)
            loc_ref[k * cols + 16 * g : k * cols + 16 * g + 16, :] = v
            a_ref[rows, k * LANES : (k + 1) * LANES] = v
    ends = pick(a_ref[...], lane_mask(32, n, 0, LANES - 1)) + edge_ref[...]
    ends = jnp.concatenate([ends, jnp.zeros((cols, LANES - 32), F32)], axis=1)
    pay = ends[0:16, :]
    for g in range(1, cols // 16):
        pay = pay + pltpu.roll(ends[16 * g : 16 * g + 16, :], 32 * g, 1)
    return jnp.concatenate([pay, row_ref[...]], axis=0)


def own_body(
    pack_ref, base_ref, far_ref, near_ref, up_ref, edge_ref, row_ref, pre_ref,
    buf_ref, h_ref, a_ref,
):
    size = base_ref.shape[0] * base_ref.shape[1]
    other = 1 - lax.axis_index("core")
    pay = rise(
        pack_ref, base_ref, lambda rows: far_ref[rows, :], lambda rows: near_ref[other, rows, :],
        up_ref, edge_ref, row_ref, buf_ref, h_ref, a_ref,
    )
    buf_ref[size : size + 24, :] = pay
    buf_ref[size + 24 : size + 40, :] = pre_ref[...]


def far_body(
    pack_ref, base_ref, start_ref, next_ref, up_ref, edge_ref, row_ref, buf_ref, both_ref,
    loc_ref, pay_ref, h_ref, a_ref,
):
    size = base_ref.shape[0] * base_ref.shape[1]
    other = 1 - lax.axis_index("core")
    pay = rise(
        pack_ref, base_ref, lambda rows: start_ref[rows, :], lambda rows: next_ref[rows, :],
        up_ref, edge_ref, row_ref, loc_ref, h_ref, a_ref,
    )
    for peer in range(pay_ref.shape[0]):
        pay_ref[peer, 0:24, :] = buf_ref[size : size + 24, :]
        pay_ref[peer, 24:48, :] = both_ref[other, size : size + 24, :]
        pay_ref[peer, 48:72, :] = pay


def entering(r_ref, station):
    mine = lax.axis_index("line")
    at0 = 24 * station
    state = jnp.zeros((16, LANES), F32)
    entry = state
    top = state
    for at in range(r_ref.shape[0] - 1):
        lead = pltpu.roll(r_ref[at + 1, at0 : at0 + 16, :], LANES - 16, 1)
        tail = r_ref[at, at0 + 17 : at0 + 18, :] * lead
        top = jnp.where(mine == at, tail, top)
        state = r_ref[at, at0 + 16 : at0 + 17, :] * state + (r_ref[at, at0 : at0 + 16, :] + tail)
        entry = jnp.where(mine == at + 1, state, entry)
    return entry, top


def down_body(
    pack_ref, r_ref, buf_ref, both_ref, floc_ref, fpre_ref, down_ref, ext_ref, row_ref,
    loc_ref, pay_ref, h_ref, a_ref,
):
    n, cols, _ = loc_ref.shape
    size = n * cols
    other = 1 - lax.axis_index("core")
    mine, _ = entering(r_ref, 0)
    near, near_top = entering(r_ref, 1)
    far, far_top = entering(r_ref, 2)
    top = near_top + far_top
    lane = lane_ids(16)
    last, first = lane == LANES - 1, lane == 0
    for m in range(n):
        npre = both_ref[other, size + 24 + m : size + 25 + m, :]
        fpre = fpre_ref[m : m + 1, :]
        for g in range(cols // 16):
            rows, at = slice(m * cols + 16 * g, m * cols + 16 * g + 16), 32 * g + m
            v = both_ref[other, rows, :] + floc_ref[rows, :]
            v = v + npre * near[:, at : at + 1] + fpre * far[:, at : at + 1]
            h_ref[m, 16 * g : 16 * g + 16, :] = jnp.where(last, v + top[:, at : at + 1], v)
    one = lane_ids(1) == 0
    for k in range(n):
        up = pack_ref[size + n * n + k : size + n * n + k + 1, :]
        pre = buf_ref[size + 24 + k : size + 25 + k, :]
        pre = jnp.where(one, 1.0, pltpu.roll(pre, 1, 1))
        for g in range(cols // 16):
            rows = slice(16 * g, 16 * g + 16)
            wide, at = slice(k * cols + 16 * g, k * cols + 16 * g + 16), 32 * g + k
            below = jnp.where(first, 0.0, pltpu.roll(buf_ref[wide, :], 1, 1)) + pre * mine[:, at : at + 1]
            v = pack_ref[wide, :] + up * below + coupled(pack_ref, h_ref, k, n, rows)
            for i, d in enumerate(STEPS):
                v = v + down_ref[i, k : k + 1, :] * pltpu.roll(v, LANES - d, 1)
            loc_ref[k, rows, :] = v
            a_ref[rows, k * LANES : (k + 1) * LANES] = v
    a_ref[cols : 2 * cols, :] = ext_ref[...]
    total = dot_nt(a_ref[0:cols, :], a_ref[...])
    lane = lane_ids(16)
    edges = jnp.zeros((16, LANES), F32)
    for g in range(cols // 16):
        moved = pltpu.roll(total[16 * g : 16 * g + 16, :], (32 * g + 64) % LANES, 1)
        edges = jnp.where(lane // 32 == g, moved, edges)
    half = cols // 2
    for peer in range(pay_ref.shape[0]):
        at = half * (peer % NCORE)
        low = pltpu.roll(total[at + 16 : at + 32, :], 64, 1)
        pay_ref[peer, 0:16, :] = jnp.where(lane < 64, total[at : at + 16, :], low)
        pay_ref[peer, 16:32, :] = edges
        pay_ref[peer, 32:40, :] = row_ref[...]


def line_body(r_ref, gram_ref, entry_ref, left_ref, right_ref):
    peers = r_ref.shape[0] // NCORE
    cols = left_ref.shape[0]
    mine, core = lax.axis_index("line"), lax.axis_index("core")
    lane = lane_ids(16)
    first = lane % 32 < 16
    zero = jnp.zeros((16, LANES), F32)
    entry = zero
    for station in range(NCORE):
        state = zero
        left = [zero] * (cols // 16)
        right = [zero] * (cols // 16)
        for at in range(peers - 2, -1, -1):
            above, here = NCORE * (at + 1) + station, NCORE * at + station
            state = r_ref[above, 34:35, :] * state + r_ref[above, 16:32, :]
            entry = jnp.where((mine == at) & (core == station), state, entry)
            back = pltpu.roll(state, LANES - 16, 1)
            cross = r_ref[here, 16:32, :] + (0.5 * r_ref[here, 35:36, :]) * back
            a = jnp.where(first, cross, state)
            b = jnp.where(first, back, pltpu.roll(cross, 16, 1))
            for g in range(cols // 16):
                shift = (32 * (at - g)) % LANES
                left[g] = jnp.where(lane // 32 == at, pltpu.roll(a, shift, 1), left[g])
                right[g] = jnp.where(lane // 32 == at, pltpu.roll(b, shift, 1), right[g])
        for g in range(cols // 16):
            rows = slice(16 * g, 16 * g + 16)
            left_ref[rows, station * LANES : (station + 1) * LANES] = left[g]
            right_ref[rows, station * LANES : (station + 1) * LANES] = right[g]
    half = cols // 2
    mine = left_ref[pl.ds(pl.multiple_of(half * core, half), half), :]
    fix = dot_nt(mine, right_ref[...])
    total = jnp.concatenate([fix[0:16, :], fix[16:32, :]], axis=1)
    for i in range(r_ref.shape[0]):
        total = total + r_ref[i, 0:16, :]
    for peer in range(gram_ref.shape[0]):
        gram_ref[peer] = total
    entry_ref[...] = entry


def sum_body(r_ref, o_ref):
    total = r_ref[0]
    for i in range(1, r_ref.shape[0]):
        total = total + r_ref[i]
    for peer in range(o_ref.shape[0]):
        o_ref[peer] = total


def inverse_factor(scale, gram, v_ref):
    cols = gram.shape[0]
    count = cols // 8
    lane, row = lane_ids(8), row_ids(8)
    tiles = []
    for t in range(count):
        unit = jnp.where(lane - 64 == row + 8 * t, 1.0, 0.0)
        tiles.append(jnp.where(lane < 64, gram[8 * t : 8 * t + 8, :], unit))
    for p in range(count):
        later = range(p + 1, count)
        r = [tiles[p][i : i + 1, :] for i in range(8)]
        s = {}
        for i in range(8):
            for j in range(i + 1):
                at = 8 * p + j
                s[i, j] = jnp.broadcast_to(r[i][:, at : at + 1], (1, LANES))
        c = []
        for i in range(8):
            at = 8 * p + i
            c.append([jnp.broadcast_to(tiles[t][:, at : at + 1], (8, LANES)) for t in later])
        scaled = []
        for i in range(8):
            inv = 1.0 / s[i, i]
            for t in range(i + 1, 8):
                f = s[t, i] * inv
                for u in range(i + 1, t + 1):
                    s[t, u] = s[t, u] - f * s[u, i]
                r[t] = r[t] - f * r[i]
                c[t] = [x - f * y for x, y in zip(c[t], c[i])]
            v_ref[8 * p + i : 8 * p + i + 1, :] = r[i] * (scale / jnp.sqrt(s[i, i]))
            scaled.append(r[i] * inv)
        for x, t in enumerate(later):
            for i in range(8):
                tiles[t] = tiles[t] - c[i][x] * scaled[i]
    return pltpu.roll(v_ref[...], 64, 1)[:, 0:64]


def basis_body(scale, r_ref, loc_ref, suf_ref, entry_ref, out_ref, f_ref, v_ref):
    n, cols, _ = loc_ref.shape
    for k in range(n):
        suf = suf_ref[k : k + 1, :]
        for g in range(cols // 16):
            rows, at = slice(16 * g, 16 * g + 16), 32 * g + 16 + k
            v = loc_ref[k, rows, :] + suf * entry_ref[:, at : at + 1]
            f_ref[rows, k * LANES : (k + 1) * LANES] = v
    parts = []
    for core in range(NCORE):
        packed = r_ref[core]
        for i in range(NCORE + core, r_ref.shape[0], NCORE):
            packed = packed + r_ref[i]
        parts += [packed, pltpu.roll(packed, 64, 1)]
    unpacked = jnp.concatenate(parts, axis=0)
    inv = inverse_factor(scale, unpacked, v_ref)
    out = jnp.dot(inv, f_ref[...], precision=HIGH, preferred_element_type=F32)
    for k in range(n):
        out_ref[k] = out[:, k * LANES : (k + 1) * LANES]


def in_hbm(value):
    return pltpu.with_memory_space_constraint(value, pltpu.HBM)


def exchange(value, axis):
    return lax.all_to_all(value, axis, 0, 0, tiled=True)


def local(forcing, block_inverse, wall_rates, span_couple):
    n, cols, _, pts = forcing.shape
    peers = lax.axis_size("line")
    stations = lax.axis_size("z") * lax.axis_size("y") * lax.axis_size("core")
    rows = n * stations * pts * peers
    field = (n, cols, pts)
    f, b, w, c = map(in_hbm, (forcing.reshape(field), block_inverse, wall_rates, span_couple))
    pairs = [(i, 1 if i % 2 else -1) for i in range(stations)]
    across = [(i, (i + d) % stations) for i, d in pairs]
    beyond = [(i, (i - 2 * d) % stations) for i, d in pairs]
    work = 2 * n * n * cols * pts
    size = n * cols
    scratch = pltpu.VMEM(field, F32)
    wide = pltpu.VMEM((cols, n * pts), F32)
    tall = pltpu.VMEM((2 * cols, n * pts), F32)

    inputs = [pltpu.VMEM(a.shape, F32) for a in (f, b, w)]
    start, pack = call(
        start_body,
        [(size, pts), (size + n * n + 2 * n, pts)],
        work,
        inputs + [pltpu.SMEM(c.shape, F32), pltpu.SemaphoreType.DMA((4,))],
        HBM,
    )(f, b, w, c)
    fpack = lax.ppermute(pack, TILE, across)
    near = lax.all_gather(start, "core")
    steps, rows16 = (len(STEPS), 16, pts), (16, pts)
    tables = [field, (cols, 32), steps, rows16, (8, pts)]
    held, tables_of, _ = lax.optimization_barrier((start, pack, near))
    beyond = lax.ppermute(held, TILE, beyond)
    base, edge, up, pre, row, down, suf, ext = call(
        side_body, tables + [steps, rows16, (64, n * pts)], work // 4, [wide]
    )(tables_of)
    buf = call(own_body, [(size + 40, pts)], 2 * work, [scratch, wide])(
        pack, base, fpack, near, up, edge, row, pre
    )[0]
    both = lax.all_gather(buf, "core")
    fbase, fedge, fup, fpre, frow = call(far_side_body, tables, work // 4, [wide])(fpack)
    floc, pay = call(far_body, [(size, pts), (peers, 72, pts)], 2 * work, [scratch, wide])(
        fpack, fbase, start, beyond, fup, fedge, frow, buf, both
    )
    got = exchange(pay, "line")
    loc, pay = call(down_body, [field, (peers * NCORE, 40, pts)], 4 * work, [scratch, tall])(
        pack, got, buf, both, floc, fpre, down, ext, row
    )
    side = pltpu.VMEM((cols, NCORE * pts), F32)
    part = (cols // 4, pts)
    gram, entry = call(line_body, [(NY,) + part, (16, pts)], work // 4, [side, side])(
        exchange(pay, ("line", "core"))
    )
    gram = call(sum_body, (NZ * NCORE,) + part)(exchange(gram, "y"))
    gram = exchange(gram, ("z", "core"))

    def basis(*refs):
        basis_body(math.sqrt(rows), *refs)

    out = call(basis, field, 4 * work, [wide, pltpu.VMEM((cols, pts), F32)])(
        gram, loc, suf, entry
    )
    return out.reshape(n, cols, 1, pts)


def solution(mesh):
    devices = mesh.devices.reshape(mesh.shape["line"], NZ, NY, NCORE)
    inner = Mesh(devices, ("line",) + TILE)
    spec = P(None, None, TILE, "line")
    return jax.shard_map(
        local, mesh=inner, in_specs=(spec, spec, spec, P()), out_specs=spec, check_vma=False
    )
```

```python
import math

import jax
import jax.numpy as jnp
from jax import lax
from jax.experimental import pallas as pl
from jax.experimental.pallas import tpu as pltpu
from jax.sharding import Mesh, PartitionSpec as P

NZ, NY, NCORE = 8, 8, 2
TILE = ("z", "y", "core")
HIGH = lax.Precision.HIGHEST
F32 = jnp.float32
LANES = 128
LIMIT = 16 << 20
STEPS = (1, 2, 4, 8, 16, 32, 64)
VMEM = pl.BlockSpec(memory_space=pltpu.VMEM)
HBM = pl.BlockSpec(memory_space=pltpu.HBM)


def lane_ids(rows):
    return lax.broadcasted_iota(jnp.int32, (rows, LANES), 1)


def row_ids(rows):
    return lax.broadcasted_iota(jnp.int32, (rows, LANES), 0)


def dot_nt(a, b):
    return lax.dot_general(
        a, b, (((1,), (1,)), ((), ())), precision=HIGH, preferred_element_type=F32
    )


def call(body, outs, flops=0, scratch=(), space=VMEM):
    many = isinstance(outs[0], tuple)
    shapes = [jax.ShapeDtypeStruct(s, F32) for s in (outs if many else [outs])]

    def run(*args):
        size = sum(a.size for a in args) + sum(math.prod(s.shape) for s in shapes)
        return pl.pallas_call(
            body,
            out_shape=shapes if many else shapes[0],
            in_specs=[space] * len(args),
            out_specs=[VMEM] * len(shapes) if many else VMEM,
            scratch_shapes=list(scratch),
            compiler_params=pltpu.CompilerParams(vmem_limit_bytes=LIMIT),
            cost_estimate=pl.CostEstimate(
                flops=flops, bytes_accessed=4 * size, transcendentals=0
            ),
        )(*args)

    return run


def apply_rows(block, n, take):
    total = block(0) * take(0)
    for m in range(1, n):
        total = total + block(m) * take(m)
    return total


def pick(values, mask):
    total = None
    for _ in range(3):
        piece = values.astype(jnp.bfloat16)
        values = values - piece.astype(F32)
        part = lax.dot_general(
            piece, mask, (((1,), (1,)), ((), ())), preferred_element_type=F32
        )
        total = part if total is None else total + part
    return total


def end_mask(n):
    wide = (32, n * LANES)
    col = lax.broadcasted_iota(jnp.int32, wide, 1)
    row = lax.broadcasted_iota(jnp.int32, wide, 0)
    return (col == jnp.where(row < 16, row * LANES + LANES - 1, (row - 16) * LANES)).astype(
        jnp.bfloat16
    )


def start_body(f_hbm, b_hbm, w_hbm, c_hbm, s_ref, pack_ref, f_ref, b_ref, w_ref, c_ref, sems):
    copies = [
        pltpu.make_async_copy(src, dst, sems.at[i])
        for i, (src, dst) in enumerate(
            ((f_hbm, f_ref), (b_hbm, b_ref), (w_hbm, w_ref), (c_hbm, c_ref))
        )
    ]
    for copy in copies:
        copy.start()
    for copy in copies:
        copy.wait()
    n, cols, _ = f_ref.shape
    for g in range(0, cols, 16):
        vals = [f_ref[m, g : g + 16, :] for m in range(n)]
        for k in range(n):
            v = apply_rows(lambda m: b_ref[k, m], n, lambda m: vals[m])
            s_ref[k * cols + g : k * cols + g + 16, :] = v
            pack_ref[k * cols + g : k * cols + g + 16, :] = v
    at = n * cols
    for k in range(n):
        for m in range(n):
            pack_ref[at + k * n + m : at + k * n + m + 1, :] = c_ref[m] * b_ref[k, m]
    at += n * n
    for i in range(2):
        for k in range(n):
            pack_ref[at + i * n + k : at + i * n + k + 1, :] = w_ref[i, k]


def rate_tables(up, down):
    n = up.shape[0]
    lane = lane_ids(n)
    pre, suf = up, down
    p = jnp.where(lane >= 1, up, 0.0)
    q = jnp.where(lane < LANES - 1, down, 0.0)
    ps, qs = [], []
    for d in STEPS:
        ps.append(p)
        qs.append(q)
        p = p * pltpu.roll(p, d, 1)
        q = q * pltpu.roll(q, LANES - d, 1)
        pre = jnp.where(lane >= d, pre * pltpu.roll(pre, d, 1), pre)
        suf = jnp.where(lane < LANES - d, suf * pltpu.roll(suf, LANES - d, 1), suf)
    norm = jnp.sum(suf * suf, axis=1, keepdims=True)
    table = jnp.zeros((8, LANES), F32)
    at, row = lane_ids(8), row_ids(8)
    for k in range(n):
        mine = jnp.where(row == 0, pre[k : k + 1, LANES - 1 : LANES], 0.0)
        mine = jnp.where(row == 1, down[k : k + 1, LANES - 1 : LANES], mine)
        mine = jnp.where(row == 2, suf[k : k + 1, 0:1], mine)
        mine = jnp.where(row == 3, norm[k : k + 1, 0:1], mine)
        table = jnp.where(lax.rem(at, 16) == k, mine, table)
    return ps, qs, pre, suf, table


def sweep_tables(n, cols, pack_ref, base_ref, up_ref, pre_ref, row_ref):
    at = n * cols + n * n
    up, down = pack_ref[at : at + n, :], pack_ref[at + n : at + 2 * n, :]
    ps, qs, pre, suf, table = rate_tables(up, down)
    for i, p in enumerate(ps):
        up_ref[i, 0:n, :] = p
    pre_ref[0:n, :] = pre
    row_ref[...] = table
    inner = lane_ids(cols) < LANES - 1
    for k in range(n):
        start = pack_ref[k * cols : (k + 1) * cols, :]
        above = jnp.where(inner, pltpu.roll(start, LANES - 1, 1), 0.0)
        base_ref[k] = start + down[k : k + 1, :] * above
    return qs, suf


def side_body(pack_ref, base_ref, up_ref, pre_ref, row_ref, down_ref, suf_ref, ext_ref):
    n, cols, _ = base_ref.shape
    qs, suf = sweep_tables(n, cols, pack_ref, base_ref, up_ref, pre_ref, row_ref)
    for i, q in enumerate(qs):
        down_ref[i, 0:n, :] = q
    suf_ref[0:n, :] = suf
    place = row_ids(32)
    first = (lane_ids(32) == 0).astype(F32)
    for k in range(n):
        block = jnp.where(place == k, jnp.broadcast_to(suf[k : k + 1, :], (32, LANES)), 0.0)
        block = jnp.where(place == 16 + k, first, block)
        ext_ref[:, k * LANES : (k + 1) * LANES] = block


def other_body(near_ref, out_ref):
    out_ref[...] = near_ref[1 - lax.axis_index("core")]


def coupled(pack_ref, h_ref, k, n, rows):
    at = n * h_ref.shape[1] + k * n
    return apply_rows(
        lambda m: pack_ref[at + m : at + m + 1, :], n, lambda m: h_ref[m, rows, :]
    )


def rise(pack_ref, base_ref, one, two, up_ref, loc_ref, h_ref, a_ref):
    n, cols, _ = base_ref.shape
    for m in range(n):
        rows = slice(m * cols, (m + 1) * cols)
        h_ref[m] = one(rows) + two(rows)
    first = lane_ids(16) == 0
    for k in range(n):
        for g in range(cols // 16):
            rows = slice(16 * g, 16 * g + 16)
            v = base_ref[k, rows, :] + coupled(pack_ref, h_ref, k, n, rows)
            for i, d in enumerate(STEPS):
                v = v + up_ref[i, k : k + 1, :] * pltpu.roll(v, d, 1)
            wide = slice(k * cols + 16 * g, k * cols + 16 * g + 16)
            loc_ref[wide, :] = v
            a_ref[rows, k * LANES : (k + 1) * LANES] = jnp.where(first, pack_ref[wide, :], v)
    ends = pick(a_ref[...], end_mask(n))
    ends = jnp.concatenate([ends, jnp.zeros((cols, LANES - 32), F32)], axis=1)
    pay = ends[0:16, :]
    for g in range(1, cols // 16):
        pay = pay + pltpu.roll(ends[16 * g : 16 * g + 16, :], 32 * g, 1)
    return pay


def own_body(
    pack_ref, base_ref, far_ref, near_ref, up_ref, row_ref, pre_ref,
    buf_ref, fbase_ref, fup_ref, fpre_ref, frow_ref, h_ref, a_ref,
):
    n, cols, _ = base_ref.shape
    size = n * cols
    other = 1 - lax.axis_index("core")
    sweep_tables(n, cols, far_ref, fbase_ref, fup_ref, fpre_ref, frow_ref)
    buf_ref[size : size + 16, :] = rise(
        pack_ref, base_ref, lambda rows: far_ref[rows, :], lambda rows: near_ref[other, rows, :],
        up_ref, buf_ref, h_ref, a_ref,
    )
    buf_ref[size + 16 : size + 24, :] = row_ref[...]
    buf_ref[size + 24 : size + 40, :] = pre_ref[...]


def far_body(
    pack_ref, base_ref, start_ref, next_ref, up_ref, row_ref, buf_ref, both_ref,
    loc_ref, pay_ref, h_ref, a_ref,
):
    size = base_ref.shape[0] * base_ref.shape[1]
    other = 1 - lax.axis_index("core")
    pay = rise(
        pack_ref, base_ref, lambda rows: start_ref[rows, :], lambda rows: next_ref[rows, :],
        up_ref, loc_ref, h_ref, a_ref,
    )
    own, near = buf_ref[size : size + 24, :], both_ref[other, size : size + 24, :]
    row = row_ids(8)
    table = jnp.where(row < 2, own[16:24, :], pltpu.roll(near[16:24, :], 2, 0))
    table = jnp.where(row < 4, table, pltpu.roll(row_ref[...], 4, 0))
    for peer in range(pay_ref.shape[0]):
        pay_ref[peer, 0:16, :] = own[0:16, :]
        pay_ref[peer, 16:32, :] = near[0:16, :]
        pay_ref[peer, 32:48, :] = pay
        pay_ref[peer, 48:56, :] = table


def entering(r_ref, station):
    mine = lax.axis_index("line")
    at0, row = 16 * station, 48 + 2 * station
    state = jnp.zeros((16, LANES), F32)
    entry = state
    top = state
    for at in range(r_ref.shape[0] - 1):
        lead = pltpu.roll(r_ref[at + 1, at0 : at0 + 16, :], LANES - 16, 1)
        tail = r_ref[at, row + 1 : row + 2, :] * lead
        top = jnp.where(mine == at, tail, top)
        state = r_ref[at, row : row + 1, :] * state + (r_ref[at, at0 : at0 + 16, :] + tail)
        entry = jnp.where(mine == at + 1, state, entry)
    return entry, top


def packed_blocks(gram):
    lane, row = lane_ids(32), row_ids(32)
    corner = pltpu.roll(gram[32:64, :], LANES - 32, 1)
    joined = jnp.where(lane >= row, gram[0:32, :], corner)
    extra = jnp.sum(jnp.where(lane == row, corner, 0.0), axis=0, keepdims=True)
    quarter = lane_ids(8) // 32
    blocks = []
    for part in (pltpu.roll(gram[0:32, :], LANES - 32, 1), joined):
        block = jnp.zeros((8, LANES), F32)
        for a in range(4):
            block = jnp.where(quarter == a, pltpu.roll(part[8 * a : 8 * a + 8, :], 32 * a, 1), block)
        blocks.append(block)
    return (blocks[0], jnp.zeros((1, LANES), F32)), (blocks[1], extra)


def unpacked(upper, joined, extra):
    def spread(block):
        return jnp.concatenate([pltpu.roll(block, (LANES - 32 * a) % LANES, 1) for a in range(4)], axis=0)

    lane, row = lane_ids(32), row_ids(32)
    upper, joined = spread(upper), spread(joined)
    turned = jnp.where(lane < 32, joined, pltpu.roll(upper, 32, 1)).T
    turned = jnp.concatenate([turned, jnp.zeros((LANES, LANES - 32), F32)], axis=1)
    first, second = turned[0:32, :], turned[32:64, :]
    low = jnp.where(lane >= row, joined, first)
    high = jnp.where(lane < row, joined, jnp.where(lane == row, extra, first))
    top = jnp.where(lane < 32, low, pltpu.roll(upper, 32, 1))
    bottom = jnp.where(lane < 32, second, pltpu.roll(high, 32, 1))
    return jnp.concatenate([top, bottom], axis=0)


def down_body(
    pack_ref, r_ref, buf_ref, both_ref, floc_ref, fpre_ref, down_ref, ext_ref, row_ref,
    loc_ref, pay_ref, h_ref, a_ref,
):
    n, cols, _ = loc_ref.shape
    size = n * cols
    other = 1 - lax.axis_index("core")
    mine, _ = entering(r_ref, 0)
    near, near_top = entering(r_ref, 1)
    far, far_top = entering(r_ref, 2)
    top = near_top + far_top
    lane = lane_ids(16)
    last, first = lane == LANES - 1, lane == 0
    for m in range(n):
        npre = both_ref[other, size + 24 + m : size + 25 + m, :]
        fpre = fpre_ref[m : m + 1, :]
        for g in range(cols // 16):
            rows, at = slice(m * cols + 16 * g, m * cols + 16 * g + 16), 32 * g + m
            v = both_ref[other, rows, :] + floc_ref[rows, :]
            v = v + npre * near[:, at : at + 1] + fpre * far[:, at : at + 1]
            h_ref[m, 16 * g : 16 * g + 16, :] = jnp.where(last, v + top[:, at : at + 1], v)
    one = lane_ids(1) == 0
    for k in range(n):
        up = pack_ref[size + n * n + k : size + n * n + k + 1, :]
        pre = buf_ref[size + 24 + k : size + 25 + k, :]
        pre = jnp.where(one, 1.0, pltpu.roll(pre, 1, 1))
        for g in range(cols // 16):
            rows = slice(16 * g, 16 * g + 16)
            wide, at = slice(k * cols + 16 * g, k * cols + 16 * g + 16), 32 * g + k
            below = jnp.where(first, 0.0, pltpu.roll(buf_ref[wide, :], 1, 1)) + pre * mine[:, at : at + 1]
            v = pack_ref[wide, :] + up * below + coupled(pack_ref, h_ref, k, n, rows)
            for i, d in enumerate(STEPS):
                v = v + down_ref[i, k : k + 1, :] * pltpu.roll(v, LANES - d, 1)
            loc_ref[k, rows, :] = v
            a_ref[rows, k * LANES : (k + 1) * LANES] = v
    a_ref[cols : cols + 32, :] = ext_ref[...]
    total = dot_nt(a_ref[0:cols, :], a_ref[...])
    total = jnp.concatenate([total, jnp.zeros((cols, 32), F32)], axis=1)
    lane = lane_ids(16)
    edges = jnp.zeros((16, LANES), F32)
    for g in range(cols // 16):
        moved = pltpu.roll(total[16 * g : 16 * g + 16, :], (32 * g + 64) % LANES, 1)
        edges = jnp.where(lane // 32 == g, moved, edges)
    blocks = packed_blocks(total)
    for peer in range(pay_ref.shape[0]):
        block, extra = blocks[peer % NCORE]
        pay_ref[peer, 0:8, :] = block
        pay_ref[peer, 8:24, :] = edges
        pay_ref[peer, 24:32, :] = jnp.where(row_ids(8) == 4, extra, row_ref[...])


def line_body(r_ref, gram_ref, entry_ref, left_ref, right_ref):
    peers = r_ref.shape[0] // NCORE
    cols = left_ref.shape[0]
    mine, core = lax.axis_index("line"), lax.axis_index("core")
    lane = lane_ids(16)
    first = lane % 32 < 16
    zero = jnp.zeros((16, LANES), F32)
    entry = zero
    for station in range(NCORE):
        state = zero
        left = [zero] * (cols // 16)
        right = [zero] * (cols // 16)
        for at in range(peers - 2, -1, -1):
            above, here = NCORE * (at + 1) + station, NCORE * at + station
            state = r_ref[above, 26:27, :] * state + r_ref[above, 8:24, :]
            entry = jnp.where((mine == at) & (core == station), state, entry)
            back = pltpu.roll(state, LANES - 16, 1)
            cross = r_ref[here, 8:24, :] + (0.5 * r_ref[here, 27:28, :]) * back
            a = jnp.where(first, cross, state)
            b = jnp.where(first, back, pltpu.roll(cross, 16, 1))
            for g in range(cols // 16):
                shift = (32 * (at - g)) % LANES
                left[g] = jnp.where(lane // 32 == at, pltpu.roll(a, shift, 1), left[g])
                right[g] = jnp.where(lane // 32 == at, pltpu.roll(b, shift, 1), right[g])
        for g in range(cols // 16):
            rows = slice(16 * g, 16 * g + 16)
            left_ref[rows, station * LANES : (station + 1) * LANES] = left[g]
            right_ref[rows, station * LANES : (station + 1) * LANES] = right[g]
    fix = dot_nt(left_ref[...], right_ref[...])
    fix = jnp.concatenate([fix, jnp.zeros((cols, LANES - cols), F32)], axis=1)
    (one, none), (two, extra) = packed_blocks(fix)
    total = jnp.where(core == 0, one, two)
    extra = jnp.where(core == 0, none, extra)
    for i in range(r_ref.shape[0]):
        total = total + r_ref[i, 0:8, :]
        extra = extra + r_ref[i, 28:29, :]
    spread_rows(gram_ref, [total[i : i + 1, :] for i in range(8)] + [extra])
    entry_ref[...] = entry


def spread_rows(out_ref, rows):
    for peer in range(out_ref.shape[0]):
        for i, row in enumerate(rows):
            out_ref[peer, i] = row


def summed_rows(r_ref, first, step):
    rows = []
    for i in range(r_ref.shape[1]):
        total = r_ref[first, i]
        for peer in range(first + step, r_ref.shape[0], step):
            total = total + r_ref[peer, i]
        rows.append(total)
    return rows


def sum_body(r_ref, o_ref):
    spread_rows(o_ref, summed_rows(r_ref, 0, 1))


def inverse_factor(scale, gram, v_ref):
    cols = gram.shape[0]
    count = cols // 8
    lane, row = lane_ids(8), row_ids(8)
    tiles = []
    for t in range(count):
        unit = jnp.where(lane - 64 == row + 8 * t, 1.0, 0.0)
        tiles.append(jnp.where(lane < 64, gram[8 * t : 8 * t + 8, :], unit))
    for p in range(count):
        later = range(p + 1, count)
        r = [tiles[p][i : i + 1, :] for i in range(8)]
        s = {}
        for i in range(8):
            for j in range(i + 1):
                at = 8 * p + j
                s[i, j] = jnp.broadcast_to(r[i][:, at : at + 1], (1, LANES))
        c = []
        for i in range(8):
            at = 8 * p + i
            c.append([jnp.broadcast_to(tiles[t][:, at : at + 1], (8, LANES)) for t in later])
        scaled = []
        for i in range(8):
            inv = 1.0 / s[i, i]
            for t in range(i + 1, 8):
                f = s[t, i] * inv
                for u in range(i + 1, t + 1):
                    s[t, u] = s[t, u] - f * s[u, i]
                r[t] = r[t] - f * r[i]
                c[t] = [x - f * y for x, y in zip(c[t], c[i])]
            v_ref[8 * p + i : 8 * p + i + 1, :] = r[i] * (scale / jnp.sqrt(s[i, i]))
            scaled.append(r[i] * inv)
        for x, t in enumerate(later):
            for i in range(8):
                tiles[t] = tiles[t] - c[i][x] * scaled[i]
    return pltpu.roll(v_ref[...], 64, 1)[:, 0:64]


def basis_body(scale, r_ref, loc_ref, suf_ref, entry_ref, out_ref, f_ref, v_ref):
    n, cols, _ = loc_ref.shape
    for k in range(n):
        suf = suf_ref[k : k + 1, :]
        for g in range(cols // 16):
            rows, at = slice(16 * g, 16 * g + 16), 32 * g + 16 + k
            v = loc_ref[k, rows, :] + suf * entry_ref[:, at : at + 1]
            f_ref[rows, k * LANES : (k + 1) * LANES] = v
    upper, joined = (summed_rows(r_ref, core, NCORE) for core in range(NCORE))
    gram = unpacked(jnp.concatenate(upper[:8], axis=0), jnp.concatenate(joined[:8], axis=0), joined[8])
    inv = inverse_factor(scale, gram, v_ref)
    out = jnp.dot(inv, f_ref[...], precision=HIGH, preferred_element_type=F32)
    for k in range(n):
        out_ref[k] = out[:, k * LANES : (k + 1) * LANES]


def in_hbm(value):
    return pltpu.with_memory_space_constraint(value, pltpu.HBM)


def exchange(value, axis):
    return lax.all_to_all(value, axis, 0, 0, tiled=True)


def local(forcing, block_inverse, wall_rates, span_couple):
    n, cols, _, pts = forcing.shape
    peers = lax.axis_size("line")
    stations = lax.axis_size("z") * lax.axis_size("y") * lax.axis_size("core")
    rows = n * stations * pts * peers
    field = (n, cols, pts)
    f, b, w, c = map(in_hbm, (forcing.reshape(field), block_inverse, wall_rates, span_couple))
    pairs = [(i, 1 if i % 2 else -1) for i in range(stations)]
    across = [(i, (i + d) % stations) for i, d in pairs]
    work = 2 * n * n * cols * pts
    size = n * cols
    scratch = pltpu.VMEM(field, F32)
    wide = pltpu.VMEM((cols, n * pts), F32)
    tall = pltpu.VMEM((cols + 32, n * pts), F32)

    inputs = [pltpu.VMEM(a.shape, F32) for a in (f, b, w)]
    start, pack = call(
        start_body,
        [(size, pts), (size + n * n + 2 * n, pts)],
        work,
        inputs + [pltpu.SMEM(c.shape, F32), pltpu.SemaphoreType.DMA((4,))],
        HBM,
    )(f, b, w, c)
    fpack = lax.ppermute(pack, TILE, across)
    near = lax.all_gather(start, "core")
    steps, rows16 = (len(STEPS), 16, pts), (16, pts)
    tables = [field, steps, rows16, (8, pts)]
    beyond = lax.ppermute(call(other_body, (size, pts))(near), TILE, across)
    tables_of, near = lax.optimization_barrier((pack, near))
    base, up, pre, row, down, suf, ext = call(
        side_body, tables + [steps, rows16, (32, n * pts)], work // 4
    )(tables_of)
    buf, fbase, fup, fpre, frow = call(
        own_body, [(size + 40, pts)] + tables, 2 * work, [scratch, wide]
    )(pack, base, fpack, near, up, row, pre)
    both = lax.all_gather(buf, "core")
    floc, pay = call(far_body, [(size, pts), (peers, 56, pts)], 2 * work, [scratch, wide])(
        fpack, fbase, start, beyond, fup, frow, buf, both
    )
    got = exchange(pay, "line")
    loc, pay = call(down_body, [field, (peers * NCORE, 32, pts)], 4 * work, [scratch, tall])(
        pack, got, buf, both, floc, fpre, down, ext, row
    )
    side = pltpu.VMEM((cols, NCORE * pts), F32)
    part = (9, 1, pts)
    gram, entry = call(line_body, [(NY,) + part, (16, pts)], work // 4, [side, side])(
        exchange(pay, ("line", "core"))
    )
    gram = call(sum_body, (NZ * NCORE,) + part)(exchange(gram, "y"))
    gram = exchange(gram, ("z", "core"))

    def basis(*refs):
        basis_body(math.sqrt(rows), *refs)

    out = call(basis, field, 4 * work, [wide, pltpu.VMEM((cols, pts), F32)])(
        gram, loc, suf, entry
    )
    return out.reshape(n, cols, 1, pts)


def solution(mesh):
    devices = mesh.devices.reshape(mesh.shape["line"], NZ, NY, NCORE)
    inner = Mesh(devices, ("line",) + TILE)
    spec = P(None, None, TILE, "line")
    return jax.shard_map(
        local, mesh=inner, in_specs=(spec, spec, spec, P()), out_specs=spec, check_vma=False
    )
```

```python
import math

import jax
import jax.numpy as jnp
from jax import lax
from jax.experimental import pallas as pl
from jax.experimental.pallas import tpu as pltpu
from jax.sharding import Mesh, PartitionSpec as P

NZ, NY, NCORE = 8, 8, 2
TILE = ("z", "y", "core")
HIGH = lax.Precision.HIGHEST
F32 = jnp.float32
LANES = 128
LIMIT = 16 << 20
STEPS = (1, 2, 4, 8, 16, 32, 64)
VMEM = pl.BlockSpec(memory_space=pltpu.VMEM)
HBM = pl.BlockSpec(memory_space=pltpu.HBM)


def lane_ids(rows):
    return lax.broadcasted_iota(jnp.int32, (rows, LANES), 1)


def row_ids(rows):
    return lax.broadcasted_iota(jnp.int32, (rows, LANES), 0)


def dot_nt(a, b):
    return lax.dot_general(
        a, b, (((1,), (1,)), ((), ())), precision=HIGH, preferred_element_type=F32
    )


def call(body, outs, flops=0, scratch=(), space=VMEM):
    many = isinstance(outs[0], tuple)
    shapes = [jax.ShapeDtypeStruct(s, F32) for s in (outs if many else [outs])]

    def run(*args):
        size = sum(a.size for a in args) + sum(math.prod(s.shape) for s in shapes)
        return pl.pallas_call(
            body,
            out_shape=shapes if many else shapes[0],
            in_specs=[space] * len(args),
            out_specs=[VMEM] * len(shapes) if many else VMEM,
            scratch_shapes=list(scratch),
            compiler_params=pltpu.CompilerParams(vmem_limit_bytes=LIMIT),
            cost_estimate=pl.CostEstimate(
                flops=flops, bytes_accessed=4 * size, transcendentals=0
            ),
        )(*args)

    return run


def apply_rows(block, n, take):
    total = block(0) * take(0)
    for m in range(1, n):
        total = total + block(m) * take(m)
    return total


def pick(values, mask):
    total = None
    for _ in range(3):
        piece = values.astype(jnp.bfloat16)
        values = values - piece.astype(F32)
        part = lax.dot_general(
            piece, mask, (((1,), (1,)), ((), ())), preferred_element_type=F32
        )
        total = part if total is None else total + part
    return total


def end_mask(n):
    wide = (32, n * LANES)
    col = lax.broadcasted_iota(jnp.int32, wide, 1)
    row = lax.broadcasted_iota(jnp.int32, wide, 0)
    return (col == jnp.where(row < 16, row * LANES + LANES - 1, (row - 16) * LANES)).astype(
        jnp.bfloat16
    )


def rate_tables(up, down):
    n = up.shape[0]
    lane = lane_ids(n)
    pre, suf = up, down
    p = jnp.where(lane >= 1, up, 0.0)
    q = jnp.where(lane < LANES - 1, down, 0.0)
    ps, qs = [], []
    for d in STEPS:
        ps.append(p)
        qs.append(q)
        p = p * pltpu.roll(p, d, 1)
        q = q * pltpu.roll(q, LANES - d, 1)
        pre = jnp.where(lane >= d, pre * pltpu.roll(pre, d, 1), pre)
        suf = jnp.where(lane < LANES - d, suf * pltpu.roll(suf, LANES - d, 1), suf)
    norm = jnp.sum(suf * suf, axis=1, keepdims=True)
    table = jnp.zeros((8, LANES), F32)
    at, row = lane_ids(8), row_ids(8)
    for k in range(n):
        mine = jnp.where(row == 0, pre[k : k + 1, LANES - 1 : LANES], 0.0)
        mine = jnp.where(row == 1, down[k : k + 1, LANES - 1 : LANES], mine)
        mine = jnp.where(row == 2, suf[k : k + 1, 0:1], mine)
        mine = jnp.where(row == 3, norm[k : k + 1, 0:1], mine)
        table = jnp.where(lax.rem(at, 16) == k, mine, table)
    return ps, qs, pre, suf, table


def start_body(
    f_hbm, b_hbm, w_hbm, c_hbm, s_ref, pack_ref, f_ref, b_ref, w_ref, c_ref, sems
):
    n, cols, _ = f_ref.shape
    few = [(w_hbm, w_ref), (c_hbm, c_ref), (b_hbm, b_ref)]
    few += [(f_hbm.at[:, g : g + 16, :], f_ref.at[:, g : g + 16, :]) for g in range(0, cols, 16)]
    copies = [pltpu.make_async_copy(src, dst, sems.at[i]) for i, (src, dst) in enumerate(few)]
    for copy in copies:
        copy.start()
    size = n * cols
    at = size + n * n
    for copy in copies[:3]:
        copy.wait()
    for k in range(n):
        for m in range(n):
            pack_ref[size + k * n + m : size + k * n + m + 1, :] = c_ref[m] * b_ref[k, m]
    for i in range(2):
        for k in range(n):
            pack_ref[at + i * n + k : at + i * n + k + 1, :] = w_ref[i, k]
    for i, g in enumerate(range(0, cols, 16)):
        copies[3 + i].wait()
        vals = [f_ref[m, g : g + 16, :] for m in range(n)]
        for k in range(n):
            v = apply_rows(lambda m: b_ref[k, m], n, lambda m: vals[m])
            s_ref[k * cols + g : k * cols + g + 16, :] = v
            pack_ref[k * cols + g : k * cols + g + 16, :] = v


def side_body(pack_ref, up_ref, down_ref, suf_ref, tab_ref, ext_ref):
    n = ext_ref.shape[1] // LANES
    at = pack_ref.shape[0] - 2 * n
    ps, qs, pre, suf, table = rate_tables(pack_ref[at : at + n, :], pack_ref[at + n : at + 2 * n, :])
    tab_ref[0:8, :] = table
    tab_ref[8 : 8 + n, :] = pre
    for i, (p, q) in enumerate(zip(ps, qs)):
        up_ref[i, 0:n, :] = p
        down_ref[i, 0:n, :] = q
    suf_ref[0:n, :] = suf
    place = row_ids(32)
    first = (lane_ids(32) == 0).astype(F32)
    for k in range(n):
        block = jnp.where(place == k, jnp.broadcast_to(suf[k : k + 1, :], (32, LANES)), 0.0)
        ext_ref[:, k * LANES : (k + 1) * LANES] = jnp.where(place == 16 + k, first, block)


def other_body(near_ref, out_ref):
    out_ref[...] = near_ref[1 - lax.axis_index("core")]


def coupled(pack_ref, h_ref, k, n, rows):
    at = n * h_ref.shape[1] + k * n
    return apply_rows(
        lambda m: pack_ref[at + m : at + m + 1, :], n, lambda m: h_ref[m, rows, :]
    )


def rise(pack_ref, one, two, up_ref, loc_ref, h_ref, a_ref, between=lambda k: None):
    n, cols, _ = h_ref.shape
    for m in range(n):
        rows = slice(m * cols, (m + 1) * cols)
        h_ref[m] = one(rows) + two(rows)
    lane = lane_ids(16)
    first, inner = lane == 0, lane < LANES - 1
    for k in range(n):
        at = n * cols + n * n + n + k
        fall = pack_ref[at : at + 1, :]
        between(k)
        for g in range(cols // 16):
            rows = slice(16 * g, 16 * g + 16)
            wide = slice(k * cols + 16 * g, k * cols + 16 * g + 16)
            start = pack_ref[wide, :]
            above = jnp.where(inner, pltpu.roll(start, LANES - 1, 1), 0.0)
            v = start + fall * above + coupled(pack_ref, h_ref, k, n, rows)
            for i, d in enumerate(STEPS):
                v = v + up_ref[i, k : k + 1, :] * pltpu.roll(v, d, 1)
            loc_ref[wide, :] = v
            a_ref[rows, k * LANES : (k + 1) * LANES] = jnp.where(first, start, v)
    ends = pick(a_ref[...], end_mask(n))
    ends = jnp.concatenate([ends, jnp.zeros((cols, LANES - 32), F32)], axis=1)
    pay = ends[0:16, :]
    for g in range(1, cols // 16):
        pay = pay + pltpu.roll(ends[16 * g : 16 * g + 16, :], 32 * g, 1)
    return pay


def own_body(pack_ref, far_ref, near_ref, up_ref, tab_ref, buf_ref, fup_ref, ftab_ref, h_ref, a_ref):
    n, cols, _ = h_ref.shape
    size = n * cols
    at = size + n * n
    other = 1 - lax.axis_index("core")
    up, down = far_ref[at : at + n, :], far_ref[at + n : at + 2 * n, :]
    lane = lane_ids(n)
    state = [jnp.where(lane >= 1, up, 0.0), up]

    def far_table(k):
        if k < len(STEPS):
            d = STEPS[k]
            p, pre = state
            fup_ref[k, 0:n, :] = p
            state[0] = p * pltpu.roll(p, d, 1)
            state[1] = jnp.where(lane >= d, pre * pltpu.roll(pre, d, 1), pre)

    buf_ref[size : size + 16, :] = rise(
        pack_ref, lambda rows: far_ref[rows, :], lambda rows: near_ref[other, rows, :],
        up_ref, buf_ref, h_ref, a_ref, far_table,
    )
    buf_ref[size + 16 : size + 40, :] = tab_ref[...]
    pre = state[1]
    ftab_ref[8 : 8 + n, :] = pre
    table = jnp.zeros((8, LANES), F32)
    at, row = lane_ids(8), row_ids(8)
    for k in range(n):
        mine = jnp.where(row == 0, pre[k : k + 1, LANES - 1 : LANES], down[k : k + 1, LANES - 1 : LANES])
        table = jnp.where(lax.rem(at, 16) == k, mine, table)
    ftab_ref[0:8, :] = table


def far_body(
    pack_ref, start_ref, next_ref, up_ref, tab_ref, buf_ref, both_ref, loc_ref, pay_ref, h_ref, a_ref
):
    n, cols, _ = h_ref.shape
    size = n * cols
    other = 1 - lax.axis_index("core")
    pay = rise(
        pack_ref, lambda rows: start_ref[rows, :], lambda rows: next_ref[rows, :],
        up_ref, loc_ref, h_ref, a_ref,
    )
    own, near = buf_ref[size : size + 24, :], both_ref[other, size : size + 24, :]
    row = row_ids(8)
    table = jnp.where(row < 2, own[16:24, :], pltpu.roll(near[16:24, :], 2, 0))
    table = jnp.where(row < 4, table, pltpu.roll(tab_ref[0:8, :], 4, 0))
    for peer in range(pay_ref.shape[0]):
        pay_ref[peer, 0:16, :] = own[0:16, :]
        pay_ref[peer, 16:32, :] = near[0:16, :]
        pay_ref[peer, 32:48, :] = pay
        pay_ref[peer, 48:56, :] = table


def entering(r_ref, station):
    mine = lax.axis_index("line")
    at0, row = 16 * station, 48 + 2 * station
    state = jnp.zeros((16, LANES), F32)
    entry = state
    top = state
    for at in range(r_ref.shape[0] - 1):
        lead = pltpu.roll(r_ref[at + 1, at0 : at0 + 16, :], LANES - 16, 1)
        tail = r_ref[at, row + 1 : row + 2, :] * lead
        top = jnp.where(mine == at, tail, top)
        state = r_ref[at, row : row + 1, :] * state + (r_ref[at, at0 : at0 + 16, :] + tail)
        entry = jnp.where(mine == at + 1, state, entry)
    return entry, top


def packed_blocks(gram):
    lane, row = lane_ids(32), row_ids(32)
    corner = pltpu.roll(gram[32:64, :], LANES - 32, 1)
    joined = jnp.where(lane >= row, gram[0:32, :], corner)
    extra = jnp.sum(jnp.where(lane == row, corner, 0.0), axis=0, keepdims=True)
    quarter = lane_ids(8) // 32
    blocks = []
    for part in (pltpu.roll(gram[0:32, :], LANES - 32, 1), joined):
        block = jnp.zeros((8, LANES), F32)
        for a in range(4):
            block = jnp.where(quarter == a, pltpu.roll(part[8 * a : 8 * a + 8, :], 32 * a, 1), block)
        blocks.append(block)
    return (blocks[0], jnp.zeros((1, LANES), F32)), (blocks[1], extra)


def unpacked(upper, joined, extra):
    def spread(block):
        return jnp.concatenate([pltpu.roll(block, (LANES - 32 * a) % LANES, 1) for a in range(4)], axis=0)

    lane, row = lane_ids(32), row_ids(32)
    upper, joined = spread(upper), spread(joined)
    turned = jnp.where(lane < 32, joined, pltpu.roll(upper, 32, 1)).T
    turned = jnp.concatenate([turned, jnp.zeros((LANES, LANES - 32), F32)], axis=1)
    first, second = turned[0:32, :], turned[32:64, :]
    low = jnp.where(lane >= row, joined, first)
    high = jnp.where(lane < row, joined, jnp.where(lane == row, extra, first))
    top = jnp.where(lane < 32, low, pltpu.roll(upper, 32, 1))
    bottom = jnp.where(lane < 32, second, pltpu.roll(high, 32, 1))
    return jnp.concatenate([top, bottom], axis=0)


def down_body(
    pack_ref, r_ref, buf_ref, both_ref, floc_ref, ftab_ref, down_ref, ext_ref,
    loc_ref, pay_ref, h_ref, a_ref,
):
    n, cols, _ = loc_ref.shape
    size = n * cols
    other = 1 - lax.axis_index("core")
    mine, _ = entering(r_ref, 0)
    near, near_top = entering(r_ref, 1)
    far, far_top = entering(r_ref, 2)
    top = near_top + far_top
    lane = lane_ids(16)
    last, first = lane == LANES - 1, lane == 0
    for m in range(n):
        npre = both_ref[other, size + 24 + m : size + 25 + m, :]
        fpre = ftab_ref[8 + m : 9 + m, :]
        for g in range(cols // 16):
            rows, at = slice(m * cols + 16 * g, m * cols + 16 * g + 16), 32 * g + m
            v = both_ref[other, rows, :] + floc_ref[rows, :]
            v = v + npre * near[:, at : at + 1] + fpre * far[:, at : at + 1]
            h_ref[m, 16 * g : 16 * g + 16, :] = jnp.where(last, v + top[:, at : at + 1], v)
    one = lane_ids(1) == 0
    for k in range(n):
        up = pack_ref[size + n * n + k : size + n * n + k + 1, :]
        pre = buf_ref[size + 24 + k : size + 25 + k, :]
        pre = jnp.where(one, 1.0, pltpu.roll(pre, 1, 1))
        for g in range(cols // 16):
            rows = slice(16 * g, 16 * g + 16)
            wide, at = slice(k * cols + 16 * g, k * cols + 16 * g + 16), 32 * g + k
            below = jnp.where(first, 0.0, pltpu.roll(buf_ref[wide, :], 1, 1)) + pre * mine[:, at : at + 1]
            v = pack_ref[wide, :] + up * below + coupled(pack_ref, h_ref, k, n, rows)
            for i, d in enumerate(STEPS):
                v = v + down_ref[i, k : k + 1, :] * pltpu.roll(v, LANES - d, 1)
            loc_ref[k, rows, :] = v
            a_ref[rows, k * LANES : (k + 1) * LANES] = v
    a_ref[cols : cols + 32, :] = ext_ref[...]
    total = dot_nt(a_ref[0:cols, :], a_ref[...])
    total = jnp.concatenate([total, jnp.zeros((cols, 32), F32)], axis=1)
    lane = lane_ids(16)
    edges = jnp.zeros((16, LANES), F32)
    for g in range(cols // 16):
        moved = pltpu.roll(total[16 * g : 16 * g + 16, :], (32 * g + 64) % LANES, 1)
        edges = jnp.where(lane // 32 == g, moved, edges)
    blocks = packed_blocks(total)
    for peer in range(pay_ref.shape[0]):
        block, extra = blocks[peer % NCORE]
        pay_ref[peer, 0:8, :] = block
        pay_ref[peer, 8:24, :] = edges
        pay_ref[peer, 24:32, :] = jnp.where(row_ids(8) == 4, extra, buf_ref[size + 16 : size + 24, :])


def line_body(r_ref, gram_ref, entry_ref, left_ref, right_ref):
    peers = r_ref.shape[0] // NCORE
    cols = left_ref.shape[0]
    mine, core = lax.axis_index("line"), lax.axis_index("core")
    lane = lane_ids(16)
    first = lane % 32 < 16
    zero = jnp.zeros((16, LANES), F32)
    entry = zero
    for station in range(NCORE):
        state = zero
        left = [zero] * (cols // 16)
        right = [zero] * (cols // 16)
        for at in range(peers - 2, -1, -1):
            above, here = NCORE * (at + 1) + station, NCORE * at + station
            state = r_ref[above, 26:27, :] * state + r_ref[above, 8:24, :]
            entry = jnp.where((mine == at) & (core == station), state, entry)
            back = pltpu.roll(state, LANES - 16, 1)
            cross = r_ref[here, 8:24, :] + (0.5 * r_ref[here, 27:28, :]) * back
            a = jnp.where(first, cross, state)
            b = jnp.where(first, back, pltpu.roll(cross, 16, 1))
            for g in range(cols // 16):
                shift = (32 * (at - g)) % LANES
                left[g] = jnp.where(lane // 32 == at, pltpu.roll(a, shift, 1), left[g])
                right[g] = jnp.where(lane // 32 == at, pltpu.roll(b, shift, 1), right[g])
        for g in range(cols // 16):
            rows = slice(16 * g, 16 * g + 16)
            left_ref[rows, station * LANES : (station + 1) * LANES] = left[g]
            right_ref[rows, station * LANES : (station + 1) * LANES] = right[g]
    fix = dot_nt(left_ref[...], right_ref[...])
    fix = jnp.concatenate([fix, jnp.zeros((cols, LANES - cols), F32)], axis=1)
    (one, none), (two, extra) = packed_blocks(fix)
    total = jnp.where(core == 0, one, two)
    extra = jnp.where(core == 0, none, extra)
    for i in range(r_ref.shape[0]):
        total = total + r_ref[i, 0:8, :]
        extra = extra + r_ref[i, 28:29, :]
    spread_rows(gram_ref, [total[i : i + 1, :] for i in range(8)] + [extra])
    entry_ref[...] = entry


def spread_rows(out_ref, rows):
    for peer in range(out_ref.shape[0]):
        for i, row in enumerate(rows):
            out_ref[peer, i] = row


def summed_rows(r_ref, first, step):
    rows = []
    for i in range(r_ref.shape[1]):
        total = r_ref[first, i]
        for peer in range(first + step, r_ref.shape[0], step):
            total = total + r_ref[peer, i]
        rows.append(total)
    return rows


def sum_body(r_ref, o_ref):
    spread_rows(o_ref, summed_rows(r_ref, 0, 1))


def inverse_factor(scale, gram, v_ref):
    cols = gram.shape[0]
    count = cols // 8
    lane, row = lane_ids(8), row_ids(8)
    tiles = []
    for t in range(count):
        unit = jnp.where(lane - 64 == row + 8 * t, 1.0, 0.0)
        tiles.append(jnp.where(lane < 64, gram[8 * t : 8 * t + 8, :], unit))
    for p in range(count):
        later = range(p + 1, count)
        r = [tiles[p][i : i + 1, :] for i in range(8)]
        s = {}
        for i in range(8):
            for j in range(i + 1):
                at = 8 * p + j
                s[i, j] = jnp.broadcast_to(r[i][:, at : at + 1], (1, LANES))
        c = []
        for i in range(8):
            at = 8 * p + i
            c.append([jnp.broadcast_to(tiles[t][:, at : at + 1], (8, LANES)) for t in later])
        scaled = []
        for i in range(8):
            inv = 1.0 / s[i, i]
            for t in range(i + 1, 8):
                f = s[t, i] * inv
                for u in range(i + 1, t + 1):
                    s[t, u] = s[t, u] - f * s[u, i]
                r[t] = r[t] - f * r[i]
                c[t] = [x - f * y for x, y in zip(c[t], c[i])]
            v_ref[8 * p + i : 8 * p + i + 1, :] = r[i] * (scale / jnp.sqrt(s[i, i]))
            scaled.append(r[i] * inv)
        for x, t in enumerate(later):
            for i in range(8):
                tiles[t] = tiles[t] - c[i][x] * scaled[i]
    return pltpu.roll(v_ref[...], 64, 1)[:, 0:64]


def basis_body(scale, r_ref, loc_ref, suf_ref, entry_ref, out_ref, f_ref, v_ref):
    n, cols, _ = loc_ref.shape
    for k in range(n):
        suf = suf_ref[k : k + 1, :]
        for g in range(cols // 16):
            rows, at = slice(16 * g, 16 * g + 16), 32 * g + 16 + k
            v = loc_ref[k, rows, :] + suf * entry_ref[:, at : at + 1]
            f_ref[rows, k * LANES : (k + 1) * LANES] = v
    upper, joined = (summed_rows(r_ref, core, NCORE) for core in range(NCORE))
    gram = unpacked(jnp.concatenate(upper[:8], axis=0), jnp.concatenate(joined[:8], axis=0), joined[8])
    inv = inverse_factor(scale, gram, v_ref)
    out = jnp.dot(inv, f_ref[...], precision=HIGH, preferred_element_type=F32)
    for k in range(n):
        out_ref[k] = out[:, k * LANES : (k + 1) * LANES]


def in_hbm(value):
    return pltpu.with_memory_space_constraint(value, pltpu.HBM)


def exchange(value, axis):
    return lax.all_to_all(value, axis, 0, 0, tiled=True)


def local(forcing, block_inverse, wall_rates, span_couple):
    n, cols, _, pts = forcing.shape
    peers = lax.axis_size("line")
    stations = lax.axis_size("z") * lax.axis_size("y") * lax.axis_size("core")
    rows = n * stations * pts * peers
    field = (n, cols, pts)
    f, b, w, c = map(in_hbm, (forcing.reshape(field), block_inverse, wall_rates, span_couple))
    pairs = [(i, 1 if i % 2 else -1) for i in range(stations)]
    across = [(i, (i + d) % stations) for i, d in pairs]
    work = 2 * n * n * cols * pts
    size = n * cols
    scratch = pltpu.VMEM(field, F32)
    wide = pltpu.VMEM((cols, n * pts), F32)
    tall = pltpu.VMEM((cols + 32, n * pts), F32)

    inputs = [pltpu.VMEM(a.shape, F32) for a in (f, b, w)] + [pltpu.SMEM(c.shape, F32)]
    steps = (len(STEPS), 16, pts)
    start, pack = call(
        start_body,
        [(size, pts), (size + n * n + 2 * n, pts)],
        work,
        inputs + [pltpu.SemaphoreType.DMA((3 + cols // 16,))],
        HBM,
    )(f, b, w, c)
    fpack = lax.ppermute(pack, TILE, across)
    near = lax.all_gather(start, "core")
    tables_of, near = lax.optimization_barrier((pack, near))
    beyond = lax.ppermute(call(other_body, (size, pts))(near), TILE, across)
    up, down, suf, tab, ext = call(
        side_body, [steps, steps, (16, pts), (24, pts), (32, n * pts)], work // 4
    )(tables_of)
    buf, fup, ftab = call(own_body, [(size + 40, pts), steps, (24, pts)], 2 * work, [scratch, wide])(
        pack, fpack, near, up, tab
    )
    both = lax.all_gather(buf, "core")
    floc, pay = call(far_body, [(size, pts), (peers, 56, pts)], 2 * work, [scratch, wide])(
        fpack, start, beyond, fup, ftab, buf, both
    )
    got = exchange(pay, "line")
    loc, pay = call(down_body, [field, (peers * NCORE, 32, pts)], 4 * work, [scratch, tall])(
        pack, got, buf, both, floc, ftab, down, ext
    )
    side = pltpu.VMEM((cols, NCORE * pts), F32)
    part = (9, 1, pts)
    gram, entry = call(line_body, [(NY,) + part, (16, pts)], work // 4, [side, side])(
        exchange(pay, ("line", "core"))
    )
    gram = call(sum_body, (NZ * NCORE,) + part)(exchange(gram, "y"))
    gram = exchange(gram, ("z", "core"))

    def basis(*refs):
        basis_body(math.sqrt(rows), *refs)

    out = call(basis, field, 4 * work, [wide, pltpu.VMEM((cols, pts), F32)])(
        gram, loc, suf, entry
    )
    return out.reshape(n, cols, 1, pts)


def solution(mesh):
    devices = mesh.devices.reshape(mesh.shape["line"], NZ, NY, NCORE)
    inner = Mesh(devices, ("line",) + TILE)
    spec = P(None, None, TILE, "line")
    return jax.shard_map(
        local, mesh=inner, in_specs=(spec, spec, spec, P()), out_specs=spec, check_vma=False
    )
```

```python
import math

import jax
import jax.numpy as jnp
from jax import lax
from jax.experimental import pallas as pl
from jax.experimental.pallas import tpu as pltpu
from jax.sharding import Mesh, PartitionSpec as P

NZ, NY, NCORE = 8, 8, 2
TILE = ("z", "y", "core")
HIGH = lax.Precision.HIGHEST
F32 = jnp.float32
LANES = 128
LIMIT = 16 << 20
STEPS = (1, 2, 4, 8, 16, 32, 64)
VMEM = pl.BlockSpec(memory_space=pltpu.VMEM)
HBM = pl.BlockSpec(memory_space=pltpu.HBM)


def lane_ids(rows):
    return lax.broadcasted_iota(jnp.int32, (rows, LANES), 1)


def row_ids(rows):
    return lax.broadcasted_iota(jnp.int32, (rows, LANES), 0)


def dot_nt(a, b):
    return lax.dot_general(
        a, b, (((1,), (1,)), ((), ())), precision=HIGH, preferred_element_type=F32
    )


def call(body, outs, flops=0, scratch=(), space=VMEM):
    many = isinstance(outs[0], tuple)
    shapes = [jax.ShapeDtypeStruct(s, F32) for s in (outs if many else [outs])]

    def run(*args):
        size = sum(a.size for a in args) + sum(math.prod(s.shape) for s in shapes)
        return pl.pallas_call(
            body,
            out_shape=shapes if many else shapes[0],
            in_specs=[space] * len(args),
            out_specs=[VMEM] * len(shapes) if many else VMEM,
            scratch_shapes=list(scratch),
            compiler_params=pltpu.CompilerParams(vmem_limit_bytes=LIMIT),
            cost_estimate=pl.CostEstimate(
                flops=flops, bytes_accessed=4 * size, transcendentals=0
            ),
        )(*args)

    return run


def apply_rows(block, n, take):
    total = block(0) * take(0)
    for m in range(1, n):
        total = total + block(m) * take(m)
    return total


def pick(values, mask):
    total = None
    for _ in range(3):
        piece = values.astype(jnp.bfloat16)
        values = values - piece.astype(F32)
        part = lax.dot_general(
            piece, mask, (((1,), (1,)), ((), ())), preferred_element_type=F32
        )
        total = part if total is None else total + part
    return total


def end_mask(n):
    wide = (32, n * LANES)
    col = lax.broadcasted_iota(jnp.int32, wide, 1)
    row = lax.broadcasted_iota(jnp.int32, wide, 0)
    return (col == jnp.where(row < 16, row * LANES + LANES - 1, (row - 16) * LANES)).astype(
        jnp.bfloat16
    )


def rate_tables(up, down):
    n = up.shape[0]
    lane = lane_ids(n)
    pre, suf = up, down
    p = jnp.where(lane >= 1, up, 0.0)
    q = jnp.where(lane < LANES - 1, down, 0.0)
    ps, qs = [], []
    for d in STEPS:
        ps.append(p)
        qs.append(q)
        p = p * pltpu.roll(p, d, 1)
        q = q * pltpu.roll(q, LANES - d, 1)
        pre = jnp.where(lane >= d, pre * pltpu.roll(pre, d, 1), pre)
        suf = jnp.where(lane < LANES - d, suf * pltpu.roll(suf, LANES - d, 1), suf)
    norm = jnp.sum(suf * suf, axis=1, keepdims=True)
    table = jnp.zeros((8, LANES), F32)
    at, row = lane_ids(8), row_ids(8)
    for k in range(n):
        mine = jnp.where(row == 0, pre[k : k + 1, LANES - 1 : LANES], 0.0)
        mine = jnp.where(row == 1, down[k : k + 1, LANES - 1 : LANES], mine)
        mine = jnp.where(row == 2, suf[k : k + 1, 0:1], mine)
        mine = jnp.where(row == 3, norm[k : k + 1, 0:1], mine)
        table = jnp.where(lax.rem(at, 16) == k, mine, table)
    return ps, qs, pre, suf, table


def start_body(
    f_hbm, b_hbm, w_hbm, c_hbm, s_ref, pack_ref, f_ref, b_ref, w_ref, c_ref, sems
):
    n, cols, _ = f_ref.shape
    few = [(w_hbm, w_ref), (c_hbm, c_ref), (b_hbm, b_ref)]
    few += [(f_hbm.at[:, g : g + 16, :], f_ref.at[:, g : g + 16, :]) for g in range(0, cols, 16)]
    copies = [pltpu.make_async_copy(src, dst, sems.at[i]) for i, (src, dst) in enumerate(few)]
    for copy in copies:
        copy.start()
    size = n * cols
    at = size + n * n
    for copy in copies[:3]:
        copy.wait()
    for k in range(n):
        for m in range(n):
            pack_ref[size + k * n + m : size + k * n + m + 1, :] = c_ref[m] * b_ref[k, m]
    for i in range(2):
        for k in range(n):
            pack_ref[at + i * n + k : at + i * n + k + 1, :] = w_ref[i, k]
    for i, g in enumerate(range(0, cols, 16)):
        copies[3 + i].wait()
        vals = [f_ref[m, g : g + 16, :] for m in range(n)]
        for k in range(n):
            v = apply_rows(lambda m: b_ref[k, m], n, lambda m: vals[m])
            s_ref[k * cols + g : k * cols + g + 16, :] = v
            pack_ref[k * cols + g : k * cols + g + 16, :] = v


def side_body(pack_ref, up_ref, down_ref, suf_ref, tab_ref, ext_ref):
    n = ext_ref.shape[1] // LANES
    at = pack_ref.shape[0] - 2 * n
    ps, qs, pre, suf, table = rate_tables(pack_ref[at : at + n, :], pack_ref[at + n : at + 2 * n, :])
    tab_ref[0:8, :] = table
    tab_ref[8 : 8 + n, :] = pre
    for i, (p, q) in enumerate(zip(ps, qs)):
        up_ref[i, 0:n, :] = p
        down_ref[i, 0:n, :] = q
    suf_ref[0:n, :] = suf
    place = row_ids(32)
    first = (lane_ids(32) == 0).astype(F32)
    for k in range(n):
        block = jnp.where(place == k, jnp.broadcast_to(suf[k : k + 1, :], (32, LANES)), 0.0)
        ext_ref[:, k * LANES : (k + 1) * LANES] = jnp.where(place == 16 + k, first, block)


def other_body(near_ref, out_ref):
    out_ref[...] = near_ref[1 - lax.axis_index("core")]


def coupled(pack_ref, h_ref, k, n, rows):
    at = n * h_ref.shape[1] + k * n
    return apply_rows(
        lambda m: pack_ref[at + m : at + m + 1, :], n, lambda m: h_ref[m, rows, :]
    )


def rise(pack_ref, one, two, up_ref, loc_ref, h_ref, a_ref, between=lambda k: None):
    n, cols, _ = h_ref.shape
    for m in range(n):
        rows = slice(m * cols, (m + 1) * cols)
        h_ref[m] = one(rows) + two(rows)
    lane = lane_ids(16)
    first, inner = lane == 0, lane < LANES - 1
    for k in range(n):
        at = n * cols + n * n + n + k
        fall = pack_ref[at : at + 1, :]
        between(k)
        for g in range(cols // 16):
            rows = slice(16 * g, 16 * g + 16)
            wide = slice(k * cols + 16 * g, k * cols + 16 * g + 16)
            start = pack_ref[wide, :]
            above = jnp.where(inner, pltpu.roll(start, LANES - 1, 1), 0.0)
            v = start + fall * above + coupled(pack_ref, h_ref, k, n, rows)
            for i, d in enumerate(STEPS):
                v = v + up_ref[i, k : k + 1, :] * pltpu.roll(v, d, 1)
            loc_ref[wide, :] = v
            a_ref[rows, k * LANES : (k + 1) * LANES] = jnp.where(first, start, v)
    ends = pick(a_ref[...], end_mask(n))
    ends = jnp.concatenate([ends, jnp.zeros((cols, LANES - 32), F32)], axis=1)
    pay = ends[0:16, :]
    for g in range(1, cols // 16):
        pay = pay + pltpu.roll(ends[16 * g : 16 * g + 16, :], 32 * g, 1)
    return pay


def own_body(pack_ref, far_ref, near_ref, up_ref, tab_ref, buf_ref, fup_ref, ftab_ref, h_ref, a_ref):
    n, cols, _ = h_ref.shape
    size = n * cols
    at = size + n * n
    other = 1 - lax.axis_index("core")
    up, down = far_ref[at : at + n, :], far_ref[at + n : at + 2 * n, :]
    lane = lane_ids(n)
    state = [jnp.where(lane >= 1, up, 0.0), up]

    def far_table(k):
        if k < len(STEPS):
            d = STEPS[k]
            p, pre = state
            fup_ref[k, 0:n, :] = p
            state[0] = p * pltpu.roll(p, d, 1)
            state[1] = jnp.where(lane >= d, pre * pltpu.roll(pre, d, 1), pre)

    buf_ref[size : size + 16, :] = rise(
        pack_ref, lambda rows: far_ref[rows, :], lambda rows: near_ref[other, rows, :],
        up_ref, buf_ref, h_ref, a_ref, far_table,
    )
    buf_ref[size + 16 : size + 40, :] = tab_ref[...]
    pre = state[1]
    ftab_ref[8 : 8 + n, :] = pre
    table = jnp.zeros((8, LANES), F32)
    at, row = lane_ids(8), row_ids(8)
    for k in range(n):
        mine = jnp.where(row == 0, pre[k : k + 1, LANES - 1 : LANES], down[k : k + 1, LANES - 1 : LANES])
        table = jnp.where(lax.rem(at, 16) == k, mine, table)
    ftab_ref[0:8, :] = table


def far_body(
    pack_ref, start_ref, next_ref, up_ref, tab_ref, buf_ref, both_ref, loc_ref, pay_ref, h_ref, a_ref
):
    n, cols, _ = h_ref.shape
    size = n * cols
    other = 1 - lax.axis_index("core")
    pay = rise(
        pack_ref, lambda rows: start_ref[rows, :], lambda rows: next_ref[rows, :],
        up_ref, loc_ref, h_ref, a_ref,
    )
    own, near = buf_ref[size : size + 24, :], both_ref[other, size : size + 24, :]
    row = row_ids(8)
    table = jnp.where(row < 2, own[16:24, :], pltpu.roll(near[16:24, :], 2, 0))
    table = jnp.where(row < 4, table, pltpu.roll(tab_ref[0:8, :], 4, 0))
    for peer in range(pay_ref.shape[0]):
        pay_ref[peer, 0:16, :] = own[0:16, :]
        pay_ref[peer, 16:32, :] = near[0:16, :]
        pay_ref[peer, 32:48, :] = pay
        pay_ref[peer, 48:56, :] = table


def entering(r_ref, station):
    mine = lax.axis_index("line")
    at0, row = 16 * station, 48 + 2 * station
    state = jnp.zeros((16, LANES), F32)
    entry = state
    top = state
    for at in range(r_ref.shape[0] - 1):
        lead = pltpu.roll(r_ref[at + 1, at0 : at0 + 16, :], LANES - 16, 1)
        tail = r_ref[at, row + 1 : row + 2, :] * lead
        top = jnp.where(mine == at, tail, top)
        state = r_ref[at, row : row + 1, :] * state + (r_ref[at, at0 : at0 + 16, :] + tail)
        entry = jnp.where(mine == at + 1, state, entry)
    return entry, top


def packed_blocks(gram):
    lane, row = lane_ids(32), row_ids(32)
    corner = pltpu.roll(gram[32:64, :], LANES - 32, 1)
    joined = jnp.where(lane >= row, gram[0:32, :], corner)
    extra = jnp.sum(jnp.where(lane == row, corner, 0.0), axis=0, keepdims=True)
    quarter = lane_ids(8) // 32
    blocks = []
    for part in (pltpu.roll(gram[0:32, :], LANES - 32, 1), joined):
        block = jnp.zeros((8, LANES), F32)
        for a in range(4):
            block = jnp.where(quarter == a, pltpu.roll(part[8 * a : 8 * a + 8, :], 32 * a, 1), block)
        blocks.append(block)
    return (blocks[0], jnp.zeros((1, LANES), F32)), (blocks[1], extra)


def unpacked(upper, joined, extra):
    def spread(block):
        return jnp.concatenate([pltpu.roll(block, (LANES - 32 * a) % LANES, 1) for a in range(4)], axis=0)

    lane, row = lane_ids(32), row_ids(32)
    upper, joined = spread(upper), spread(joined)
    turned = jnp.where(lane < 32, joined, pltpu.roll(upper, 32, 1)).T
    turned = jnp.concatenate([turned, jnp.zeros((LANES, LANES - 32), F32)], axis=1)
    first, second = turned[0:32, :], turned[32:64, :]
    low = jnp.where(lane >= row, joined, first)
    high = jnp.where(lane < row, joined, jnp.where(lane == row, extra, first))
    top = jnp.where(lane < 32, low, pltpu.roll(upper, 32, 1))
    bottom = jnp.where(lane < 32, second, pltpu.roll(high, 32, 1))
    return jnp.concatenate([top, bottom], axis=0)


def down_body(
    pack_ref, r_ref, buf_ref, both_ref, floc_ref, ftab_ref, down_ref, ext_ref,
    loc_ref, pay_ref, h_ref, a_ref,
):
    n, cols, _ = loc_ref.shape
    size = n * cols
    other = 1 - lax.axis_index("core")
    mine, _ = entering(r_ref, 0)
    near, near_top = entering(r_ref, 1)
    far, far_top = entering(r_ref, 2)
    top = near_top + far_top
    lane = lane_ids(16)
    last, first = lane == LANES - 1, lane == 0
    for m in range(n):
        npre = both_ref[other, size + 24 + m : size + 25 + m, :]
        fpre = ftab_ref[8 + m : 9 + m, :]
        for g in range(cols // 16):
            rows, at = slice(m * cols + 16 * g, m * cols + 16 * g + 16), 32 * g + m
            v = both_ref[other, rows, :] + floc_ref[rows, :]
            v = v + npre * near[:, at : at + 1] + fpre * far[:, at : at + 1]
            h_ref[m, 16 * g : 16 * g + 16, :] = jnp.where(last, v + top[:, at : at + 1], v)
    one = lane_ids(1) == 0
    for k in range(n):
        up = pack_ref[size + n * n + k : size + n * n + k + 1, :]
        pre = buf_ref[size + 24 + k : size + 25 + k, :]
        pre = jnp.where(one, 1.0, pltpu.roll(pre, 1, 1))
        for g in range(cols // 16):
            rows = slice(16 * g, 16 * g + 16)
            wide, at = slice(k * cols + 16 * g, k * cols + 16 * g + 16), 32 * g + k
            below = jnp.where(first, 0.0, pltpu.roll(buf_ref[wide, :], 1, 1)) + pre * mine[:, at : at + 1]
            v = pack_ref[wide, :] + up * below + coupled(pack_ref, h_ref, k, n, rows)
            for i, d in enumerate(STEPS):
                v = v + down_ref[i, k : k + 1, :] * pltpu.roll(v, LANES - d, 1)
            loc_ref[k, rows, :] = v
            a_ref[rows, k * LANES : (k + 1) * LANES] = v
    a_ref[cols : cols + 32, :] = ext_ref[...]
    total = dot_nt(a_ref[0:cols, :], a_ref[...])
    total = jnp.concatenate([total, jnp.zeros((cols, 32), F32)], axis=1)
    lane = lane_ids(16)
    edges = jnp.zeros((16, LANES), F32)
    for g in range(cols // 16):
        moved = pltpu.roll(total[16 * g : 16 * g + 16, :], (32 * g + 64) % LANES, 1)
        edges = jnp.where(lane // 32 == g, moved, edges)
    (one, _), (two, extra) = packed_blocks(total)
    for peer in range(pay_ref.shape[0]):
        pay_ref[peer, 0:8, :] = one
        pay_ref[peer, 8:16, :] = two
        pay_ref[peer, 16:32, :] = edges
        pay_ref[peer, 32:40, :] = jnp.where(row_ids(8) == 4, extra, buf_ref[size + 16 : size + 24, :])


def line_body(r_ref, gram_ref, entry_ref, left_ref, right_ref):
    peers = r_ref.shape[0]
    cols = left_ref.shape[0]
    mine = lax.axis_index("line")
    lane = lane_ids(16)
    first = lane % 32 < 16
    zero = jnp.zeros((16, LANES), F32)
    entry = zero
    state = zero
    left = [zero] * (cols // 16)
    right = [zero] * (cols // 16)
    for at in range(peers - 2, -1, -1):
        state = r_ref[at + 1, 34:35, :] * state + r_ref[at + 1, 16:32, :]
        entry = jnp.where(mine == at, state, entry)
        back = pltpu.roll(state, LANES - 16, 1)
        cross = r_ref[at, 16:32, :] + (0.5 * r_ref[at, 35:36, :]) * back
        a = jnp.where(first, cross, state)
        b = jnp.where(first, back, pltpu.roll(cross, 16, 1))
        for g in range(cols // 16):
            shift = (32 * (at - g)) % LANES
            left[g] = jnp.where(lane // 32 == at, pltpu.roll(a, shift, 1), left[g])
            right[g] = jnp.where(lane // 32 == at, pltpu.roll(b, shift, 1), right[g])
    for g in range(cols // 16):
        rows = slice(16 * g, 16 * g + 16)
        left_ref[rows, :] = left[g]
        right_ref[rows, :] = right[g]
    fix = dot_nt(left_ref[...], right_ref[...])
    fix = jnp.concatenate([fix, jnp.zeros((cols, LANES - cols), F32)], axis=1)
    (one, none), (two, extra) = packed_blocks(fix)
    for at in range(peers):
        one = one + r_ref[at, 0:8, :]
        two = two + r_ref[at, 8:16, :]
        extra = extra + r_ref[at, 36:37, :]
    for block, row, core in ((one, none, 0), (two, extra, 1)):
        for peer in range(core, gram_ref.shape[0], NCORE):
            for i in range(8):
                gram_ref[peer, i] = block[i : i + 1, :]
            gram_ref[peer, 8] = row
    entry_ref[...] = entry


def spread_rows(out_ref, rows):
    for peer in range(out_ref.shape[0]):
        for i, row in enumerate(rows):
            out_ref[peer, i] = row


def summed_rows(r_ref, first, step):
    rows = []
    for i in range(r_ref.shape[1]):
        total = r_ref[first, i]
        for peer in range(first + step, r_ref.shape[0], step):
            total = total + r_ref[peer, i]
        rows.append(total)
    return rows


def sum_body(r_ref, o_ref):
    spread_rows(o_ref, summed_rows(r_ref, 0, 1))


def inverse_factor(scale, gram, v_ref):
    cols = gram.shape[0]
    count = cols // 8
    lane, row = lane_ids(8), row_ids(8)
    tiles = []
    for t in range(count):
        unit = jnp.where(lane - 64 == row + 8 * t, 1.0, 0.0)
        tiles.append(jnp.where(lane < 64, gram[8 * t : 8 * t + 8, :], unit))
    for p in range(count):
        later = range(p + 1, count)
        r = [tiles[p][i : i + 1, :] for i in range(8)]
        s = {}
        for i in range(8):
            for j in range(i + 1):
                at = 8 * p + j
                s[i, j] = jnp.broadcast_to(r[i][:, at : at + 1], (1, LANES))
        c = []
        for i in range(8):
            at = 8 * p + i
            c.append([jnp.broadcast_to(tiles[t][:, at : at + 1], (8, LANES)) for t in later])
        scaled = []
        for i in range(8):
            inv = 1.0 / s[i, i]
            for t in range(i + 1, 8):
                f = s[t, i] * inv
                for u in range(i + 1, t + 1):
                    s[t, u] = s[t, u] - f * s[u, i]
                r[t] = r[t] - f * r[i]
                c[t] = [x - f * y for x, y in zip(c[t], c[i])]
            v_ref[8 * p + i : 8 * p + i + 1, :] = r[i] * (scale / jnp.sqrt(s[i, i]))
            scaled.append(r[i] * inv)
        for x, t in enumerate(later):
            for i in range(8):
                tiles[t] = tiles[t] - c[i][x] * scaled[i]
    return pltpu.roll(v_ref[...], 64, 1)[:, 0:64]


def basis_body(scale, r_ref, loc_ref, suf_ref, entry_ref, out_ref, f_ref, v_ref):
    n, cols, _ = loc_ref.shape
    for k in range(n):
        suf = suf_ref[k : k + 1, :]
        for g in range(cols // 16):
            rows, at = slice(16 * g, 16 * g + 16), 32 * g + 16 + k
            v = loc_ref[k, rows, :] + suf * entry_ref[:, at : at + 1]
            f_ref[rows, k * LANES : (k + 1) * LANES] = v
    upper, joined = (summed_rows(r_ref, core, NCORE) for core in range(NCORE))
    gram = unpacked(jnp.concatenate(upper[:8], axis=0), jnp.concatenate(joined[:8], axis=0), joined[8])
    inv = inverse_factor(scale, gram, v_ref)
    out = jnp.dot(inv, f_ref[...], precision=HIGH, preferred_element_type=F32)
    for k in range(n):
        out_ref[k] = out[:, k * LANES : (k + 1) * LANES]


def in_hbm(value):
    return pltpu.with_memory_space_constraint(value, pltpu.HBM)


def exchange(value, axis):
    return lax.all_to_all(value, axis, 0, 0, tiled=True)


def local(forcing, block_inverse, wall_rates, span_couple):
    n, cols, _, pts = forcing.shape
    peers = lax.axis_size("line")
    stations = lax.axis_size("z") * lax.axis_size("y") * lax.axis_size("core")
    rows = n * stations * pts * peers
    field = (n, cols, pts)
    f, b, w, c = map(in_hbm, (forcing.reshape(field), block_inverse, wall_rates, span_couple))
    pairs = [(i, 1 if i % 2 else -1) for i in range(stations)]
    across = [(i, (i + d) % stations) for i, d in pairs]
    work = 2 * n * n * cols * pts
    size = n * cols
    scratch = pltpu.VMEM(field, F32)
    wide = pltpu.VMEM((cols, n * pts), F32)
    tall = pltpu.VMEM((cols + 32, n * pts), F32)

    inputs = [pltpu.VMEM(a.shape, F32) for a in (f, b, w)] + [pltpu.SMEM(c.shape, F32)]
    steps = (len(STEPS), 16, pts)
    start, pack = call(
        start_body,
        [(size, pts), (size + n * n + 2 * n, pts)],
        work,
        inputs + [pltpu.SemaphoreType.DMA((3 + cols // 16,))],
        HBM,
    )(f, b, w, c)
    fpack = lax.ppermute(pack, TILE, across)
    near = lax.all_gather(start, "core")
    tables_of, near = lax.optimization_barrier((pack, near))
    beyond = lax.ppermute(call(other_body, (size, pts))(near), TILE, across)
    up, down, suf, tab, ext = call(
        side_body, [steps, steps, (16, pts), (24, pts), (32, n * pts)], work // 4
    )(tables_of)
    buf, fup, ftab = call(own_body, [(size + 40, pts), steps, (24, pts)], 2 * work, [scratch, wide])(
        pack, fpack, near, up, tab
    )
    both = lax.all_gather(buf, "core")
    floc, pay = call(far_body, [(size, pts), (peers, 56, pts)], 2 * work, [scratch, wide])(
        fpack, start, beyond, fup, ftab, buf, both
    )
    got = exchange(pay, "line")
    loc, pay = call(down_body, [field, (peers, 40, pts)], 4 * work, [scratch, tall])(
        pack, got, buf, both, floc, ftab, down, ext
    )
    side = pltpu.VMEM((cols, pts), F32)
    part = (9, 1, pts)
    gram, entry = call(line_body, [(NY * NCORE,) + part, (16, pts)], work // 4, [side, side])(
        exchange(pay, "line")
    )
    gram = call(sum_body, (NZ * NCORE,) + part)(exchange(gram, ("y", "core")))
    gram = exchange(gram, ("z", "core"))

    def basis(*refs):
        basis_body(math.sqrt(rows), *refs)

    out = call(basis, field, 4 * work, [wide, pltpu.VMEM((cols, pts), F32)])(
        gram, loc, suf, entry
    )
    return out.reshape(n, cols, 1, pts)


def solution(mesh):
    devices = mesh.devices.reshape(mesh.shape["line"], NZ, NY, NCORE)
    inner = Mesh(devices, ("line",) + TILE)
    spec = P(None, None, TILE, "line")
    return jax.shard_map(
        local, mesh=inner, in_specs=(spec, spec, spec, P()), out_specs=spec, check_vma=False
    )
```

```python
import math

import jax
import jax.numpy as jnp
from jax import lax
from jax.experimental import pallas as pl
from jax.experimental.pallas import tpu as pltpu
from jax.sharding import Mesh, PartitionSpec as P

NZ, NY, NCORE = 8, 8, 2
TILE = ("z", "y", "core")
HIGH = lax.Precision.HIGHEST
F32 = jnp.float32
LANES = 128
LIMIT = 16 << 20
STEPS = (1, 2, 4, 8, 16, 32, 64)
VMEM = pl.BlockSpec(memory_space=pltpu.VMEM)
HBM = pl.BlockSpec(memory_space=pltpu.HBM)


def lane_ids(rows):
    return lax.broadcasted_iota(jnp.int32, (rows, LANES), 1)


def row_ids(rows):
    return lax.broadcasted_iota(jnp.int32, (rows, LANES), 0)


def dot_nt(a, b):
    return lax.dot_general(
        a, b, (((1,), (1,)), ((), ())), precision=HIGH, preferred_element_type=F32
    )


def call(body, outs, flops=0, scratch=(), space=VMEM):
    many = isinstance(outs[0], tuple)
    shapes = [jax.ShapeDtypeStruct(s, F32) for s in (outs if many else [outs])]

    def run(*args):
        size = sum(a.size for a in args) + sum(math.prod(s.shape) for s in shapes)
        return pl.pallas_call(
            body,
            out_shape=shapes if many else shapes[0],
            in_specs=[space] * len(args),
            out_specs=[VMEM] * len(shapes) if many else VMEM,
            scratch_shapes=list(scratch),
            compiler_params=pltpu.CompilerParams(vmem_limit_bytes=LIMIT),
            cost_estimate=pl.CostEstimate(
                flops=flops, bytes_accessed=4 * size, transcendentals=0
            ),
        )(*args)

    return run


def apply_rows(block, n, take):
    total = block(0) * take(0)
    for m in range(1, n):
        total = total + block(m) * take(m)
    return total


def pick(values, mask):
    total = None
    for _ in range(3):
        piece = values.astype(jnp.bfloat16)
        values = values - piece.astype(F32)
        part = lax.dot_general(
            piece, mask, (((1,), (1,)), ((), ())), preferred_element_type=F32
        )
        total = part if total is None else total + part
    return total


def end_mask(n):
    wide = (32, n * LANES)
    col = lax.broadcasted_iota(jnp.int32, wide, 1)
    row = lax.broadcasted_iota(jnp.int32, wide, 0)
    return (col == jnp.where(row < 16, row * LANES + LANES - 1, (row - 16) * LANES)).astype(
        jnp.bfloat16
    )


def rate_tables(up, down):
    n = up.shape[0]
    lane = lane_ids(n)
    pre, suf = up, down
    p = jnp.where(lane >= 1, up, 0.0)
    q = jnp.where(lane < LANES - 1, down, 0.0)
    ps, qs = [], []
    for d in STEPS:
        ps.append(p)
        qs.append(q)
        p = p * pltpu.roll(p, d, 1)
        q = q * pltpu.roll(q, LANES - d, 1)
        pre = jnp.where(lane >= d, pre * pltpu.roll(pre, d, 1), pre)
        suf = jnp.where(lane < LANES - d, suf * pltpu.roll(suf, LANES - d, 1), suf)
    norm = jnp.sum(suf * suf, axis=1, keepdims=True)
    table = jnp.zeros((8, LANES), F32)
    at, row = lane_ids(8), row_ids(8)
    for k in range(n):
        mine = jnp.where(row == 0, pre[k : k + 1, LANES - 1 : LANES], 0.0)
        mine = jnp.where(row == 1, down[k : k + 1, LANES - 1 : LANES], mine)
        mine = jnp.where(row == 2, suf[k : k + 1, 0:1], mine)
        mine = jnp.where(row == 3, norm[k : k + 1, 0:1], mine)
        table = jnp.where(lax.rem(at, 16) == k, mine, table)
    return ps, qs, pre, suf, table


def start_body(
    f_hbm, b_hbm, w_hbm, c_hbm, s_ref, pack_ref, f_ref, b_ref, w_ref, c_ref, sems
):
    n, cols, _ = f_ref.shape
    few = [(w_hbm, w_ref), (c_hbm, c_ref), (b_hbm, b_ref)]
    few += [(f_hbm.at[:, g : g + 16, :], f_ref.at[:, g : g + 16, :]) for g in range(0, cols, 16)]
    copies = [pltpu.make_async_copy(src, dst, sems.at[i]) for i, (src, dst) in enumerate(few)]
    for copy in copies:
        copy.start()
    size = n * cols
    at = size + n * n
    for copy in copies[:3]:
        copy.wait()
    for k in range(n):
        for m in range(n):
            pack_ref[size + k * n + m : size + k * n + m + 1, :] = c_ref[m] * b_ref[k, m]
    for i in range(2):
        for k in range(n):
            pack_ref[at + i * n + k : at + i * n + k + 1, :] = w_ref[i, k]
    for i, g in enumerate(range(0, cols, 16)):
        copies[3 + i].wait()
        vals = [f_ref[m, g : g + 16, :] for m in range(n)]
        for k in range(n):
            v = apply_rows(lambda m: b_ref[k, m], n, lambda m: vals[m])
            s_ref[k * cols + g : k * cols + g + 16, :] = v
            pack_ref[k * cols + g : k * cols + g + 16, :] = v


def side_body(pack_ref, up_ref, down_ref, suf_ref, tab_ref, ext_ref):
    n = ext_ref.shape[1] // LANES
    at = pack_ref.shape[0] - 2 * n
    ps, qs, pre, suf, table = rate_tables(pack_ref[at : at + n, :], pack_ref[at + n : at + 2 * n, :])
    tab_ref[0:8, :] = table
    tab_ref[8 : 8 + n, :] = pre
    for i, (p, q) in enumerate(zip(ps, qs)):
        up_ref[i, 0:n, :] = p
        down_ref[i, 0:n, :] = q
    suf_ref[0:n, :] = suf
    place = row_ids(32)
    first = (lane_ids(32) == 0).astype(F32)
    for k in range(n):
        block = jnp.where(place == k, jnp.broadcast_to(suf[k : k + 1, :], (32, LANES)), 0.0)
        ext_ref[:, k * LANES : (k + 1) * LANES] = jnp.where(place == 16 + k, first, block)


def other_body(near_ref, out_ref):
    out_ref[...] = near_ref[1 - lax.axis_index("core")]


def coupled(pack_ref, h_ref, k, n, rows):
    at = n * h_ref.shape[1] + k * n
    return apply_rows(
        lambda m: pack_ref[at + m : at + m + 1, :], n, lambda m: h_ref[m, rows, :]
    )


def rise(pack_ref, one, two, up_ref, loc_ref, h_ref, a_ref, between=lambda k: None):
    n, cols, _ = h_ref.shape
    for m in range(n):
        rows = slice(m * cols, (m + 1) * cols)
        h_ref[m] = one(rows) + two(rows)
    lane = lane_ids(32)
    first, inner = lane == 0, lane < LANES - 1
    for k in range(n):
        at = n * cols + n * n + n + k
        fall = pack_ref[at : at + 1, :]
        between(k)
        for g in range(cols // 32):
            rows = slice(32 * g, 32 * g + 32)
            wide = slice(k * cols + 32 * g, k * cols + 32 * g + 32)
            start = pack_ref[wide, :]
            above = jnp.where(inner, pltpu.roll(start, LANES - 1, 1), 0.0)
            v = start + fall * above + coupled(pack_ref, h_ref, k, n, rows)
            for i, d in enumerate(STEPS):
                v = v + up_ref[i, k : k + 1, :] * pltpu.roll(v, d, 1)
            loc_ref[wide, :] = v
            a_ref[rows, k * LANES : (k + 1) * LANES] = jnp.where(first, start, v)
    ends = pick(a_ref[...], end_mask(n))
    ends = jnp.concatenate([ends, jnp.zeros((cols, LANES - 32), F32)], axis=1)
    pay = ends[0:16, :]
    for g in range(1, cols // 16):
        pay = pay + pltpu.roll(ends[16 * g : 16 * g + 16, :], 32 * g, 1)
    return pay


def own_body(pack_ref, far_ref, near_ref, up_ref, tab_ref, buf_ref, fup_ref, ftab_ref, h_ref, a_ref):
    n, cols, _ = h_ref.shape
    size = n * cols
    at = size + n * n
    other = 1 - lax.axis_index("core")
    up, down = far_ref[at : at + n, :], far_ref[at + n : at + 2 * n, :]
    lane = lane_ids(n)
    state = [jnp.where(lane >= 1, up, 0.0), up]

    def far_table(k):
        if k < len(STEPS):
            d = STEPS[k]
            p, pre = state
            fup_ref[k, 0:n, :] = p
            state[0] = p * pltpu.roll(p, d, 1)
            state[1] = jnp.where(lane >= d, pre * pltpu.roll(pre, d, 1), pre)

    buf_ref[size : size + 16, :] = rise(
        pack_ref, lambda rows: far_ref[rows, :], lambda rows: near_ref[other, rows, :],
        up_ref, buf_ref, h_ref, a_ref, far_table,
    )
    buf_ref[size + 16 : size + 40, :] = tab_ref[...]
    pre = state[1]
    ftab_ref[8 : 8 + n, :] = pre
    table = jnp.zeros((8, LANES), F32)
    at, row = lane_ids(8), row_ids(8)
    for k in range(n):
        mine = jnp.where(row == 0, pre[k : k + 1, LANES - 1 : LANES], down[k : k + 1, LANES - 1 : LANES])
        table = jnp.where(lax.rem(at, 16) == k, mine, table)
    ftab_ref[0:8, :] = table


def far_body(
    pack_ref, start_ref, next_ref, up_ref, tab_ref, buf_ref, both_ref, loc_ref, pay_ref, h_ref, a_ref
):
    n, cols, _ = h_ref.shape
    size = n * cols
    other = 1 - lax.axis_index("core")
    pay = rise(
        pack_ref, lambda rows: start_ref[rows, :], lambda rows: next_ref[rows, :],
        up_ref, loc_ref, h_ref, a_ref,
    )
    own, near = buf_ref[size : size + 24, :], both_ref[other, size : size + 24, :]
    row = row_ids(8)
    table = jnp.where(row < 2, own[16:24, :], pltpu.roll(near[16:24, :], 2, 0))
    table = jnp.where(row < 4, table, pltpu.roll(tab_ref[0:8, :], 4, 0))
    for peer in range(pay_ref.shape[0]):
        pay_ref[peer, 0:16, :] = own[0:16, :]
        pay_ref[peer, 16:32, :] = near[0:16, :]
        pay_ref[peer, 32:48, :] = pay
        pay_ref[peer, 48:56, :] = table


def entering(r_ref, station):
    mine = lax.axis_index("line")
    at0, row = 16 * station, 48 + 2 * station
    state = jnp.zeros((16, LANES), F32)
    entry = state
    top = state
    for at in range(r_ref.shape[0] - 1):
        lead = pltpu.roll(r_ref[at + 1, at0 : at0 + 16, :], LANES - 16, 1)
        tail = r_ref[at, row + 1 : row + 2, :] * lead
        top = jnp.where(mine == at, tail, top)
        state = r_ref[at, row : row + 1, :] * state + (r_ref[at, at0 : at0 + 16, :] + tail)
        entry = jnp.where(mine == at + 1, state, entry)
    return entry, top


def packed_blocks(gram):
    lane, row = lane_ids(32), row_ids(32)
    corner = pltpu.roll(gram[32:64, :], LANES - 32, 1)
    joined = jnp.where(lane >= row, gram[0:32, :], corner)
    extra = jnp.sum(jnp.where(lane == row, corner, 0.0), axis=0, keepdims=True)
    quarter = lane_ids(8) // 32
    blocks = []
    for part in (pltpu.roll(gram[0:32, :], LANES - 32, 1), joined):
        block = jnp.zeros((8, LANES), F32)
        for a in range(4):
            block = jnp.where(quarter == a, pltpu.roll(part[8 * a : 8 * a + 8, :], 32 * a, 1), block)
        blocks.append(block)
    return (blocks[0], jnp.zeros((1, LANES), F32)), (blocks[1], extra)


def unpacked(upper, joined, extra):
    def spread(block):
        return jnp.concatenate([pltpu.roll(block, (LANES - 32 * a) % LANES, 1) for a in range(4)], axis=0)

    lane, row = lane_ids(32), row_ids(32)
    upper, joined = spread(upper), spread(joined)
    turned = jnp.where(lane < 32, joined, pltpu.roll(upper, 32, 1)).T
    turned = jnp.concatenate([turned, jnp.zeros((LANES, LANES - 32), F32)], axis=1)
    first, second = turned[0:32, :], turned[32:64, :]
    low = jnp.where(lane >= row, joined, first)
    high = jnp.where(lane < row, joined, jnp.where(lane == row, extra, first))
    top = jnp.where(lane < 32, low, pltpu.roll(upper, 32, 1))
    bottom = jnp.where(lane < 32, second, pltpu.roll(high, 32, 1))
    return jnp.concatenate([top, bottom], axis=0)


def down_body(
    pack_ref, r_ref, buf_ref, both_ref, floc_ref, ftab_ref, down_ref, ext_ref,
    loc_ref, pay_ref, h_ref, a_ref,
):
    n, cols, _ = loc_ref.shape
    size = n * cols
    other = 1 - lax.axis_index("core")
    mine, _ = entering(r_ref, 0)
    near, near_top = entering(r_ref, 1)
    far, far_top = entering(r_ref, 2)
    top = near_top + far_top
    lane = lane_ids(16)
    last, first = lane == LANES - 1, lane == 0
    for m in range(n):
        npre = both_ref[other, size + 24 + m : size + 25 + m, :]
        fpre = ftab_ref[8 + m : 9 + m, :]
        for g in range(cols // 16):
            rows, at = slice(m * cols + 16 * g, m * cols + 16 * g + 16), 32 * g + m
            v = both_ref[other, rows, :] + floc_ref[rows, :]
            v = v + npre * near[:, at : at + 1] + fpre * far[:, at : at + 1]
            h_ref[m, 16 * g : 16 * g + 16, :] = jnp.where(last, v + top[:, at : at + 1], v)
    one = lane_ids(1) == 0
    for k in range(n):
        up = pack_ref[size + n * n + k : size + n * n + k + 1, :]
        pre = buf_ref[size + 24 + k : size + 25 + k, :]
        pre = jnp.where(one, 1.0, pltpu.roll(pre, 1, 1))
        for g in range(cols // 32):
            rows = slice(32 * g, 32 * g + 32)
            wide, at = slice(k * cols + 32 * g, k * cols + 32 * g + 32), 64 * g + k
            entry = jnp.concatenate([mine[:, at : at + 1], mine[:, at + 32 : at + 33]], axis=0)
            below = jnp.where(lane_ids(32) == 0, 0.0, pltpu.roll(buf_ref[wide, :], 1, 1)) + pre * entry
            v = pack_ref[wide, :] + up * below + coupled(pack_ref, h_ref, k, n, rows)
            for i, d in enumerate(STEPS):
                v = v + down_ref[i, k : k + 1, :] * pltpu.roll(v, LANES - d, 1)
            loc_ref[k, rows, :] = v
            a_ref[rows, k * LANES : (k + 1) * LANES] = v
    a_ref[cols : cols + 32, :] = ext_ref[...]
    total = dot_nt(a_ref[0:cols, :], a_ref[...])
    total = jnp.concatenate([total, jnp.zeros((cols, 32), F32)], axis=1)
    lane = lane_ids(16)
    edges = jnp.zeros((16, LANES), F32)
    for g in range(cols // 16):
        moved = pltpu.roll(total[16 * g : 16 * g + 16, :], (32 * g + 64) % LANES, 1)
        edges = jnp.where(lane // 32 == g, moved, edges)
    (one, _), (two, extra) = packed_blocks(total)
    for peer in range(pay_ref.shape[0]):
        pay_ref[peer, 0:8, :] = one
        pay_ref[peer, 8:16, :] = two
        pay_ref[peer, 16:32, :] = edges
        pay_ref[peer, 32:40, :] = jnp.where(row_ids(8) == 4, extra, buf_ref[size + 16 : size + 24, :])


def line_body(r_ref, gram_ref, entry_ref, left_ref, right_ref):
    peers = r_ref.shape[0]
    cols = left_ref.shape[0]
    mine = lax.axis_index("line")
    lane = lane_ids(16)
    first = lane % 32 < 16
    zero = jnp.zeros((16, LANES), F32)
    entry = zero
    state = zero
    left = [zero] * (cols // 16)
    right = [zero] * (cols // 16)
    for at in range(peers - 2, -1, -1):
        state = r_ref[at + 1, 34:35, :] * state + r_ref[at + 1, 16:32, :]
        entry = jnp.where(mine == at, state, entry)
        back = pltpu.roll(state, LANES - 16, 1)
        cross = r_ref[at, 16:32, :] + (0.5 * r_ref[at, 35:36, :]) * back
        a = jnp.where(first, cross, state)
        b = jnp.where(first, back, pltpu.roll(cross, 16, 1))
        for g in range(cols // 16):
            shift = (32 * (at - g)) % LANES
            left[g] = jnp.where(lane // 32 == at, pltpu.roll(a, shift, 1), left[g])
            right[g] = jnp.where(lane // 32 == at, pltpu.roll(b, shift, 1), right[g])
    for g in range(cols // 16):
        rows = slice(16 * g, 16 * g + 16)
        left_ref[rows, :] = left[g]
        right_ref[rows, :] = right[g]
    fix = dot_nt(left_ref[...], right_ref[...])
    fix = jnp.concatenate([fix, jnp.zeros((cols, LANES - cols), F32)], axis=1)
    (one, none), (two, extra) = packed_blocks(fix)
    for at in range(peers):
        one = one + r_ref[at, 0:8, :]
        two = two + r_ref[at, 8:16, :]
        extra = extra + r_ref[at, 36:37, :]
    for block, row, core in ((one, none, 0), (two, extra, 1)):
        for peer in range(core, gram_ref.shape[0], NCORE):
            for i in range(8):
                gram_ref[peer, i] = block[i : i + 1, :]
            gram_ref[peer, 8] = row
    entry_ref[...] = entry


def spread_rows(out_ref, rows):
    for peer in range(out_ref.shape[0]):
        for i, row in enumerate(rows):
            out_ref[peer, i] = row


def summed_rows(r_ref, first, step):
    rows = []
    for i in range(r_ref.shape[1]):
        total = r_ref[first, i]
        for peer in range(first + step, r_ref.shape[0], step):
            total = total + r_ref[peer, i]
        rows.append(total)
    return rows


def sum_body(r_ref, o_ref):
    spread_rows(o_ref, summed_rows(r_ref, 0, 1))


def inverse_factor(scale, gram, v_ref):
    cols = gram.shape[0]
    count = cols // 8
    lane, row = lane_ids(8), row_ids(8)
    tiles = []
    for t in range(count):
        unit = jnp.where(lane - 64 == row + 8 * t, 1.0, 0.0)
        tiles.append(jnp.where(lane < 64, gram[8 * t : 8 * t + 8, :], unit))
    for p in range(count):
        later = range(p + 1, count)
        r = [tiles[p][i : i + 1, :] for i in range(8)]
        s = {}
        for i in range(8):
            for j in range(i + 1):
                at = 8 * p + j
                s[i, j] = jnp.broadcast_to(r[i][:, at : at + 1], (1, LANES))
        c = []
        for i in range(8):
            at = 8 * p + i
            c.append([jnp.broadcast_to(tiles[t][:, at : at + 1], (8, LANES)) for t in later])
        scaled = []
        for i in range(8):
            inv = 1.0 / s[i, i]
            for t in range(i + 1, 8):
                f = s[t, i] * inv
                for u in range(i + 1, t + 1):
                    s[t, u] = s[t, u] - f * s[u, i]
                r[t] = r[t] - f * r[i]
                c[t] = [x - f * y for x, y in zip(c[t], c[i])]
            v_ref[8 * p + i : 8 * p + i + 1, :] = r[i] * (scale / jnp.sqrt(s[i, i]))
            scaled.append(r[i] * inv)
        for x, t in enumerate(later):
            for i in range(8):
                tiles[t] = tiles[t] - c[i][x] * scaled[i]
    return pltpu.roll(v_ref[...], 64, 1)[:, 0:64]


def basis_body(scale, r_ref, loc_ref, suf_ref, entry_ref, out_ref, f_ref, v_ref):
    n, cols, _ = loc_ref.shape
    for k in range(n):
        suf = suf_ref[k : k + 1, :]
        for g in range(cols // 16):
            rows, at = slice(16 * g, 16 * g + 16), 32 * g + 16 + k
            v = loc_ref[k, rows, :] + suf * entry_ref[:, at : at + 1]
            f_ref[rows, k * LANES : (k + 1) * LANES] = v
    upper, joined = (summed_rows(r_ref, core, NCORE) for core in range(NCORE))
    gram = unpacked(jnp.concatenate(upper[:8], axis=0), jnp.concatenate(joined[:8], axis=0), joined[8])
    inv = inverse_factor(scale, gram, v_ref)
    out = jnp.dot(inv, f_ref[...], precision=HIGH, preferred_element_type=F32)
    for k in range(n):
        out_ref[k] = out[:, k * LANES : (k + 1) * LANES]


def in_hbm(value):
    return pltpu.with_memory_space_constraint(value, pltpu.HBM)


def exchange(value, axis):
    return lax.all_to_all(value, axis, 0, 0, tiled=True)


def local(forcing, block_inverse, wall_rates, span_couple):
    n, cols, _, pts = forcing.shape
    peers = lax.axis_size("line")
    stations = lax.axis_size("z") * lax.axis_size("y") * lax.axis_size("core")
    rows = n * stations * pts * peers
    field = (n, cols, pts)
    f, b, w, c = map(in_hbm, (forcing.reshape(field), block_inverse, wall_rates, span_couple))
    pairs = [(i, 1 if i % 2 else -1) for i in range(stations)]
    across = [(i, (i + d) % stations) for i, d in pairs]
    work = 2 * n * n * cols * pts
    size = n * cols
    scratch = pltpu.VMEM(field, F32)
    wide = pltpu.VMEM((cols, n * pts), F32)
    tall = pltpu.VMEM((cols + 32, n * pts), F32)

    inputs = [pltpu.VMEM(a.shape, F32) for a in (f, b, w)] + [pltpu.SMEM(c.shape, F32)]
    steps = (len(STEPS), 16, pts)
    start, pack = call(
        start_body,
        [(size, pts), (size + n * n + 2 * n, pts)],
        work,
        inputs + [pltpu.SemaphoreType.DMA((3 + cols // 16,))],
        HBM,
    )(f, b, w, c)
    fpack = lax.ppermute(pack, TILE, across)
    near = lax.all_gather(start, "core")
    tables_of, near = lax.optimization_barrier((pack, near))
    beyond = lax.ppermute(call(other_body, (size, pts))(near), TILE, across)
    up, down, suf, tab, ext = call(
        side_body, [steps, steps, (16, pts), (24, pts), (32, n * pts)], work // 4
    )(tables_of)
    buf, fup, ftab = call(own_body, [(size + 40, pts), steps, (24, pts)], 2 * work, [scratch, wide])(
        pack, fpack, near, up, tab
    )
    both = lax.all_gather(buf, "core")
    floc, pay = call(far_body, [(size, pts), (peers, 56, pts)], 2 * work, [scratch, wide])(
        fpack, start, beyond, fup, ftab, buf, both
    )
    got = exchange(pay, "line")
    loc, pay = call(down_body, [field, (peers, 40, pts)], 4 * work, [scratch, tall])(
        pack, got, buf, both, floc, ftab, down, ext
    )
    side = pltpu.VMEM((cols, pts), F32)
    part = (9, 1, pts)
    gram, entry = call(line_body, [(NY * NCORE,) + part, (16, pts)], work // 4, [side, side])(
        exchange(pay, "line")
    )
    gram = call(sum_body, (NZ * NCORE,) + part)(exchange(gram, ("y", "core")))
    gram = exchange(gram, ("z", "core"))

    def basis(*refs):
        basis_body(math.sqrt(rows), *refs)

    out = call(basis, field, 4 * work, [wide, pltpu.VMEM((cols, pts), F32)])(
        gram, loc, suf, entry
    )
    return out.reshape(n, cols, 1, pts)


def solution(mesh):
    devices = mesh.devices.reshape(mesh.shape["line"], NZ, NY, NCORE)
    inner = Mesh(devices, ("line",) + TILE)
    spec = P(None, None, TILE, "line")
    return jax.shard_map(
        local, mesh=inner, in_specs=(spec, spec, spec, P()), out_specs=spec, check_vma=False
    )
```

```python
import math

import jax
import jax.numpy as jnp
from jax import lax
from jax.experimental import pallas as pl
from jax.experimental.pallas import tpu as pltpu
from jax.sharding import Mesh, PartitionSpec as P

NZ, NY, NCORE = 8, 8, 2
TILE = ("z", "y", "core")
HIGH = lax.Precision.HIGHEST
F32 = jnp.float32
LANES = 128
LIMIT = 16 << 20
STEPS = (1, 2, 4, 8, 16, 32, 64)
VMEM = pl.BlockSpec(memory_space=pltpu.VMEM)
HBM = pl.BlockSpec(memory_space=pltpu.HBM)


def lane_ids(rows):
    return lax.broadcasted_iota(jnp.int32, (rows, LANES), 1)


def row_ids(rows):
    return lax.broadcasted_iota(jnp.int32, (rows, LANES), 0)


def dot_nt(a, b):
    return lax.dot_general(
        a, b, (((1,), (1,)), ((), ())), precision=HIGH, preferred_element_type=F32
    )


def call(body, outs, flops=0, scratch=(), space=VMEM):
    many = isinstance(outs[0], tuple)
    shapes = [jax.ShapeDtypeStruct(s, F32) for s in (outs if many else [outs])]

    def run(*args):
        size = sum(a.size for a in args) + sum(math.prod(s.shape) for s in shapes)
        return pl.pallas_call(
            body,
            out_shape=shapes if many else shapes[0],
            in_specs=[space] * len(args),
            out_specs=[VMEM] * len(shapes) if many else VMEM,
            scratch_shapes=list(scratch),
            compiler_params=pltpu.CompilerParams(vmem_limit_bytes=LIMIT),
            cost_estimate=pl.CostEstimate(
                flops=flops, bytes_accessed=4 * size, transcendentals=0
            ),
        )(*args)

    return run


def apply_rows(block, n, take):
    total = block(0) * take(0)
    for m in range(1, n):
        total = total + block(m) * take(m)
    return total


def pick(values, mask):
    total = None
    for _ in range(3):
        piece = values.astype(jnp.bfloat16)
        values = values - piece.astype(F32)
        part = lax.dot_general(
            piece, mask, (((1,), (1,)), ((), ())), preferred_element_type=F32
        )
        total = part if total is None else total + part
    return total


def end_mask(n):
    wide = (32, n * LANES)
    col = lax.broadcasted_iota(jnp.int32, wide, 1)
    row = lax.broadcasted_iota(jnp.int32, wide, 0)
    return (col == jnp.where(row < 16, row * LANES + LANES - 1, (row - 16) * LANES)).astype(
        jnp.bfloat16
    )


def rate_tables(up, down):
    n = up.shape[0]
    lane = lane_ids(n)
    pre, suf = up, down
    p = jnp.where(lane >= 1, up, 0.0)
    q = jnp.where(lane < LANES - 1, down, 0.0)
    ps, qs = [], []
    for d in STEPS:
        ps.append(p)
        qs.append(q)
        p = p * pltpu.roll(p, d, 1)
        q = q * pltpu.roll(q, LANES - d, 1)
        pre = jnp.where(lane >= d, pre * pltpu.roll(pre, d, 1), pre)
        suf = jnp.where(lane < LANES - d, suf * pltpu.roll(suf, LANES - d, 1), suf)
    norm = jnp.sum(suf * suf, axis=1, keepdims=True)
    table = jnp.zeros((8, LANES), F32)
    at, row = lane_ids(8), row_ids(8)
    for k in range(n):
        mine = jnp.where(row == 0, pre[k : k + 1, LANES - 1 : LANES], 0.0)
        mine = jnp.where(row == 1, down[k : k + 1, LANES - 1 : LANES], mine)
        mine = jnp.where(row == 2, suf[k : k + 1, 0:1], mine)
        mine = jnp.where(row == 3, norm[k : k + 1, 0:1], mine)
        table = jnp.where(lax.rem(at, 16) == k, mine, table)
    return ps, qs, pre, suf, table


def start_body(
    f_hbm, b_hbm, w_hbm, c_hbm, s_ref, pack_ref, f_ref, b_ref, w_ref, c_ref, sems
):
    n, cols, _ = f_ref.shape
    few = [(w_hbm, w_ref), (c_hbm, c_ref), (b_hbm, b_ref)]
    few += [(f_hbm.at[:, g : g + 16, :], f_ref.at[:, g : g + 16, :]) for g in range(0, cols, 16)]
    copies = [pltpu.make_async_copy(src, dst, sems.at[i]) for i, (src, dst) in enumerate(few)]
    for copy in copies:
        copy.start()
    size = n * cols
    at = size + n * n
    for copy in copies[:3]:
        copy.wait()
    for k in range(n):
        for m in range(n):
            pack_ref[size + k * n + m : size + k * n + m + 1, :] = c_ref[m] * b_ref[k, m]
    for i in range(2):
        for k in range(n):
            pack_ref[at + i * n + k : at + i * n + k + 1, :] = w_ref[i, k]
    for i, g in enumerate(range(0, cols, 16)):
        copies[3 + i].wait()
        vals = [f_ref[m, g : g + 16, :] for m in range(n)]
        for k in range(n):
            v = apply_rows(lambda m: b_ref[k, m], n, lambda m: vals[m])
            s_ref[k * cols + g : k * cols + g + 16, :] = v
            pack_ref[k * cols + g : k * cols + g + 16, :] = v


def side_body(pack_ref, up_ref, down_ref, suf_ref, tab_ref, ext_ref):
    n = ext_ref.shape[1] // LANES
    at = pack_ref.shape[0] - 2 * n
    ps, qs, pre, suf, table = rate_tables(pack_ref[at : at + n, :], pack_ref[at + n : at + 2 * n, :])
    tab_ref[0:8, :] = table
    tab_ref[8 : 8 + n, :] = pre
    for i, (p, q) in enumerate(zip(ps, qs)):
        up_ref[i, 0:n, :] = p
        down_ref[i, 0:n, :] = q
    suf_ref[0:n, :] = suf
    place = row_ids(32)
    first = (lane_ids(32) == 0).astype(F32)
    for k in range(n):
        block = jnp.where(place == k, jnp.broadcast_to(suf[k : k + 1, :], (32, LANES)), 0.0)
        ext_ref[:, k * LANES : (k + 1) * LANES] = jnp.where(place == 16 + k, first, block)


def other_body(near_ref, out_ref):
    out_ref[...] = near_ref[1 - lax.axis_index("core")]


def coupled(pack_ref, h_ref, k, n, rows):
    at = n * h_ref.shape[1] + k * n
    return apply_rows(
        lambda m: pack_ref[at + m : at + m + 1, :], n, lambda m: h_ref[m, rows, :]
    )


def rise(pack_ref, one, two, up_ref, loc_ref, h_ref, a_ref, between=lambda k: None):
    n, cols, _ = h_ref.shape
    for m in range(n):
        rows = slice(m * cols, (m + 1) * cols)
        h_ref[m] = one(rows) + two(rows)
    lane = lane_ids(16)
    first, inner = lane == 0, lane < LANES - 1
    for k in range(n):
        at = n * cols + n * n + n + k
        fall = pack_ref[at : at + 1, :]
        between(k)
        for g in range(cols // 16):
            rows = slice(16 * g, 16 * g + 16)
            wide = slice(k * cols + 16 * g, k * cols + 16 * g + 16)
            start = pack_ref[wide, :]
            above = jnp.where(inner, pltpu.roll(start, LANES - 1, 1), 0.0)
            v = start + fall * above + coupled(pack_ref, h_ref, k, n, rows)
            for i, d in enumerate(STEPS):
                v = v + up_ref[i, k : k + 1, :] * pltpu.roll(v, d, 1)
            loc_ref[wide, :] = v
            a_ref[rows, k * LANES : (k + 1) * LANES] = jnp.where(first, start, v)
    ends = pick(a_ref[...], end_mask(n))
    ends = jnp.concatenate([ends, jnp.zeros((cols, LANES - 32), F32)], axis=1)
    pay = ends[0:16, :]
    for g in range(1, cols // 16):
        pay = pay + pltpu.roll(ends[16 * g : 16 * g + 16, :], 32 * g, 1)
    return pay


def own_body(pack_ref, far_ref, near_ref, up_ref, tab_ref, buf_ref, fup_ref, ftab_ref, h_ref, a_ref):
    n, cols, _ = h_ref.shape
    size = n * cols
    at = size + n * n
    other = 1 - lax.axis_index("core")
    up, down = far_ref[at : at + n, :], far_ref[at + n : at + 2 * n, :]
    lane = lane_ids(n)
    state = [jnp.where(lane >= 1, up, 0.0), up]

    def far_table(k):
        if k < len(STEPS):
            d = STEPS[k]
            p, pre = state
            fup_ref[k, 0:n, :] = p
            state[0] = p * pltpu.roll(p, d, 1)
            state[1] = jnp.where(lane >= d, pre * pltpu.roll(pre, d, 1), pre)

    buf_ref[size : size + 16, :] = rise(
        pack_ref, lambda rows: far_ref[rows, :], lambda rows: near_ref[other, rows, :],
        up_ref, buf_ref, h_ref, a_ref, far_table,
    )
    buf_ref[size + 16 : size + 40, :] = tab_ref[...]
    pre = state[1]
    ftab_ref[8 : 8 + n, :] = pre
    table = jnp.zeros((8, LANES), F32)
    at, row = lane_ids(8), row_ids(8)
    for k in range(n):
        mine = jnp.where(row == 0, pre[k : k + 1, LANES - 1 : LANES], down[k : k + 1, LANES - 1 : LANES])
        table = jnp.where(lax.rem(at, 16) == k, mine, table)
    ftab_ref[0:8, :] = table


def far_body(
    pack_ref, start_ref, next_ref, up_ref, tab_ref, buf_ref, both_ref, loc_ref, pay_ref, h_ref, a_ref
):
    n, cols, _ = h_ref.shape
    size = n * cols
    other = 1 - lax.axis_index("core")
    pay = rise(
        pack_ref, lambda rows: start_ref[rows, :], lambda rows: next_ref[rows, :],
        up_ref, loc_ref, h_ref, a_ref,
    )
    own, near = buf_ref[size : size + 24, :], both_ref[other, size : size + 24, :]
    row = row_ids(8)
    table = jnp.where(row < 2, own[16:24, :], pltpu.roll(near[16:24, :], 2, 0))
    table = jnp.where(row < 4, table, pltpu.roll(tab_ref[0:8, :], 4, 0))
    for peer in range(pay_ref.shape[0]):
        pay_ref[peer, 0:16, :] = own[0:16, :]
        pay_ref[peer, 16:32, :] = near[0:16, :]
        pay_ref[peer, 32:48, :] = pay
        pay_ref[peer, 48:56, :] = table


def entering(r_ref, station):
    mine = lax.axis_index("line")
    at0, row = 16 * station, 48 + 2 * station
    state = jnp.zeros((16, LANES), F32)
    entry = state
    top = state
    for at in range(r_ref.shape[0] - 1):
        lead = pltpu.roll(r_ref[at + 1, at0 : at0 + 16, :], LANES - 16, 1)
        tail = r_ref[at, row + 1 : row + 2, :] * lead
        top = jnp.where(mine == at, tail, top)
        state = r_ref[at, row : row + 1, :] * state + (r_ref[at, at0 : at0 + 16, :] + tail)
        entry = jnp.where(mine == at + 1, state, entry)
    return entry, top


def packed_blocks(gram):
    lane, row = lane_ids(32), row_ids(32)
    corner = pltpu.roll(gram[32:64, :], LANES - 32, 1)
    joined = jnp.where(lane >= row, gram[0:32, :], corner)
    extra = jnp.sum(jnp.where(lane == row, corner, 0.0), axis=0, keepdims=True)
    quarter = lane_ids(8) // 32
    blocks = []
    for part in (pltpu.roll(gram[0:32, :], LANES - 32, 1), joined):
        block = jnp.zeros((8, LANES), F32)
        for a in range(4):
            block = jnp.where(quarter == a, pltpu.roll(part[8 * a : 8 * a + 8, :], 32 * a, 1), block)
        blocks.append(block)
    return (blocks[0], jnp.zeros((1, LANES), F32)), (blocks[1], extra)


def unpacked(upper, joined, extra):
    def spread(block):
        return jnp.concatenate([pltpu.roll(block, (LANES - 32 * a) % LANES, 1) for a in range(4)], axis=0)

    lane, row = lane_ids(32), row_ids(32)
    upper, joined = spread(upper), spread(joined)
    turned = jnp.where(lane < 32, joined, pltpu.roll(upper, 32, 1)).T
    turned = jnp.concatenate([turned, jnp.zeros((LANES, LANES - 32), F32)], axis=1)
    first, second = turned[0:32, :], turned[32:64, :]
    low = jnp.where(lane >= row, joined, first)
    high = jnp.where(lane < row, joined, jnp.where(lane == row, extra, first))
    top = jnp.where(lane < 32, low, pltpu.roll(upper, 32, 1))
    bottom = jnp.where(lane < 32, second, pltpu.roll(high, 32, 1))
    return jnp.concatenate([top, bottom], axis=0)


def down_body(
    pack_ref, r_ref, buf_ref, both_ref, floc_ref, ftab_ref, down_ref, ext_ref,
    loc_ref, pay_ref, h_ref, a_ref,
):
    n, cols, _ = loc_ref.shape
    size = n * cols
    other = 1 - lax.axis_index("core")
    mine, _ = entering(r_ref, 0)
    near, near_top = entering(r_ref, 1)
    far, far_top = entering(r_ref, 2)
    top = near_top + far_top
    lane = lane_ids(16)
    last, first = lane == LANES - 1, lane == 0
    for m in range(n):
        npre = both_ref[other, size + 24 + m : size + 25 + m, :]
        fpre = ftab_ref[8 + m : 9 + m, :]
        for g in range(cols // 16):
            rows, at = slice(m * cols + 16 * g, m * cols + 16 * g + 16), 32 * g + m
            v = both_ref[other, rows, :] + floc_ref[rows, :]
            v = v + npre * near[:, at : at + 1] + fpre * far[:, at : at + 1]
            h_ref[m, 16 * g : 16 * g + 16, :] = jnp.where(last, v + top[:, at : at + 1], v)
    one = lane_ids(1) == 0
    for k in range(n):
        up = pack_ref[size + n * n + k : size + n * n + k + 1, :]
        pre = buf_ref[size + 24 + k : size + 25 + k, :]
        pre = jnp.where(one, 1.0, pltpu.roll(pre, 1, 1))
        for g in range(cols // 16):
            rows = slice(16 * g, 16 * g + 16)
            wide, at = slice(k * cols + 16 * g, k * cols + 16 * g + 16), 32 * g + k
            below = jnp.where(first, 0.0, pltpu.roll(buf_ref[wide, :], 1, 1)) + pre * mine[:, at : at + 1]
            v = pack_ref[wide, :] + up * below + coupled(pack_ref, h_ref, k, n, rows)
            for i, d in enumerate(STEPS):
                v = v + down_ref[i, k : k + 1, :] * pltpu.roll(v, LANES - d, 1)
            loc_ref[k, rows, :] = v
            a_ref[rows, k * LANES : (k + 1) * LANES] = v
    a_ref[cols : cols + 32, :] = ext_ref[...]
    total = dot_nt(a_ref[0:cols, :], a_ref[...])
    total = jnp.concatenate([total, jnp.zeros((cols, 32), F32)], axis=1)
    lane = lane_ids(16)
    edges = jnp.zeros((16, LANES), F32)
    for g in range(cols // 16):
        moved = pltpu.roll(total[16 * g : 16 * g + 16, :], (32 * g + 64) % LANES, 1)
        edges = jnp.where(lane // 32 == g, moved, edges)
    (one, _), (two, extra) = packed_blocks(total)
    for peer in range(pay_ref.shape[0]):
        pay_ref[peer, 0:8, :] = one
        pay_ref[peer, 8:16, :] = two
        pay_ref[peer, 16:32, :] = edges
        pay_ref[peer, 32:40, :] = jnp.where(row_ids(8) == 4, extra, buf_ref[size + 16 : size + 24, :])


def line_body(r_ref, gram_ref, entry_ref, left_ref, right_ref):
    peers = r_ref.shape[0]
    cols = left_ref.shape[0]
    mine = lax.axis_index("line")
    lane = lane_ids(16)
    first = lane % 32 < 16
    zero = jnp.zeros((16, LANES), F32)
    entry = zero
    state = zero
    left = [zero] * (cols // 16)
    right = [zero] * (cols // 16)
    for at in range(peers - 2, -1, -1):
        state = r_ref[at + 1, 34:35, :] * state + r_ref[at + 1, 16:32, :]
        entry = jnp.where(mine == at, state, entry)
        back = pltpu.roll(state, LANES - 16, 1)
        cross = r_ref[at, 16:32, :] + (0.5 * r_ref[at, 35:36, :]) * back
        a = jnp.where(first, cross, state)
        b = jnp.where(first, back, pltpu.roll(cross, 16, 1))
        for g in range(cols // 16):
            shift = (32 * (at - g)) % LANES
            left[g] = jnp.where(lane // 32 == at, pltpu.roll(a, shift, 1), left[g])
            right[g] = jnp.where(lane // 32 == at, pltpu.roll(b, shift, 1), right[g])
    for g in range(cols // 16):
        rows = slice(16 * g, 16 * g + 16)
        left_ref[rows, :] = left[g]
        right_ref[rows, :] = right[g]
    fix = dot_nt(left_ref[...], right_ref[...])
    fix = jnp.concatenate([fix, jnp.zeros((cols, LANES - cols), F32)], axis=1)
    (one, none), (two, extra) = packed_blocks(fix)
    for at in range(peers):
        one = one + r_ref[at, 0:8, :]
        two = two + r_ref[at, 8:16, :]
        extra = extra + r_ref[at, 36:37, :]
    for block, row, core in ((one, none, 0), (two, extra, 1)):
        for peer in range(core, gram_ref.shape[0], NCORE):
            for i in range(8):
                gram_ref[peer, i] = block[i : i + 1, :]
            gram_ref[peer, 8] = row
    entry_ref[...] = entry


def spread_rows(out_ref, rows):
    for peer in range(out_ref.shape[0]):
        for i, row in enumerate(rows):
            out_ref[peer, i] = row


def summed_rows(r_ref, first, step):
    rows = []
    for i in range(r_ref.shape[1]):
        total = r_ref[first, i]
        for peer in range(first + step, r_ref.shape[0], step):
            total = total + r_ref[peer, i]
        rows.append(total)
    return rows


def sum_body(r_ref, o_ref):
    spread_rows(o_ref, summed_rows(r_ref, 0, 1))


def inverse_factor(scale, gram, v_ref, after):
    cols = gram.shape[0]
    count = cols // 8
    lane, row = lane_ids(8), row_ids(8)
    tiles = []
    for t in range(count):
        unit = jnp.where(lane - 64 == row + 8 * t, 1.0, 0.0)
        tiles.append(jnp.where(lane < 64, gram[8 * t : 8 * t + 8, :], unit))
    for p in range(count):
        later = range(p + 1, count)
        r = [tiles[p][i : i + 1, :] for i in range(8)]
        s = {}
        for i in range(8):
            for j in range(i + 1):
                at = 8 * p + j
                s[i, j] = jnp.broadcast_to(r[i][:, at : at + 1], (1, LANES))
        c = []
        for i in range(8):
            at = 8 * p + i
            c.append([jnp.broadcast_to(tiles[t][:, at : at + 1], (8, LANES)) for t in later])
        scaled = []
        for i in range(8):
            inv = 1.0 / s[i, i]
            for t in range(i + 1, 8):
                f = s[t, i] * inv
                for u in range(i + 1, t + 1):
                    s[t, u] = s[t, u] - f * s[u, i]
                r[t] = r[t] - f * r[i]
                c[t] = [x - f * y for x, y in zip(c[t], c[i])]
            v_ref[8 * p + i : 8 * p + i + 1, :] = r[i] * (scale / jnp.sqrt(s[i, i]))
            scaled.append(r[i] * inv)
        for x, t in enumerate(later):
            for i in range(8):
                tiles[t] = tiles[t] - c[i][x] * scaled[i]
        after(p)


def basis_body(scale, r_ref, loc_ref, suf_ref, entry_ref, out_ref, f_ref, v_ref):
    n, cols, _ = loc_ref.shape
    for k in range(n):
        suf = suf_ref[k : k + 1, :]
        for g in range(cols // 16):
            rows, at = slice(16 * g, 16 * g + 16), 32 * g + 16 + k
            v = loc_ref[k, rows, :] + suf * entry_ref[:, at : at + 1]
            f_ref[rows, k * LANES : (k + 1) * LANES] = v
    upper, joined = (summed_rows(r_ref, core, NCORE) for core in range(NCORE))
    gram = unpacked(jnp.concatenate(upper[:8], axis=0), jnp.concatenate(joined[:8], axis=0), joined[8])
    half = cols // 2

    def product(low, depth):
        inv = pltpu.roll(v_ref[low : low + half, :], 64, 1)[:, 0:depth]
        out = jnp.dot(inv, f_ref[0:depth, :], precision=HIGH, preferred_element_type=F32)
        for k in range(n):
            out_ref[k, low : low + half, :] = out[:, k * LANES : (k + 1) * LANES]

    inverse_factor(scale, gram, v_ref, lambda p: product(0, half) if p == half // 8 - 1 else None)
    product(half, cols)


def in_hbm(value):
    return pltpu.with_memory_space_constraint(value, pltpu.HBM)


def exchange(value, axis):
    return lax.all_to_all(value, axis, 0, 0, tiled=True)


def local(forcing, block_inverse, wall_rates, span_couple):
    n, cols, _, pts = forcing.shape
    peers = lax.axis_size("line")
    stations = lax.axis_size("z") * lax.axis_size("y") * lax.axis_size("core")
    rows = n * stations * pts * peers
    field = (n, cols, pts)
    f, b, w, c = map(in_hbm, (forcing.reshape(field), block_inverse, wall_rates, span_couple))
    pairs = [(i, 1 if i % 2 else -1) for i in range(stations)]
    across = [(i, (i + d) % stations) for i, d in pairs]
    work = 2 * n * n * cols * pts
    size = n * cols
    scratch = pltpu.VMEM(field, F32)
    wide = pltpu.VMEM((cols, n * pts), F32)
    tall = pltpu.VMEM((cols + 32, n * pts), F32)

    inputs = [pltpu.VMEM(a.shape, F32) for a in (f, b, w)] + [pltpu.SMEM(c.shape, F32)]
    steps = (len(STEPS), 16, pts)
    start, pack = call(
        start_body,
        [(size, pts), (size + n * n + 2 * n, pts)],
        work,
        inputs + [pltpu.SemaphoreType.DMA((3 + cols // 16,))],
        HBM,
    )(f, b, w, c)
    fpack = lax.ppermute(pack, TILE, across)
    near = lax.all_gather(start, "core")
    tables_of, near = lax.optimization_barrier((pack, near))
    beyond = lax.ppermute(call(other_body, (size, pts))(near), TILE, across)
    up, down, suf, tab, ext = call(
        side_body, [steps, steps, (16, pts), (24, pts), (32, n * pts)], work // 4
    )(tables_of)
    buf, fup, ftab = call(own_body, [(size + 40, pts), steps, (24, pts)], 2 * work, [scratch, wide])(
        pack, fpack, near, up, tab
    )
    both = lax.all_gather(buf, "core")
    floc, pay = call(far_body, [(size, pts), (peers, 56, pts)], 2 * work, [scratch, wide])(
        fpack, start, beyond, fup, ftab, buf, both
    )
    got = exchange(pay, "line")
    loc, pay = call(down_body, [field, (peers, 40, pts)], 4 * work, [scratch, tall])(
        pack, got, buf, both, floc, ftab, down, ext
    )
    side = pltpu.VMEM((cols, pts), F32)
    part = (9, 1, pts)
    gram, entry = call(line_body, [(NY * NCORE,) + part, (16, pts)], work // 4, [side, side])(
        exchange(pay, "line")
    )
    gram = call(sum_body, (NZ * NCORE,) + part)(exchange(gram, ("y", "core")))
    gram = exchange(gram, ("z", "core"))

    def basis(*refs):
        basis_body(math.sqrt(rows), *refs)

    out = call(basis, field, 4 * work, [wide, pltpu.VMEM((cols, pts), F32)])(
        gram, loc, suf, entry
    )
    return out.reshape(n, cols, 1, pts)


def solution(mesh):
    devices = mesh.devices.reshape(mesh.shape["line"], NZ, NY, NCORE)
    inner = Mesh(devices, ("line",) + TILE)
    spec = P(None, None, TILE, "line")
    return jax.shard_map(
        local, mesh=inner, in_specs=(spec, spec, spec, P()), out_specs=spec, check_vma=False
    )
```
